512 devices in a mesh: tile: 128 (over z, x, core), layer: 4 (over y).
Axes of the slice: x: 4, y: 4, z: 16, core: 2. Of those that a mesh axis runs over, the one named last changes fastest.
Arguments:
- head_start: float32 [8, 8192, 512], P('layer', 'tile'), may hold values from -2 to 0.5
- soil_class: int32 [8, 8192, 512], P('layer', 'tile'), may hold values from 0 to 11
- land_mask: int32 [8192, 512], P('tile'), may hold values 0 or 1
- ks_table: float32 [12], replicated, may hold values from 0.2 to 5
- alpha_table: float32 [12], replicated, may hold values from 0.5 to 2
- store_table: float32 [12], replicated, may hold values from 0.5 to 2
- section: float32 [2048, 128], P('tile'), may hold values from -6 to 6
- cross_owner: int32 [128, 256], P('tile'), may hold values from 0 to 127, as said below
- cross_local: int32 [128, 256], P('tile'), may hold values from 0 to 15
- node_cell: int32 [128, 256, 128], P('tile'), may hold values from -1 to 32767, as said below
- bed_cond: float32 [128, 256, 128], P('tile'), may hold values from 0.5 to 4
Outputs:
- head: float32 [8, 8192, 512], P('layer', 'tile')
- inflow: float32 [2048, 128], P('tile', 'layer')
The draws below stay inside these ranges and needn't reach their ends.
Inputs may be any that keep to these rules, and one draw needn't show every extreme that they name: `cross_owner`: no strip's row names one owner in more than 2 slots, and in every row some owner is named in exactly 2 slots. `node_cell`: -1 marks a node outside the strip; other values index the strip's top-layer cells row-major over 64 x 512. In each strip the slots with nodes come first, the rest are padding with every node -1.
All inputs are finite; a program needn't handle non-finite values. No bound on the sum of `land_mask` on one device may be relied on, other than what follows from the above.
Results may differ from the reference program's by a relative error of at most 0.00002.
Values sent between devices are 32-bit elements; how exact they have to be, the bound alone decides.
A program may use at most 64 MiB of HBM per device.

```python
import math
import jax
import jax.numpy as jnp

CX = 64
NY = 512
NCLASS = 12
NODES = 128
RPT = 16
CSLOT = 256
ITERS = 2
SWEEPS = 3
TILES = 128
NX = 8192
NZ = 8
REACHES = 2048


def draw_cross_owner(key, part):
    rounds = (CSLOT + TILES - 1) // TILES
    keys = jax.random.split(key, TILES * rounds)
    perms = jax.vmap(lambda single: jax.random.permutation(single, TILES))(keys)
    return perms.reshape(TILES, rounds * TILES)[:, :CSLOT].astype(jnp.int32)


def draw_node_cell(key, part):
    key_live, key_start, key_length, key_cell = jax.random.split(jax.random.fold_in(key, 17), 4)
    live_slots = jax.random.randint(key_live, (TILES, 1), CSLOT // 2, CSLOT + 1)
    slot_order = jnp.arange(CSLOT, dtype=jnp.int32)[None, :]
    slot_live = slot_order < live_slots
    length = jax.random.randint(key_length, (TILES, CSLOT, 1), NODES // 2, NODES + 1)
    start = jax.random.randint(key_start, (TILES, CSLOT, 1), 0, NODES - length + 1)
    node_order = jnp.arange(NODES, dtype=jnp.int32)[None, None, :]
    inside = (node_order >= start) & (node_order < start + length) & slot_live[:, :, None]
    chosen = jax.random.randint(key_cell, (TILES, CSLOT, NODES), 0, CX * NY)
    return jnp.where(inside, chosen, -1).astype(jnp.int32)


def set_ends(array, key, low, largest):
    spot = [jax.random.randint(jax.random.fold_in(key, axis), (), 0, length) for axis, length in enumerate(array.shape)]
    main_axis = array.shape.index(max(array.shape))
    next_to = spot[:main_axis] + [(spot[main_axis] + 1) % array.shape[main_axis]] + spot[main_axis + 1:]
    return array.at[tuple(spot)].set(low).at[tuple(next_to)].set(largest)


def block_scale(stream_key, extent, pieces, smallest, largest):
    loudness = 1.0
    for position, shards_of in pieces:
        draws = jax.random.uniform(jax.random.fold_in(jax.random.fold_in(stream_key, 6), position), (shards_of,), jnp.float32, smallest / len(pieces), largest / len(pieces))
        loudness = loudness * jnp.repeat(jnp.exp(draws), extent[position] // shards_of).reshape((-1,) + (1,) * (len(extent) - 1 - position))
    return loudness


def noise(key, dims, scale, limit, cuts=(), kind=jnp.bfloat16):
    drawn = scale * jax.random.normal(key, dims, jnp.float32)
    if cuts:
        drawn = drawn * block_scale(key, dims, cuts, -0.22, 0.18)
    return jnp.clip(drawn, -limit, limit).astype(kind)


def setup_inputs(seed: int = 0) -> dict:
    streams_of = jax.random.split(jax.random.key(seed), 12)
    return {
        "head_start": jnp.clip(-2.0 + 2.5 * jax.random.uniform(streams_of[0], (NZ, NX, NY), jnp.float32) ** block_scale(streams_of[0], (NZ, NX, NY), ((0, 4), (1, 128)), -0.2, 0.2), -2.0, 0.5),
        "soil_class": set_ends(jax.random.randint(streams_of[1], (NZ, NX, NY), 0, NCLASS), jax.random.fold_in(streams_of[1], 1), 0, NCLASS - 1).astype(jnp.int32),
        "land_mask": set_ends((jax.random.randint(streams_of[2], (NX, NY), 0, 8) < 7).astype(jnp.int32), jax.random.fold_in(streams_of[2], 1), 0, 1),
        "ks_table": jnp.clip(jnp.exp(jax.random.uniform(streams_of[3], (NCLASS,), jnp.float32, math.log(0.2), math.log(5.0))), 0.2, 5.0),
        "alpha_table": jnp.clip(jax.random.uniform(streams_of[4], (NCLASS,), jnp.float32, 0.5, 2.0), 0.5, 2.0),
        "store_table": jnp.clip(jax.random.uniform(streams_of[5], (NCLASS,), jnp.float32, 0.5, 2.0), 0.5, 2.0),
        "section": noise(streams_of[6], (REACHES, NODES), 1.0, 6.0, ((0, 128),), jnp.float32),
        "cross_owner": draw_cross_owner(jax.random.fold_in(streams_of[11], 71), 0),
        "cross_local": set_ends(jax.random.randint(streams_of[8], (TILES, CSLOT), 0, RPT), jax.random.fold_in(streams_of[8], 1), 0, RPT - 1).astype(jnp.int32),
        "node_cell": draw_node_cell(jax.random.fold_in(streams_of[11], 71), 0),
        "bed_cond": jnp.clip(jnp.exp(math.log(4.0) - 2.0794415 * jax.random.uniform(streams_of[10], (TILES, CSLOT, NODES), jnp.float32) ** block_scale(streams_of[10], (TILES, CSLOT, NODES), ((0, 128),), -0.2, 0.2)), 0.5, 4.0),
    }


LATERAL = 1.0
VERTICAL = 2.0
GRAVITY = 1.0
NEIGHBOURS = ((0, -1, VERTICAL), (0, 1, VERTICAL), (1, -1, LATERAL), (1, 1, LATERAL), (2, -1, LATERAL), (2, 1, LATERAL))


def beside(padded, axis_id, step):
    spans = [slice(1, -1), slice(1, -1), slice(1, -1)]
    spans[axis_id] = slice(1 + step, padded.shape[axis_id] - 1 + step)
    return padded[tuple(spans)]


def neighbor_weights(cond_pad, open_pad):
    centre = cond_pad[1:-1, 1:-1, 1:-1]
    centre_open = open_pad[1:-1, 1:-1, 1:-1]
    result = []
    for axis_id, step, factor in NEIGHBOURS:
        far = beside(cond_pad, axis_id, step)
        far_open = beside(open_pad, axis_id, step)
        result.append(factor * 2.0 * centre_open * far_open / (centre + far))
    return result


def relax(head_pad, weights, store, head_old, riv_diag, riv_rhs):
    total = store * head_old
    diagonal_sum = store
    for weight, (axis_id, step, factor) in zip(weights, NEIGHBOURS):
        total = total + weight * beside(head_pad, axis_id, step)
        diagonal_sum = diagonal_sum + weight
    total = total + GRAVITY * (weights[0] - weights[1]) + riv_rhs
    return total / (diagonal_sum + riv_diag)


def reference(head_start, soil_class, land_mask, ks_table, alpha_table, store_table, section, cross_owner, cross_local, node_cell, bed_cond):
    ks = ks_table[soil_class]
    alpha = alpha_table[soil_class]
    store = store_table[soil_class]
    landf = land_mask.astype(jnp.float32)[None]
    reach_row = cross_owner * RPT + cross_local
    slot_section = section[reach_row]
    tile_ids = jnp.arange(TILES, dtype=jnp.int32)[:, None, None]
    in_tile = node_cell >= 0
    safe_cell = jnp.where(in_tile, node_cell, 0)
    grid_row = tile_ids * CX + safe_cell // NY
    flat_index = jnp.where(in_tile, grid_row * NY + safe_cell % NY, NX * NY)
    bed_terms = jnp.where(in_tile, bed_cond, 0.0)
    diag_top = jnp.zeros((NX * NY,), jnp.float32).at[flat_index.reshape(-1)].add(bed_terms.reshape(-1), mode="drop")
    rhs_top = jnp.zeros((NX * NY,), jnp.float32).at[flat_index.reshape(-1)].add((bed_terms * slot_section).reshape(-1), mode="drop")
    riv_diag = jnp.zeros((NZ, NX, NY), jnp.float32).at[0].set(diag_top.reshape(NX, NY))
    riv_rhs = jnp.zeros((NZ, NX, NY), jnp.float32).at[0].set(rhs_top.reshape(NX, NY))
    head = head_start
    for picard in range(ITERS):
        conduct = ks * jnp.exp(alpha * jnp.minimum(head, 0.0))
        cond_pad = jnp.pad(conduct, 1)
        open_pad = jnp.pad(conduct * landf, 1)
        weights = neighbor_weights(cond_pad, open_pad)
        for sweep in range(SWEEPS):
            head = relax(jnp.pad(head, 1), weights, store, head_start, riv_diag, riv_rhs)
    top_flat = head[0].reshape(-1)
    node_head = top_flat[jnp.where(in_tile, flat_index, 0)]
    slot_in = jnp.where(in_tile, bed_cond * (node_head - slot_section), 0.0)
    inflow = jnp.zeros((REACHES, NODES), jnp.float32).at[reach_row.reshape(-1)].add(slot_in.reshape(-1, NODES))
    return head, inflow
```

```python
import jax
import jax.numpy as jnp
from jax import lax
from jax.experimental import pallas as pl
from jax.experimental.pallas import tpu as pltpu
from jax.sharding import PartitionSpec as P

ITERS = 2
SWEEPS = 3
GHOST = ITERS * SWEEPS


LATERAL = 1.0
VERTICAL = 2.0
GRAVITY = 1.0
NEIGHBOURS = (
    (0, -1, VERTICAL),
    (0, 1, VERTICAL),
    (1, -1, LATERAL),
    (1, 1, LATERAL),
    (2, -1, LATERAL),
    (2, 1, LATERAL),
)
CHUNK = 512


def beside(padded, axis_id, step):
    spans = [slice(1, -1), slice(1, -1), slice(1, -1)]
    spans[axis_id] = slice(1 + step, padded.shape[axis_id] - 1 + step)
    return padded[tuple(spans)]


def neighbor_weights(cond_pad, open_pad):
    centre = cond_pad[1:-1, 1:-1, 1:-1]
    centre_open = open_pad[1:-1, 1:-1, 1:-1]
    result = []
    for axis_id, step, factor in NEIGHBOURS:
        far = beside(cond_pad, axis_id, step)
        far_open = beside(open_pad, axis_id, step)
        result.append(factor * 2.0 * centre_open * far_open / (centre + far))
    return result


def relax(head_pad, weights, store, head_old, riv_diag, riv_rhs):
    total = store * head_old
    diagonal_sum = store
    for weight, (axis_id, step, factor) in zip(weights, NEIGHBOURS):
        total = total + weight * beside(head_pad, axis_id, step)
        diagonal_sum = diagonal_sum + weight
    total = total + GRAVITY * (weights[0] - weights[1]) + riv_rhs
    return total / (diagonal_sum + riv_diag)


def lookup(values_table, classes):
    result = jnp.zeros(classes.shape, jnp.float32)
    for class_id in range(values_table.shape[0]):
        result = jnp.where(classes == class_id, values_table[class_id], result)
    return result


def split3(value):
    high = value.astype(jnp.bfloat16).astype(jnp.float32)
    rest = value - high
    middle = rest.astype(jnp.bfloat16).astype(jnp.float32)
    low = rest - middle
    return high, middle, low


def scatter_kernel(rows_ref, cols_ref, diag_in_ref, rhs_in_ref, diag_ref, rhs_ref, acc_ref):
    step = pl.program_id(0)
    grid_rows, breadth = diag_ref.shape
    chunk = rows_ref.shape[1]

    @pl.when(step == 0)
    def _():
        acc_ref[...] = jnp.zeros_like(acc_ref)

    rows = rows_ref[...]

    @pl.when(jnp.max(rows) >= 0)
    def _():
        hit = lax.broadcasted_iota(jnp.int32, (grid_rows, chunk), 0) == rows
        pieces = []
        for value in (diag_in_ref[...], rhs_in_ref[...]):
            for piece in split3(value):
                pieces.append(jnp.where(hit, piece, 0.0).astype(jnp.bfloat16))
        left = jnp.concatenate(pieces, axis=0)
        cols = cols_ref[...]
        column_hit = lax.broadcasted_iota(jnp.int32, (breadth, chunk), 0) == cols
        right = jnp.where(column_hit, 1.0, 0.0).astype(jnp.bfloat16)
        acc_ref[...] += lax.dot_general(
            left, right, (((1,), (1,)), ((), ())), preferred_element_type=jnp.float32
        )

    @pl.when(step == pl.num_programs(0) - 1)
    def _():
        acc = acc_ref[...]
        g = grid_rows
        diag_ref[...] = acc[0:g] + acc[g : 2 * g] + acc[2 * g : 3 * g]
        rhs_ref[...] = acc[3 * g : 4 * g] + acc[4 * g : 5 * g] + acc[5 * g : 6 * g]


def river_terms(rows, cols, diag_values, rhs_values, grid_rows, breadth):
    count = rows.shape[1]
    lane = pl.BlockSpec((1, CHUNK), lambda i: (0, i))
    whole = pl.BlockSpec((grid_rows, breadth), lambda i: (0, 0))
    return pl.pallas_call(
        scatter_kernel,
        grid=(count // CHUNK,),
        in_specs=[lane, lane, lane, lane],
        out_specs=[whole, whole],
        out_shape=[
            jax.ShapeDtypeStruct((grid_rows, breadth), jnp.float32),
            jax.ShapeDtypeStruct((grid_rows, breadth), jnp.float32),
        ],
        scratch_shapes=[pltpu.VMEM((6 * grid_rows, breadth), jnp.float32)],
        cost_estimate=pl.CostEstimate(
            flops=2 * 6 * grid_rows * breadth * count,
            transcendentals=0,
            bytes_accessed=16 * count + 8 * grid_rows * breadth,
        ),
    )(rows, cols, diag_values, rhs_values)


def gather_kernel(top_ref, rows_ref, cols_ref, out_ref):
    grid_rows, breadth = top_ref.shape
    chunk = rows_ref.shape[1]
    stacked = jnp.concatenate(
        [piece.astype(jnp.bfloat16) for piece in split3(top_ref[...])], axis=0
    )
    cols = cols_ref[...]
    column_hit = lax.broadcasted_iota(jnp.int32, (breadth, chunk), 0) == cols
    right = jnp.where(column_hit, 1.0, 0.0).astype(jnp.bfloat16)
    picked = jnp.dot(stacked, right, preferred_element_type=jnp.float32)
    g = grid_rows
    by_row = picked[0:g] + picked[g : 2 * g] + picked[2 * g : 3 * g]
    rows = rows_ref[...]
    hit = lax.broadcasted_iota(jnp.int32, (grid_rows, chunk), 0) == rows
    out_ref[...] = jnp.sum(jnp.where(hit, by_row, 0.0), axis=0, keepdims=True)


def node_heads(top, rows, cols):
    grid_rows, breadth = top.shape
    count = rows.shape[1]
    lane = pl.BlockSpec((1, CHUNK), lambda i: (0, i))
    return pl.pallas_call(
        gather_kernel,
        grid=(count // CHUNK,),
        in_specs=[pl.BlockSpec((grid_rows, breadth), lambda i: (0, 0)), lane, lane],
        out_specs=lane,
        out_shape=jax.ShapeDtypeStruct((1, count), jnp.float32),
        cost_estimate=pl.CostEstimate(
            flops=2 * 3 * grid_rows * breadth * count,
            transcendentals=0,
            bytes_accessed=12 * count + 4 * grid_rows * breadth,
        ),
    )(top, rows, cols)


def with_ghost(block, axis, dim, width):
    count = lax.axis_size(axis)
    forward = [(i, i + 1) for i in range(count - 1)]
    backward = [(i + 1, i) for i in range(count - 1)]
    size = block.shape[dim]
    above = lax.ppermute(lax.slice_in_dim(block, size - width, size, axis=dim), axis, forward)
    below = lax.ppermute(lax.slice_in_dim(block, 0, width, axis=dim), axis, backward)
    return jnp.concatenate([above, block, below], axis=dim)


def on_device(
    head_start,
    soil_class,
    land_mask,
    ks_table,
    alpha_table,
    store_table,
    section,
    cross_owner,
    cross_local,
    node_cell,
    bed_cond,
):
    own_layers, across, breadth = head_start.shape
    reach_rows, node_count = section.shape
    tile_count = lax.axis_size("tile")
    layer_count = lax.axis_size("layer")
    tile = lax.axis_index("tile")
    layer = lax.axis_index("layer")
    quarter = node_count // layer_count
    node_first = layer * quarter

    planes = jnp.concatenate(
        [head_start, soil_class.astype(jnp.float32), land_mask.astype(jnp.float32)[None]], axis=0
    )
    planes = with_ghost(planes, "tile", 1, GHOST)
    extent = across + 2 * GHOST
    fields = planes[: 2 * own_layers].reshape(2, own_layers, extent, breadth)
    fields = lax.all_gather(fields, "layer", axis=1, tiled=True)
    global_row = tile * across - GHOST + lax.broadcasted_iota(jnp.int32, (1, extent, 1), 1)
    inside = (global_row >= 0) & (global_row < tile_count * across)
    head_old = jnp.where(inside, fields[0], 0.0)
    classes = fields[1].astype(jnp.int32)
    ks_here = jnp.where(inside, lookup(ks_table, classes), 1.0)
    alpha_here = jnp.where(inside, lookup(alpha_table, classes), 0.0)
    store_here = jnp.where(inside, lookup(store_table, classes), 1.0)
    land_here = jnp.where(inside, planes[2 * own_layers][None], 0.0)

    owners = cross_owner[0]
    positions = cross_local[0]
    node_cells = node_cell[0]
    bed_given = bed_cond[0]
    slots = owners.shape[0]
    per_owner = slots // tile_count
    order = jnp.arange(slots, dtype=jnp.int32)
    same = owners[:, None] == owners[None, :]
    rank = jnp.sum((same & (order[None, :] < order[:, None])).astype(jnp.int32), axis=1)
    place = owners * per_owner + rank
    at_place = place[None, :] == order[:, None]
    wanted = jnp.sum(jnp.where(at_place, positions[None, :], 0), axis=1)
    asked = lax.all_to_all(wanted, "tile", 0, 0, tiled=True)
    reply = jnp.take(section, asked, axis=0)
    sorted_section = lax.all_to_all(reply, "tile", 0, 0, tiled=True)
    slot_section = jnp.take(sorted_section, place, axis=0)

    in_tile = node_cells >= 0
    bed_terms = jnp.where(in_tile, bed_given, 0.0)
    cell_rows = jnp.where(in_tile, node_cells // breadth, -1)
    cell_cols = jnp.where(in_tile, node_cells % breadth, 0)
    top_diag, top_rhs = river_terms(
        cell_rows.reshape(1, -1),
        cell_cols.reshape(1, -1),
        bed_terms.reshape(1, -1),
        (bed_terms * slot_section).reshape(1, -1),
        across,
        breadth,
    )
    river = with_ghost(jnp.stack([top_diag, top_rhs]), "tile", 1, GHOST)
    layers = head_old.shape[0]
    riv_diag = jnp.pad(river[0][None], ((0, layers - 1), (0, 0), (0, 0)))
    riv_rhs = jnp.pad(river[1][None], ((0, layers - 1), (0, 0), (0, 0)))

    head = head_old
    for picard in range(ITERS):
        conduct = ks_here * jnp.exp(alpha_here * jnp.minimum(head, 0.0))
        cond_pad = jnp.pad(conduct, 1)
        open_pad = jnp.pad(conduct * land_here, 1)
        weights = neighbor_weights(cond_pad, open_pad)
        for sweep in range(SWEEPS):
            head = relax(jnp.pad(head, 1), weights, store_here, head_old, riv_diag, riv_rhs)
    kept = lax.dynamic_slice_in_dim(head[:, GHOST : GHOST + across], layer * own_layers, own_layers, 0)

    top_head = head[0, GHOST : GHOST + across]
    my_cells = lax.dynamic_slice_in_dim(node_cells, node_first, quarter, 1)
    my_bed = lax.dynamic_slice_in_dim(bed_given, node_first, quarter, 1)
    my_section = lax.dynamic_slice_in_dim(slot_section, node_first, quarter, 1)
    my_inside = my_cells >= 0
    picked = node_heads(
        top_head,
        jnp.where(my_inside, my_cells // breadth, -1).reshape(1, -1),
        jnp.where(my_inside, my_cells % breadth, 0).reshape(1, -1),
    ).reshape(slots, quarter)
    slot_in = jnp.where(my_inside, my_bed * (picked - my_section), 0.0)
    sorted_in = jnp.take(slot_in, jnp.sum(jnp.where(at_place, order[None, :], 0), axis=1), axis=0)
    arrived = lax.all_to_all(sorted_in, "tile", 0, 0, tiled=True)
    target = asked[None, :] == jnp.arange(reach_rows, dtype=jnp.int32)[:, None]
    inflow = jnp.sum(jnp.where(target[:, :, None], arrived[None], 0.0), axis=1)
    return (kept, inflow)


def solution(mesh):
    placed = (
        P("layer", "tile", None),
        P("layer", "tile", None),
        P("tile", None),
        P(),
        P(),
        P(),
        P("tile", None),
        P("tile", None),
        P("tile", None),
        P("tile", None, None),
        P("tile", None, None),
    )
    return jax.shard_map(
        on_device,
        mesh=mesh,
        in_specs=placed,
        out_specs=(P("layer", "tile", None), P("tile", "layer")),
        check_vma=False,
    )
```

```python
import functools

import jax
import jax.numpy as jnp
from jax import lax
from jax.experimental import pallas as pl
from jax.experimental.pallas import tpu as pltpu
from jax.sharding import PartitionSpec as P

ITERS = 2
SWEEPS = 3
GHOST = 8


LATERAL = 1.0
VERTICAL = 2.0
GRAVITY = 1.0
NEIGHBOURS = (
    (0, -1, VERTICAL),
    (0, 1, VERTICAL),
    (1, -1, LATERAL),
    (1, 1, LATERAL),
    (2, -1, LATERAL),
    (2, 1, LATERAL),
)
CHUNK = 512


def beside(padded, axis_id, step):
    spans = [slice(1, -1), slice(1, -1), slice(1, -1)]
    spans[axis_id] = slice(1 + step, padded.shape[axis_id] - 1 + step)
    return padded[tuple(spans)]


def neighbor_weights(cond_pad, open_pad):
    centre = cond_pad[1:-1, 1:-1, 1:-1]
    centre_open = open_pad[1:-1, 1:-1, 1:-1]
    result = []
    for axis_id, step, factor in NEIGHBOURS:
        far = beside(cond_pad, axis_id, step)
        far_open = beside(open_pad, axis_id, step)
        result.append(factor * 2.0 * centre_open * far_open / (centre + far))
    return result


def relax(head_pad, weights, store, head_old, riv_diag, riv_rhs):
    total = store * head_old
    diagonal_sum = store
    for weight, (axis_id, step, factor) in zip(weights, NEIGHBOURS):
        total = total + weight * beside(head_pad, axis_id, step)
        diagonal_sum = diagonal_sum + weight
    total = total + GRAVITY * (weights[0] - weights[1]) + riv_rhs
    return total / (diagonal_sum + riv_diag)


def lookup(values_table, classes):
    result = jnp.zeros(classes.shape, jnp.float32)
    for class_id in range(values_table.shape[0]):
        result = jnp.where(classes == class_id, values_table[class_id], result)
    return result


def split3(value):
    high = value.astype(jnp.bfloat16).astype(jnp.float32)
    rest = value - high
    middle = rest.astype(jnp.bfloat16).astype(jnp.float32)
    low = rest - middle
    return high, middle, low


def scatter_kernel(rows_ref, cols_ref, diag_in_ref, rhs_in_ref, diag_ref, rhs_ref, acc_ref):
    step = pl.program_id(0)
    grid_rows, breadth = diag_ref.shape
    chunk = rows_ref.shape[1]

    @pl.when(step == 0)
    def _():
        acc_ref[...] = jnp.zeros_like(acc_ref)

    rows = rows_ref[...]

    @pl.when(jnp.max(rows) >= 0)
    def _():
        hit = lax.broadcasted_iota(jnp.int32, (grid_rows, chunk), 0) == rows
        pieces = []
        for value in (diag_in_ref[...], rhs_in_ref[...]):
            for piece in split3(value):
                pieces.append(jnp.where(hit, piece, 0.0).astype(jnp.bfloat16))
        left = jnp.concatenate(pieces, axis=0)
        cols = cols_ref[...]
        column_hit = lax.broadcasted_iota(jnp.int32, (breadth, chunk), 0) == cols
        right = jnp.where(column_hit, 1.0, 0.0).astype(jnp.bfloat16)
        acc_ref[...] += lax.dot_general(
            left, right, (((1,), (1,)), ((), ())), preferred_element_type=jnp.float32
        )

    @pl.when(step == pl.num_programs(0) - 1)
    def _():
        acc = acc_ref[...]
        g = grid_rows
        diag_ref[...] = acc[0:g] + acc[g : 2 * g] + acc[2 * g : 3 * g]
        rhs_ref[...] = acc[3 * g : 4 * g] + acc[4 * g : 5 * g] + acc[5 * g : 6 * g]


def river_terms(rows, cols, diag_values, rhs_values, grid_rows, breadth):
    count = rows.shape[1]
    lane = pl.BlockSpec((1, CHUNK), lambda i: (0, i))
    whole = pl.BlockSpec((grid_rows, breadth), lambda i: (0, 0))
    return pl.pallas_call(
        scatter_kernel,
        grid=(count // CHUNK,),
        in_specs=[lane, lane, lane, lane],
        out_specs=[whole, whole],
        out_shape=[
            jax.ShapeDtypeStruct((grid_rows, breadth), jnp.float32),
            jax.ShapeDtypeStruct((grid_rows, breadth), jnp.float32),
        ],
        scratch_shapes=[pltpu.VMEM((6 * grid_rows, breadth), jnp.float32)],
        cost_estimate=pl.CostEstimate(
            flops=2 * 6 * grid_rows * breadth * count,
            transcendentals=0,
            bytes_accessed=16 * count + 8 * grid_rows * breadth,
        ),
    )(rows, cols, diag_values, rhs_values)


def gather_kernel(top_ref, rows_ref, cols_ref, out_ref):
    grid_rows, breadth = top_ref.shape
    chunk = rows_ref.shape[1]
    stacked = jnp.concatenate(
        [piece.astype(jnp.bfloat16) for piece in split3(top_ref[...])], axis=0
    )
    cols = cols_ref[...]
    column_hit = lax.broadcasted_iota(jnp.int32, (breadth, chunk), 0) == cols
    right = jnp.where(column_hit, 1.0, 0.0).astype(jnp.bfloat16)
    picked = jnp.dot(stacked, right, preferred_element_type=jnp.float32)
    g = grid_rows
    by_row = picked[0:g] + picked[g : 2 * g] + picked[2 * g : 3 * g]
    rows = rows_ref[...]
    hit = lax.broadcasted_iota(jnp.int32, (grid_rows, chunk), 0) == rows
    out_ref[...] = jnp.sum(jnp.where(hit, by_row, 0.0), axis=0, keepdims=True)


def node_heads(top, rows, cols):
    grid_rows, breadth = top.shape
    count = rows.shape[1]
    lane = pl.BlockSpec((1, CHUNK), lambda i: (0, i))
    return pl.pallas_call(
        gather_kernel,
        grid=(count // CHUNK,),
        in_specs=[pl.BlockSpec((grid_rows, breadth), lambda i: (0, 0)), lane, lane],
        out_specs=lane,
        out_shape=jax.ShapeDtypeStruct((1, count), jnp.float32),
        cost_estimate=pl.CostEstimate(
            flops=2 * 3 * grid_rows * breadth * count,
            transcendentals=0,
            bytes_accessed=12 * count + 4 * grid_rows * breadth,
        ),
    )(top, rows, cols)


def stencil_kernel(total_rows, tables_ref, fields_ref, land_ref, river_ref, out_ref,
                   ks_s, alpha_s, store_s, old_s, cond_s, open_s, w_s, heads_s):
    layers, rows, breadth = out_ref.shape
    classes_n = tables_ref.shape[1]
    tile = lax.axis_index("tile")
    row_id = lax.broadcasted_iota(jnp.int32, (rows, breadth), 0)
    col_id = lax.broadcasted_iota(jnp.int32, (rows, breadth), 1)
    grow = tile * (rows - 2 * GHOST) - GHOST + row_id
    inside = (grow >= 0) & (grow < total_rows)
    land = jnp.where(inside, land_ref[...], 0.0)
    moves = []
    for axis, size, ident in ((0, rows, row_id), (1, breadth, col_id)):
        for shift in (1, size - 1):
            adjacent = jnp.abs(pltpu.roll(ident, shift, axis) - ident) == 1
            moves.append((axis, shift, adjacent))

    def shifted(x):
        return [jnp.where(adjacent, pltpu.roll(x, shift, axis), 0.0) for axis, shift, adjacent in moves]

    def init(z, carry):
        classes = fields_ref[1, z].astype(jnp.int32)
        looked = [jnp.zeros((rows, breadth), jnp.float32) for _ in range(3)]
        for class_id in range(classes_n):
            hit = classes == class_id
            looked = [jnp.where(hit, tables_ref[t, class_id], looked[t]) for t in range(3)]
        ks_s[z] = jnp.where(inside, looked[0], 1.0)
        alpha_s[z] = jnp.where(inside, looked[1], 0.0)
        store_s[z] = jnp.where(inside, looked[2], 1.0)
        old_s[z] = jnp.where(inside, fields_ref[0, z], 0.0)
        return carry

    lax.fori_loop(0, layers, init, 0)
    source = old_s
    count = 0
    for picard in range(ITERS):

        def conduct(z, carry, source=source):
            k = ks_s[z] * jnp.exp(alpha_s[z] * jnp.minimum(source[z], 0.0))
            cond_s[z] = k
            open_s[z] = k * land
            return carry

        lax.fori_loop(0, layers, conduct, 0)

        def weigh(z, carry):
            c = cond_s[z]
            co = open_s[z]
            above = jnp.maximum(z - 1, 0)
            below = jnp.minimum(z + 1, layers - 1)
            far = [jnp.where(z > 0, cond_s[above], 0.0), jnp.where(z < layers - 1, cond_s[below], 0.0)]
            far_open = [jnp.where(z > 0, open_s[above], 0.0), jnp.where(z < layers - 1, open_s[below], 0.0)]
            far += shifted(c)
            far_open += shifted(co)
            for i, (_, _, factor) in enumerate(NEIGHBOURS):
                w_s[i, z] = factor * 2.0 * co * far_open[i] / (c + far[i])
            return carry

        lax.fori_loop(0, layers, weigh, 0)
        for sweep in range(SWEEPS):
            last = picard == ITERS - 1 and sweep == SWEEPS - 1
            target = out_ref if last else heads_s.at[count % 2]
            count += 1

            def relax_layer(z, carry, source=source, target=target):
                h = source[z]
                above = jnp.maximum(z - 1, 0)
                below = jnp.minimum(z + 1, layers - 1)
                near = [jnp.where(z > 0, source[above], 0.0), jnp.where(z < layers - 1, source[below], 0.0)]
                near += shifted(h)
                st = store_s[z]
                total = st * old_s[z]
                diagonal_sum = st
                for i in range(len(NEIGHBOURS)):
                    w = w_s[i, z]
                    total = total + w * near[i]
                    diagonal_sum = diagonal_sum + w
                top = z == 0
                total = total + GRAVITY * (w_s[0, z] - w_s[1, z]) + jnp.where(top, river_ref[1], 0.0)
                target[z] = total / (diagonal_sum + jnp.where(top, river_ref[0], 0.0))
                return carry

            lax.fori_loop(0, layers, relax_layer, 0)
            source = target


def stencil(tables, fields, land, river, total_rows):
    _, layers, rows, breadth = fields.shape
    vmem = pl.BlockSpec(memory_space=pltpu.VMEM)
    field = pltpu.VMEM((layers, rows, breadth), jnp.float32)
    cells = layers * rows * breadth
    return pl.pallas_call(
        functools.partial(stencil_kernel, total_rows),
        in_specs=[pl.BlockSpec(memory_space=pltpu.SMEM), vmem, vmem, vmem],
        out_specs=vmem,
        out_shape=jax.ShapeDtypeStruct((layers, rows, breadth), jnp.float32),
        scratch_shapes=[field] * 6
        + [pltpu.VMEM((6, layers, rows, breadth), jnp.float32), pltpu.VMEM((2, layers, rows, breadth), jnp.float32)],
        compiler_params=pltpu.CompilerParams(vmem_limit_bytes=48 * 1024 * 1024),
        cost_estimate=pl.CostEstimate(flops=400 * cells, transcendentals=2 * cells, bytes_accessed=12 * cells),
    )(tables, fields, land, river)


def with_ghost(block, axis, dim, width):
    count = lax.axis_size(axis)
    forward = [(i, i + 1) for i in range(count - 1)]
    backward = [(i + 1, i) for i in range(count - 1)]
    size = block.shape[dim]
    above = lax.ppermute(lax.slice_in_dim(block, size - width, size, axis=dim), axis, forward)
    below = lax.ppermute(lax.slice_in_dim(block, 0, width, axis=dim), axis, backward)
    return jnp.concatenate([above, block, below], axis=dim)


def on_device(
    head_start,
    soil_class,
    land_mask,
    ks_table,
    alpha_table,
    store_table,
    section,
    cross_owner,
    cross_local,
    node_cell,
    bed_cond,
):
    own_layers, across, breadth = head_start.shape
    reach_rows, node_count = section.shape
    tile_count = lax.axis_size("tile")
    layer_count = lax.axis_size("layer")
    tile = lax.axis_index("tile")
    layer = lax.axis_index("layer")
    quarter = node_count // layer_count
    node_first = layer * quarter

    planes = jnp.concatenate(
        [head_start, soil_class.astype(jnp.float32), land_mask.astype(jnp.float32)[None]], axis=0
    )
    planes = with_ghost(planes, "tile", 1, GHOST)
    extent = across + 2 * GHOST
    fields = planes[: 2 * own_layers].reshape(2, own_layers, extent, breadth)
    fields = lax.all_gather(fields, "layer", axis=1, tiled=True)
    owners = cross_owner[0]
    positions = cross_local[0]
    node_cells = node_cell[0]
    bed_given = bed_cond[0]
    slots = owners.shape[0]
    per_owner = slots // tile_count
    order = jnp.arange(slots, dtype=jnp.int32)
    same = owners[:, None] == owners[None, :]
    rank = jnp.sum((same & (order[None, :] < order[:, None])).astype(jnp.int32), axis=1)
    place = owners * per_owner + rank
    at_place = place[None, :] == order[:, None]
    wanted = jnp.sum(jnp.where(at_place, positions[None, :], 0), axis=1)
    asked = lax.all_to_all(wanted, "tile", 0, 0, tiled=True)
    reply = jnp.take(section, asked, axis=0)
    sorted_section = lax.all_to_all(reply, "tile", 0, 0, tiled=True)
    slot_section = jnp.take(sorted_section, place, axis=0)

    in_tile = node_cells >= 0
    bed_terms = jnp.where(in_tile, bed_given, 0.0)
    cell_rows = jnp.where(in_tile, node_cells // breadth, -1)
    cell_cols = jnp.where(in_tile, node_cells % breadth, 0)
    top_diag, top_rhs = river_terms(
        cell_rows.reshape(1, -1),
        cell_cols.reshape(1, -1),
        bed_terms.reshape(1, -1),
        (bed_terms * slot_section).reshape(1, -1),
        across,
        breadth,
    )
    river = with_ghost(jnp.stack([top_diag, top_rhs]), "tile", 1, GHOST)
    tables = jnp.stack([ks_table, alpha_table, store_table])
    head = stencil(tables, fields, planes[2 * own_layers], river, tile_count * across)
    kept = lax.dynamic_slice_in_dim(head[:, GHOST : GHOST + across], layer * own_layers, own_layers, 0)

    top_head = head[0, GHOST : GHOST + across]
    my_cells = lax.dynamic_slice_in_dim(node_cells, node_first, quarter, 1)
    my_bed = lax.dynamic_slice_in_dim(bed_given, node_first, quarter, 1)
    my_section = lax.dynamic_slice_in_dim(slot_section, node_first, quarter, 1)
    my_inside = my_cells >= 0
    picked = node_heads(
        top_head,
        jnp.where(my_inside, my_cells // breadth, -1).reshape(1, -1),
        jnp.where(my_inside, my_cells % breadth, 0).reshape(1, -1),
    ).reshape(slots, quarter)
    slot_in = jnp.where(my_inside, my_bed * (picked - my_section), 0.0)
    sorted_in = jnp.take(slot_in, jnp.sum(jnp.where(at_place, order[None, :], 0), axis=1), axis=0)
    arrived = lax.all_to_all(sorted_in, "tile", 0, 0, tiled=True)
    target = asked[None, :] == jnp.arange(reach_rows, dtype=jnp.int32)[:, None]
    inflow = jnp.sum(jnp.where(target[:, :, None], arrived[None], 0.0), axis=1)
    return (kept, inflow)


def solution(mesh):
    placed = (
        P("layer", "tile", None),
        P("layer", "tile", None),
        P("tile", None),
        P(),
        P(),
        P(),
        P("tile", None),
        P("tile", None),
        P("tile", None),
        P("tile", None, None),
        P("tile", None, None),
    )
    return jax.shard_map(
        on_device,
        mesh=mesh,
        in_specs=placed,
        out_specs=(P("layer", "tile", None), P("tile", "layer")),
        check_vma=False,
    )
```

```python
import functools

import jax
import jax.numpy as jnp
from jax import lax
from jax.experimental import pallas as pl
from jax.experimental.pallas import tpu as pltpu
from jax.sharding import PartitionSpec as P

ITERS = 2
SWEEPS = 3
GHOST = 8


LATERAL = 1.0
VERTICAL = 2.0
GRAVITY = 1.0
NEIGHBOURS = (
    (0, -1, VERTICAL),
    (0, 1, VERTICAL),
    (1, -1, LATERAL),
    (1, 1, LATERAL),
    (2, -1, LATERAL),
    (2, 1, LATERAL),
)
CHUNK = 512


def beside(padded, axis_id, step):
    spans = [slice(1, -1), slice(1, -1), slice(1, -1)]
    spans[axis_id] = slice(1 + step, padded.shape[axis_id] - 1 + step)
    return padded[tuple(spans)]


def neighbor_weights(cond_pad, open_pad):
    centre = cond_pad[1:-1, 1:-1, 1:-1]
    centre_open = open_pad[1:-1, 1:-1, 1:-1]
    result = []
    for axis_id, step, factor in NEIGHBOURS:
        far = beside(cond_pad, axis_id, step)
        far_open = beside(open_pad, axis_id, step)
        result.append(factor * 2.0 * centre_open * far_open / (centre + far))
    return result


def relax(head_pad, weights, store, head_old, riv_diag, riv_rhs):
    total = store * head_old
    diagonal_sum = store
    for weight, (axis_id, step, factor) in zip(weights, NEIGHBOURS):
        total = total + weight * beside(head_pad, axis_id, step)
        diagonal_sum = diagonal_sum + weight
    total = total + GRAVITY * (weights[0] - weights[1]) + riv_rhs
    return total / (diagonal_sum + riv_diag)


def lookup(values_table, classes):
    result = jnp.zeros(classes.shape, jnp.float32)
    for class_id in range(values_table.shape[0]):
        result = jnp.where(classes == class_id, values_table[class_id], result)
    return result


def split3(value):
    high = value.astype(jnp.bfloat16).astype(jnp.float32)
    rest = value - high
    middle = rest.astype(jnp.bfloat16).astype(jnp.float32)
    low = rest - middle
    return high, middle, low


def scatter_kernel(rows_ref, cols_ref, diag_in_ref, rhs_in_ref, diag_ref, rhs_ref, acc_ref):
    step = pl.program_id(0)
    grid_rows, breadth = diag_ref.shape
    chunk = rows_ref.shape[1]

    @pl.when(step == 0)
    def _():
        acc_ref[...] = jnp.zeros_like(acc_ref)

    rows = rows_ref[...]

    @pl.when(jnp.max(rows) >= 0)
    def _():
        hit = lax.broadcasted_iota(jnp.int32, (grid_rows, chunk), 0) == rows
        pieces = []
        for value in (diag_in_ref[...], rhs_in_ref[...]):
            for piece in split3(value):
                pieces.append(jnp.where(hit, piece, 0.0).astype(jnp.bfloat16))
        left = jnp.concatenate(pieces, axis=0)
        cols = jnp.transpose(jnp.broadcast_to(cols_ref[...], (8, chunk)))[:, 0:1]
        column_hit = lax.broadcasted_iota(jnp.int32, (chunk, breadth), 1) == cols
        right = jnp.where(column_hit, 1.0, 0.0).astype(jnp.bfloat16)
        acc_ref[...] += jnp.dot(left, right, preferred_element_type=jnp.float32)

    @pl.when(step == pl.num_programs(0) - 1)
    def _():
        acc = acc_ref[...]
        g = grid_rows
        diag_ref[...] = acc[0:g] + acc[g : 2 * g] + acc[2 * g : 3 * g]
        rhs_ref[...] = acc[3 * g : 4 * g] + acc[4 * g : 5 * g] + acc[5 * g : 6 * g]


def river_terms(rows, cols, diag_values, rhs_values, grid_rows, breadth):
    count = rows.shape[1]
    lane = pl.BlockSpec((1, CHUNK), lambda i: (0, i))
    whole = pl.BlockSpec((grid_rows, breadth), lambda i: (0, 0))
    return pl.pallas_call(
        scatter_kernel,
        grid=(count // CHUNK,),
        in_specs=[lane, lane, lane, lane],
        out_specs=[whole, whole],
        out_shape=[
            jax.ShapeDtypeStruct((grid_rows, breadth), jnp.float32),
            jax.ShapeDtypeStruct((grid_rows, breadth), jnp.float32),
        ],
        scratch_shapes=[pltpu.VMEM((6 * grid_rows, breadth), jnp.float32)],
        cost_estimate=pl.CostEstimate(
            flops=2 * 6 * grid_rows * breadth * count,
            transcendentals=0,
            bytes_accessed=16 * count + 8 * grid_rows * breadth,
        ),
    )(rows, cols, diag_values, rhs_values)


def gather_kernel(top_ref, rows_ref, cols_ref, out_ref):
    grid_rows, breadth = top_ref.shape
    chunk = rows_ref.shape[1]
    stacked = jnp.concatenate(
        [piece.astype(jnp.bfloat16) for piece in split3(top_ref[...])], axis=0
    )
    cols = cols_ref[...]
    column_hit = lax.broadcasted_iota(jnp.int32, (breadth, chunk), 0) == cols
    right = jnp.where(column_hit, 1.0, 0.0).astype(jnp.bfloat16)
    picked = jnp.dot(stacked, right, preferred_element_type=jnp.float32)
    g = grid_rows
    by_row = picked[0:g] + picked[g : 2 * g] + picked[2 * g : 3 * g]
    rows = rows_ref[...]
    hit = lax.broadcasted_iota(jnp.int32, (grid_rows, chunk), 0) == rows
    out_ref[...] = jnp.sum(jnp.where(hit, by_row, 0.0), axis=0, keepdims=True)


def node_heads(top, rows, cols):
    grid_rows, breadth = top.shape
    count = rows.shape[1]
    lane = pl.BlockSpec((1, CHUNK), lambda i: (0, i))
    return pl.pallas_call(
        gather_kernel,
        grid=(count // CHUNK,),
        in_specs=[pl.BlockSpec((grid_rows, breadth), lambda i: (0, 0)), lane, lane],
        out_specs=lane,
        out_shape=jax.ShapeDtypeStruct((1, count), jnp.float32),
        cost_estimate=pl.CostEstimate(
            flops=2 * 3 * grid_rows * breadth * count,
            transcendentals=0,
            bytes_accessed=12 * count + 4 * grid_rows * breadth,
        ),
    )(top, rows, cols)


def stencil_kernel(total_rows, tables_ref, fields_ref, land_ref, river_ref, out_ref,
                   ks_s, alpha_s, store_s, old_s, cond_s, open_s, w_s, heads_s):
    layers, rows, breadth = out_ref.shape
    classes_n = tables_ref.shape[1]
    tile = lax.axis_index("tile")
    row_id = lax.broadcasted_iota(jnp.int32, (rows, breadth), 0)
    col_id = lax.broadcasted_iota(jnp.int32, (rows, breadth), 1)
    grow = tile * (rows - 2 * GHOST) - GHOST + row_id
    inside = (grow >= 0) & (grow < total_rows)
    land = jnp.where(inside, land_ref[...], 0.0)
    moves = []
    for axis, size, ident in ((0, rows, row_id), (1, breadth, col_id)):
        for shift in (1, size - 1):
            adjacent = jnp.abs(pltpu.roll(ident, shift, axis) - ident) == 1
            moves.append((axis, shift, adjacent))

    def shifted(x):
        return [jnp.where(adjacent, pltpu.roll(x, shift, axis), 0.0) for axis, shift, adjacent in moves]

    def init(z, carry):
        classes = fields_ref[1, z].astype(jnp.int32)
        looked = [jnp.zeros((rows, breadth), jnp.float32) for _ in range(3)]
        for class_id in range(classes_n):
            hit = classes == class_id
            looked = [jnp.where(hit, tables_ref[t, class_id], looked[t]) for t in range(3)]
        ks_s[z] = jnp.where(inside, looked[0], 1.0)
        alpha_s[z] = jnp.where(inside, looked[1], 0.0)
        store_s[z] = jnp.where(inside, looked[2], 1.0)
        old_s[z] = jnp.where(inside, fields_ref[0, z], 0.0)
        return carry

    lax.fori_loop(0, layers, init, 0)
    source = old_s
    count = 0
    for picard in range(ITERS):

        def conduct(z, carry, source=source):
            k = ks_s[z] * jnp.exp(alpha_s[z] * jnp.minimum(source[z], 0.0))
            cond_s[z] = k
            open_s[z] = k * land
            return carry

        lax.fori_loop(0, layers, conduct, 0)

        def weigh(z, carry):
            c = cond_s[z]
            co = open_s[z]
            above = jnp.maximum(z - 1, 0)
            below = jnp.minimum(z + 1, layers - 1)
            far = [jnp.where(z > 0, cond_s[above], 0.0), jnp.where(z < layers - 1, cond_s[below], 0.0)]
            far_open = [jnp.where(z > 0, open_s[above], 0.0), jnp.where(z < layers - 1, open_s[below], 0.0)]
            far += shifted(c)
            far_open += shifted(co)
            for i, (_, _, factor) in enumerate(NEIGHBOURS):
                w_s[i, z] = factor * 2.0 * co * far_open[i] / (c + far[i])
            return carry

        lax.fori_loop(0, layers, weigh, 0)
        for sweep in range(SWEEPS):
            last = picard == ITERS - 1 and sweep == SWEEPS - 1
            target = out_ref if last else heads_s.at[count % 2]
            count += 1

            def relax_layer(z, carry, source=source, target=target):
                h = source[z]
                above = jnp.maximum(z - 1, 0)
                below = jnp.minimum(z + 1, layers - 1)
                near = [jnp.where(z > 0, source[above], 0.0), jnp.where(z < layers - 1, source[below], 0.0)]
                near += shifted(h)
                st = store_s[z]
                total = st * old_s[z]
                diagonal_sum = st
                for i in range(len(NEIGHBOURS)):
                    w = w_s[i, z]
                    total = total + w * near[i]
                    diagonal_sum = diagonal_sum + w
                top = z == 0
                total = total + GRAVITY * (w_s[0, z] - w_s[1, z]) + jnp.where(top, river_ref[1], 0.0)
                target[z] = total / (diagonal_sum + jnp.where(top, river_ref[0], 0.0))
                return carry

            lax.fori_loop(0, layers, relax_layer, 0)
            source = target


def stencil(tables, fields, land, river, total_rows):
    _, layers, rows, breadth = fields.shape
    vmem = pl.BlockSpec(memory_space=pltpu.VMEM)
    field = pltpu.VMEM((layers, rows, breadth), jnp.float32)
    cells = layers * rows * breadth
    return pl.pallas_call(
        functools.partial(stencil_kernel, total_rows),
        in_specs=[pl.BlockSpec(memory_space=pltpu.SMEM), vmem, vmem, vmem],
        out_specs=vmem,
        out_shape=jax.ShapeDtypeStruct((layers, rows, breadth), jnp.float32),
        scratch_shapes=[field] * 6
        + [pltpu.VMEM((6, layers, rows, breadth), jnp.float32), pltpu.VMEM((2, layers, rows, breadth), jnp.float32)],
        compiler_params=pltpu.CompilerParams(vmem_limit_bytes=48 * 1024 * 1024),
        cost_estimate=pl.CostEstimate(flops=400 * cells, transcendentals=2 * cells, bytes_accessed=12 * cells),
    )(tables, fields, land, river)


def with_ghost(block, axis, dim, width):
    count = lax.axis_size(axis)
    forward = [(i, i + 1) for i in range(count - 1)]
    backward = [(i + 1, i) for i in range(count - 1)]
    size = block.shape[dim]
    above = lax.ppermute(lax.slice_in_dim(block, size - width, size, axis=dim), axis, forward)
    below = lax.ppermute(lax.slice_in_dim(block, 0, width, axis=dim), axis, backward)
    return jnp.concatenate([above, block, below], axis=dim)


def on_device(
    head_start,
    soil_class,
    land_mask,
    ks_table,
    alpha_table,
    store_table,
    section,
    cross_owner,
    cross_local,
    node_cell,
    bed_cond,
):
    own_layers, across, breadth = head_start.shape
    reach_rows, node_count = section.shape
    tile_count = lax.axis_size("tile")
    layer_count = lax.axis_size("layer")
    tile = lax.axis_index("tile")
    layer = lax.axis_index("layer")
    quarter = node_count // layer_count
    node_first = layer * quarter

    planes = jnp.concatenate(
        [head_start, soil_class.astype(jnp.float32), land_mask.astype(jnp.float32)[None]], axis=0
    )
    planes = with_ghost(planes, "tile", 1, GHOST)
    extent = across + 2 * GHOST
    fields = planes[: 2 * own_layers].reshape(2, own_layers, extent, breadth)
    fields = lax.all_gather(fields, "layer", axis=1, tiled=True)
    owners = cross_owner[0]
    positions = cross_local[0]
    node_cells = node_cell[0]
    bed_given = bed_cond[0]
    slots = owners.shape[0]
    per_owner = slots // tile_count
    order = jnp.arange(slots, dtype=jnp.int32)
    same = owners[:, None] == owners[None, :]
    rank = jnp.sum((same & (order[None, :] < order[:, None])).astype(jnp.int32), axis=1)
    place = owners * per_owner + rank
    at_place = place[None, :] == order[:, None]
    wanted = jnp.sum(jnp.where(at_place, positions[None, :], 0), axis=1)
    asked = lax.all_to_all(wanted, "tile", 0, 0, tiled=True)
    reply = jnp.take(section, asked, axis=0)
    sorted_section = lax.all_to_all(reply, "tile", 0, 0, tiled=True)
    slot_section = jnp.take(sorted_section, place, axis=0)

    in_tile = node_cells >= 0
    bed_terms = jnp.where(in_tile, bed_given, 0.0)
    cell_rows = jnp.where(in_tile, node_cells // breadth, -1)
    cell_cols = jnp.where(in_tile, node_cells % breadth, 0)
    top_diag, top_rhs = river_terms(
        cell_rows.reshape(1, -1),
        cell_cols.reshape(1, -1),
        bed_terms.reshape(1, -1),
        (bed_terms * slot_section).reshape(1, -1),
        across,
        breadth,
    )
    river = with_ghost(jnp.stack([top_diag, top_rhs]), "tile", 1, GHOST)
    tables = jnp.stack([ks_table, alpha_table, store_table])
    head = stencil(tables, fields, planes[2 * own_layers], river, tile_count * across)
    kept = lax.dynamic_slice_in_dim(head[:, GHOST : GHOST + across], layer * own_layers, own_layers, 0)

    top_head = head[0, GHOST : GHOST + across]
    my_cells = lax.dynamic_slice_in_dim(node_cells, node_first, quarter, 1)
    my_bed = lax.dynamic_slice_in_dim(bed_given, node_first, quarter, 1)
    my_section = lax.dynamic_slice_in_dim(slot_section, node_first, quarter, 1)
    my_inside = my_cells >= 0
    picked = node_heads(
        top_head,
        jnp.where(my_inside, my_cells // breadth, -1).reshape(1, -1),
        jnp.where(my_inside, my_cells % breadth, 0).reshape(1, -1),
    ).reshape(slots, quarter)
    slot_in = jnp.where(my_inside, my_bed * (picked - my_section), 0.0)
    sorted_in = jnp.take(slot_in, jnp.sum(jnp.where(at_place, order[None, :], 0), axis=1), axis=0)
    arrived = lax.all_to_all(sorted_in, "tile", 0, 0, tiled=True)
    target = asked[None, :] == jnp.arange(reach_rows, dtype=jnp.int32)[:, None]
    inflow = jnp.sum(jnp.where(target[:, :, None], arrived[None], 0.0), axis=1)
    return (kept, inflow)


def solution(mesh):
    placed = (
        P("layer", "tile", None),
        P("layer", "tile", None),
        P("tile", None),
        P(),
        P(),
        P(),
        P("tile", None),
        P("tile", None),
        P("tile", None),
        P("tile", None, None),
        P("tile", None, None),
    )
    return jax.shard_map(
        on_device,
        mesh=mesh,
        in_specs=placed,
        out_specs=(P("layer", "tile", None), P("tile", "layer")),
        check_vma=False,
    )
```

```python
import functools

import jax
import jax.numpy as jnp
from jax import lax
from jax.experimental import pallas as pl
from jax.experimental.pallas import tpu as pltpu
from jax.sharding import PartitionSpec as P

ITERS = 2
SWEEPS = 3
GHOST = 8


LATERAL = 1.0
VERTICAL = 2.0
GRAVITY = 1.0
NEIGHBOURS = (
    (0, -1, VERTICAL),
    (0, 1, VERTICAL),
    (1, -1, LATERAL),
    (1, 1, LATERAL),
    (2, -1, LATERAL),
    (2, 1, LATERAL),
)
CHUNK = 512


def beside(padded, axis_id, step):
    spans = [slice(1, -1), slice(1, -1), slice(1, -1)]
    spans[axis_id] = slice(1 + step, padded.shape[axis_id] - 1 + step)
    return padded[tuple(spans)]


def neighbor_weights(cond_pad, open_pad):
    centre = cond_pad[1:-1, 1:-1, 1:-1]
    centre_open = open_pad[1:-1, 1:-1, 1:-1]
    result = []
    for axis_id, step, factor in NEIGHBOURS:
        far = beside(cond_pad, axis_id, step)
        far_open = beside(open_pad, axis_id, step)
        result.append(factor * 2.0 * centre_open * far_open / (centre + far))
    return result


def relax(head_pad, weights, store, head_old, riv_diag, riv_rhs):
    total = store * head_old
    diagonal_sum = store
    for weight, (axis_id, step, factor) in zip(weights, NEIGHBOURS):
        total = total + weight * beside(head_pad, axis_id, step)
        diagonal_sum = diagonal_sum + weight
    total = total + GRAVITY * (weights[0] - weights[1]) + riv_rhs
    return total / (diagonal_sum + riv_diag)


def lookup(values_table, classes):
    result = jnp.zeros(classes.shape, jnp.float32)
    for class_id in range(values_table.shape[0]):
        result = jnp.where(classes == class_id, values_table[class_id], result)
    return result


def split3(value):
    high = value.astype(jnp.bfloat16).astype(jnp.float32)
    rest = value - high
    middle = rest.astype(jnp.bfloat16).astype(jnp.float32)
    low = rest - middle
    return high, middle, low


def scatter_kernel(rows_ref, cols_ref, diag_in_ref, rhs_in_ref, diag_ref, rhs_ref, acc_ref):
    step = pl.program_id(0)
    grid_rows, breadth = diag_ref.shape
    chunk = rows_ref.shape[1]

    @pl.when(step == 0)
    def _():
        acc_ref[...] = jnp.zeros_like(acc_ref)

    rows = rows_ref[...]

    @pl.when(jnp.max(rows) >= 0)
    def _():
        hit = lax.broadcasted_iota(jnp.int32, (grid_rows, chunk), 0) == rows
        pieces = []
        for value in (diag_in_ref[...], rhs_in_ref[...]):
            for piece in split3(value):
                pieces.append(jnp.where(hit, piece, 0.0).astype(jnp.bfloat16))
        left = jnp.concatenate(pieces, axis=0)
        cols = cols_ref[...]
        column_hit = lax.broadcasted_iota(jnp.int32, (breadth, chunk), 0) == cols
        right = jnp.where(column_hit, 1.0, 0.0).astype(jnp.bfloat16)
        acc_ref[...] += lax.dot_general(
            left, right, (((1,), (1,)), ((), ())), preferred_element_type=jnp.float32
        )

    @pl.when(step == pl.num_programs(0) - 1)
    def _():
        acc = acc_ref[...]
        g = grid_rows
        diag_ref[...] = acc[0:g] + acc[g : 2 * g] + acc[2 * g : 3 * g]
        rhs_ref[...] = acc[3 * g : 4 * g] + acc[4 * g : 5 * g] + acc[5 * g : 6 * g]


def river_terms(rows, cols, diag_values, rhs_values, grid_rows, breadth):
    count = rows.shape[1]
    lane = pl.BlockSpec((1, CHUNK), lambda i: (0, i))
    whole = pl.BlockSpec((grid_rows, breadth), lambda i: (0, 0))
    return pl.pallas_call(
        scatter_kernel,
        grid=(count // CHUNK,),
        in_specs=[lane, lane, lane, lane],
        out_specs=[whole, whole],
        out_shape=[
            jax.ShapeDtypeStruct((grid_rows, breadth), jnp.float32),
            jax.ShapeDtypeStruct((grid_rows, breadth), jnp.float32),
        ],
        scratch_shapes=[pltpu.VMEM((6 * grid_rows, breadth), jnp.float32)],
        cost_estimate=pl.CostEstimate(
            flops=2 * 6 * grid_rows * breadth * count,
            transcendentals=0,
            bytes_accessed=16 * count + 8 * grid_rows * breadth,
        ),
    )(rows, cols, diag_values, rhs_values)


def gather_kernel(top_ref, rows_ref, cols_ref, out_ref):
    grid_rows, breadth = top_ref.shape
    chunk = rows_ref.shape[1]
    stacked = jnp.concatenate(
        [piece.astype(jnp.bfloat16) for piece in split3(top_ref[...])], axis=0
    )
    cols = cols_ref[...]
    column_hit = lax.broadcasted_iota(jnp.int32, (breadth, chunk), 0) == cols
    right = jnp.where(column_hit, 1.0, 0.0).astype(jnp.bfloat16)
    picked = jnp.dot(stacked, right, preferred_element_type=jnp.float32)
    g = grid_rows
    by_row = picked[0:g] + picked[g : 2 * g] + picked[2 * g : 3 * g]
    rows = rows_ref[...]
    hit = lax.broadcasted_iota(jnp.int32, (grid_rows, chunk), 0) == rows
    out_ref[...] = jnp.sum(jnp.where(hit, by_row, 0.0), axis=0, keepdims=True)


def node_heads(top, rows, cols):
    grid_rows, breadth = top.shape
    count = rows.shape[1]
    lane = pl.BlockSpec((1, CHUNK), lambda i: (0, i))
    return pl.pallas_call(
        gather_kernel,
        grid=(count // CHUNK,),
        in_specs=[pl.BlockSpec((grid_rows, breadth), lambda i: (0, 0)), lane, lane],
        out_specs=lane,
        out_shape=jax.ShapeDtypeStruct((1, count), jnp.float32),
        cost_estimate=pl.CostEstimate(
            flops=2 * 3 * grid_rows * breadth * count,
            transcendentals=0,
            bytes_accessed=12 * count + 4 * grid_rows * breadth,
        ),
    )(top, rows, cols)


def stencil_kernel(total_rows, tables_ref, fields_ref, land_ref, river_ref, out_ref,
                   ks_s, alpha_s, store_s, old_s, cond_s, open_s, w_s, heads_s):
    layers, rows, breadth = out_ref.shape
    classes_n = tables_ref.shape[1]
    tile = lax.axis_index("tile")
    row_id = lax.broadcasted_iota(jnp.int32, (rows, breadth), 0)
    col_id = lax.broadcasted_iota(jnp.int32, (rows, breadth), 1)
    grow = tile * (rows - 2 * GHOST) - GHOST + row_id
    inside = (grow >= 0) & (grow < total_rows)
    land = jnp.where(inside, land_ref[...], 0.0)
    moves = []
    for axis, size, ident in ((0, rows, row_id), (1, breadth, col_id)):
        for shift in (1, size - 1):
            adjacent = jnp.abs(pltpu.roll(ident, shift, axis) - ident) == 1
            moves.append((axis, shift, adjacent))

    def shifted(x):
        return [jnp.where(adjacent, pltpu.roll(x, shift, axis), 0.0) for axis, shift, adjacent in moves]

    def init(z, carry):
        classes = fields_ref[1, z].astype(jnp.int32)
        looked = [jnp.zeros((rows, breadth), jnp.float32) for _ in range(3)]
        for class_id in range(classes_n):
            hit = classes == class_id
            looked = [jnp.where(hit, tables_ref[t, class_id], looked[t]) for t in range(3)]
        ks_s[z] = jnp.where(inside, looked[0], 1.0)
        alpha_s[z] = jnp.where(inside, looked[1], 0.0)
        store_s[z] = jnp.where(inside, looked[2], 1.0)
        old_s[z] = jnp.where(inside, fields_ref[0, z], 0.0)
        return carry

    lax.fori_loop(0, layers, init, 0)
    source = old_s
    count = 0
    for picard in range(ITERS):

        def conduct(z, carry, source=source):
            k = ks_s[z] * jnp.exp(alpha_s[z] * jnp.minimum(source[z], 0.0))
            cond_s[z] = k
            open_s[z] = k * land
            return carry

        lax.fori_loop(0, layers, conduct, 0)

        def weigh(z, carry):
            c = cond_s[z]
            co = open_s[z]
            above = jnp.maximum(z - 1, 0)
            below = jnp.minimum(z + 1, layers - 1)
            far = [jnp.where(z > 0, cond_s[above], 0.0), jnp.where(z < layers - 1, cond_s[below], 0.0)]
            far_open = [jnp.where(z > 0, open_s[above], 0.0), jnp.where(z < layers - 1, open_s[below], 0.0)]
            far += shifted(c)
            far_open += shifted(co)
            for i, (_, _, factor) in enumerate(NEIGHBOURS):
                w_s[i, z] = factor * 2.0 * co * far_open[i] / (c + far[i])
            return carry

        lax.fori_loop(0, layers, weigh, 0)
        for sweep in range(SWEEPS):
            last = picard == ITERS - 1 and sweep == SWEEPS - 1
            target = out_ref if last else heads_s.at[count % 2]
            count += 1

            def relax_layer(z, carry, source=source, target=target):
                h = source[z]
                above = jnp.maximum(z - 1, 0)
                below = jnp.minimum(z + 1, layers - 1)
                near = [jnp.where(z > 0, source[above], 0.0), jnp.where(z < layers - 1, source[below], 0.0)]
                near += shifted(h)
                st = store_s[z]
                total = st * old_s[z]
                diagonal_sum = st
                for i in range(len(NEIGHBOURS)):
                    w = w_s[i, z]
                    total = total + w * near[i]
                    diagonal_sum = diagonal_sum + w
                top = z == 0
                total = total + GRAVITY * (w_s[0, z] - w_s[1, z]) + jnp.where(top, river_ref[1], 0.0)
                target[z] = total / (diagonal_sum + jnp.where(top, river_ref[0], 0.0))
                return carry

            lax.fori_loop(0, layers, relax_layer, 0)
            source = target


def stencil(tables, fields, land, river, total_rows):
    _, layers, rows, breadth = fields.shape
    vmem = pl.BlockSpec(memory_space=pltpu.VMEM)
    field = pltpu.VMEM((layers, rows, breadth), jnp.float32)
    cells = layers * rows * breadth
    return pl.pallas_call(
        functools.partial(stencil_kernel, total_rows),
        in_specs=[pl.BlockSpec(memory_space=pltpu.SMEM), vmem, vmem, vmem],
        out_specs=vmem,
        out_shape=jax.ShapeDtypeStruct((layers, rows, breadth), jnp.float32),
        scratch_shapes=[field] * 6
        + [pltpu.VMEM((6, layers, rows, breadth), jnp.float32), pltpu.VMEM((2, layers, rows, breadth), jnp.float32)],
        compiler_params=pltpu.CompilerParams(vmem_limit_bytes=48 * 1024 * 1024),
        cost_estimate=pl.CostEstimate(flops=400 * cells, transcendentals=2 * cells, bytes_accessed=12 * cells),
    )(tables, fields, land, river)


def exchange_kernel(x_ref, y_ref, landed, send_sem, recv_sem, local_sem):
    tiles = x_ref.shape[0]
    me = lax.axis_index("tile")
    layer = lax.axis_index("layer")
    barrier = pltpu.get_barrier_semaphore()

    def greet(i, carry):
        peer = lax.rem(me + i, tiles)
        pl.semaphore_signal(barrier, inc=1, device_id=(peer, layer), device_id_type=pl.DeviceIdType.MESH)
        return carry

    lax.fori_loop(1, tiles, greet, 0)
    pl.semaphore_wait(barrier, tiles - 1)

    def outgoing(peer):
        return pltpu.make_async_remote_copy(
            src_ref=x_ref.at[peer],
            dst_ref=landed.at[me],
            send_sem=send_sem.at[peer],
            recv_sem=recv_sem.at[me],
            device_id=(peer, layer),
            device_id_type=pl.DeviceIdType.MESH,
        )

    def incoming(source):
        return pltpu.make_async_remote_copy(
            src_ref=x_ref.at[source],
            dst_ref=landed.at[source],
            send_sem=send_sem.at[source],
            recv_sem=recv_sem.at[source],
            device_id=(source, layer),
            device_id_type=pl.DeviceIdType.MESH,
        )

    def send(i, carry):
        outgoing(lax.rem(me + i, tiles)).start()
        return carry

    lax.fori_loop(1, tiles, send, 0)
    own = pltpu.make_async_copy(x_ref.at[me], landed.at[me], local_sem)
    own.start()
    own.wait()

    def finish(i, carry):
        outgoing(lax.rem(me + i, tiles)).wait_send()
        incoming(lax.rem(me + tiles - i, tiles)).wait_recv()
        return carry

    lax.fori_loop(1, tiles, finish, 0)
    y_ref[...] = landed[...]


def exchange(x, collective):
    tiles = x.shape[0]
    vmem = pl.BlockSpec(memory_space=pltpu.VMEM)
    return pl.pallas_call(
        exchange_kernel,
        in_specs=[vmem],
        out_specs=vmem,
        out_shape=jax.ShapeDtypeStruct(x.shape, x.dtype),
        scratch_shapes=[
            pltpu.VMEM(x.shape, x.dtype),
            pltpu.SemaphoreType.DMA((tiles,)),
            pltpu.SemaphoreType.DMA((tiles,)),
            pltpu.SemaphoreType.DMA,
        ],
        compiler_params=pltpu.CompilerParams(collective_id=collective, has_side_effects=True),
    )(x)


def with_ghost(block, axis, dim, width):
    count = lax.axis_size(axis)
    forward = [(i, i + 1) for i in range(count - 1)]
    backward = [(i + 1, i) for i in range(count - 1)]
    size = block.shape[dim]
    above = lax.ppermute(lax.slice_in_dim(block, size - width, size, axis=dim), axis, forward)
    below = lax.ppermute(lax.slice_in_dim(block, 0, width, axis=dim), axis, backward)
    return jnp.concatenate([above, block, below], axis=dim)


def on_device(
    head_start,
    soil_class,
    land_mask,
    ks_table,
    alpha_table,
    store_table,
    section,
    cross_owner,
    cross_local,
    node_cell,
    bed_cond,
):
    own_layers, across, breadth = head_start.shape
    reach_rows, node_count = section.shape
    tile_count = lax.axis_size("tile")
    layer_count = lax.axis_size("layer")
    tile = lax.axis_index("tile")
    layer = lax.axis_index("layer")
    quarter = node_count // layer_count
    node_first = layer * quarter

    planes = jnp.concatenate(
        [head_start, soil_class.astype(jnp.float32), land_mask.astype(jnp.float32)[None]], axis=0
    )
    planes = with_ghost(planes, "tile", 1, GHOST)
    extent = across + 2 * GHOST
    fields = planes[: 2 * own_layers].reshape(2, own_layers, extent, breadth)
    fields = lax.all_gather(fields, "layer", axis=1, tiled=True)
    owners = cross_owner[0]
    positions = cross_local[0]
    node_cells = node_cell[0]
    bed_given = bed_cond[0]
    slots = owners.shape[0]
    per_owner = slots // tile_count
    order = jnp.arange(slots, dtype=jnp.int32)
    same = owners[:, None] == owners[None, :]
    rank = jnp.sum((same & (order[None, :] < order[:, None])).astype(jnp.int32), axis=1)
    place = owners * per_owner + rank
    at_place = place[None, :] == order[:, None]
    wanted = jnp.sum(jnp.where(at_place, positions[None, :], 0), axis=1)
    asked = exchange(wanted.reshape(tile_count, per_owner, 1), 0).reshape(slots)
    reply = jnp.take(section, asked, axis=0)
    sorted_section = exchange(reply.reshape(tile_count, per_owner, node_count), 1).reshape(slots, node_count)
    slot_section = jnp.take(sorted_section, place, axis=0)

    in_tile = node_cells >= 0
    bed_terms = jnp.where(in_tile, bed_given, 0.0)
    cell_rows = jnp.where(in_tile, node_cells // breadth, -1)
    cell_cols = jnp.where(in_tile, node_cells % breadth, 0)
    top_diag, top_rhs = river_terms(
        cell_rows.reshape(1, -1),
        cell_cols.reshape(1, -1),
        bed_terms.reshape(1, -1),
        (bed_terms * slot_section).reshape(1, -1),
        across,
        breadth,
    )
    river = with_ghost(jnp.stack([top_diag, top_rhs]), "tile", 1, GHOST)
    tables = jnp.stack([ks_table, alpha_table, store_table])
    head = stencil(tables, fields, planes[2 * own_layers], river, tile_count * across)
    kept = lax.dynamic_slice_in_dim(head[:, GHOST : GHOST + across], layer * own_layers, own_layers, 0)

    top_head = head[0, GHOST : GHOST + across]
    my_cells = lax.dynamic_slice_in_dim(node_cells, node_first, quarter, 1)
    my_bed = lax.dynamic_slice_in_dim(bed_given, node_first, quarter, 1)
    my_section = lax.dynamic_slice_in_dim(slot_section, node_first, quarter, 1)
    my_inside = my_cells >= 0
    picked = node_heads(
        top_head,
        jnp.where(my_inside, my_cells // breadth, -1).reshape(1, -1),
        jnp.where(my_inside, my_cells % breadth, 0).reshape(1, -1),
    ).reshape(slots, quarter)
    slot_in = jnp.where(my_inside, my_bed * (picked - my_section), 0.0)
    sorted_in = jnp.take(slot_in, jnp.sum(jnp.where(at_place, order[None, :], 0), axis=1), axis=0)
    arrived = exchange(sorted_in.reshape(tile_count, per_owner, quarter), 2).reshape(slots, quarter)
    target = asked[None, :] == jnp.arange(reach_rows, dtype=jnp.int32)[:, None]
    inflow = jnp.sum(jnp.where(target[:, :, None], arrived[None], 0.0), axis=1)
    return (kept, inflow)


def solution(mesh):
    placed = (
        P("layer", "tile", None),
        P("layer", "tile", None),
        P("tile", None),
        P(),
        P(),
        P(),
        P("tile", None),
        P("tile", None),
        P("tile", None),
        P("tile", None, None),
        P("tile", None, None),
    )
    return jax.shard_map(
        on_device,
        mesh=mesh,
        in_specs=placed,
        out_specs=(P("layer", "tile", None), P("tile", "layer")),
        check_vma=False,
    )
```

```python
import functools

import jax
import jax.numpy as jnp
from jax import lax
from jax.experimental import pallas as pl
from jax.experimental.pallas import tpu as pltpu
from jax.sharding import PartitionSpec as P

ITERS = 2
SWEEPS = 3
GHOST = 8


LATERAL = 1.0
VERTICAL = 2.0
GRAVITY = 1.0
NEIGHBOURS = (
    (0, -1, VERTICAL),
    (0, 1, VERTICAL),
    (1, -1, LATERAL),
    (1, 1, LATERAL),
    (2, -1, LATERAL),
    (2, 1, LATERAL),
)
CHUNK = 512
INNER = 8


def beside(padded, axis_id, step):
    spans = [slice(1, -1), slice(1, -1), slice(1, -1)]
    spans[axis_id] = slice(1 + step, padded.shape[axis_id] - 1 + step)
    return padded[tuple(spans)]


def neighbor_weights(cond_pad, open_pad):
    centre = cond_pad[1:-1, 1:-1, 1:-1]
    centre_open = open_pad[1:-1, 1:-1, 1:-1]
    result = []
    for axis_id, step, factor in NEIGHBOURS:
        far = beside(cond_pad, axis_id, step)
        far_open = beside(open_pad, axis_id, step)
        result.append(factor * 2.0 * centre_open * far_open / (centre + far))
    return result


def relax(head_pad, weights, store, head_old, riv_diag, riv_rhs):
    total = store * head_old
    diagonal_sum = store
    for weight, (axis_id, step, factor) in zip(weights, NEIGHBOURS):
        total = total + weight * beside(head_pad, axis_id, step)
        diagonal_sum = diagonal_sum + weight
    total = total + GRAVITY * (weights[0] - weights[1]) + riv_rhs
    return total / (diagonal_sum + riv_diag)


def lookup(values_table, classes):
    result = jnp.zeros(classes.shape, jnp.float32)
    for class_id in range(values_table.shape[0]):
        result = jnp.where(classes == class_id, values_table[class_id], result)
    return result


def split3(value):
    high = value.astype(jnp.bfloat16).astype(jnp.float32)
    rest = value - high
    middle = rest.astype(jnp.bfloat16).astype(jnp.float32)
    low = rest - middle
    return high, middle, low


def scatter_kernel(rows_ref, cols_ref, diag_in_ref, rhs_in_ref, diag_ref, rhs_ref, acc_ref):
    step = pl.program_id(0)
    grid_rows, breadth = diag_ref.shape
    chunk = rows_ref.shape[1]

    @pl.when(step == 0)
    def _():
        acc_ref[...] = jnp.zeros_like(acc_ref)

    rows = rows_ref[...]

    @pl.when(jnp.max(rows) >= 0)
    def _():
        hit = lax.broadcasted_iota(jnp.int32, (grid_rows, chunk), 0) == rows
        pieces = []
        for value in (diag_in_ref[...], rhs_in_ref[...]):
            for piece in split3(value):
                pieces.append(jnp.where(hit, piece, 0.0).astype(jnp.bfloat16))
        left = jnp.concatenate(pieces, axis=0)
        cols = cols_ref[...]
        column_hit = lax.broadcasted_iota(jnp.int32, (breadth, chunk), 0) == cols
        right = jnp.where(column_hit, 1.0, 0.0).astype(jnp.bfloat16)
        acc_ref[...] += lax.dot_general(
            left, right, (((1,), (1,)), ((), ())), preferred_element_type=jnp.float32
        )

    @pl.when(step == pl.num_programs(0) - 1)
    def _():
        acc = acc_ref[...]
        g = grid_rows
        diag_ref[...] = acc[0:g] + acc[g : 2 * g] + acc[2 * g : 3 * g]
        rhs_ref[...] = acc[3 * g : 4 * g] + acc[4 * g : 5 * g] + acc[5 * g : 6 * g]


def river_terms(rows, cols, diag_values, rhs_values, grid_rows, breadth):
    count = rows.shape[1]
    lane = pl.BlockSpec((1, CHUNK), lambda i: (0, i))
    whole = pl.BlockSpec((grid_rows, breadth), lambda i: (0, 0))
    return pl.pallas_call(
        scatter_kernel,
        grid=(count // CHUNK,),
        in_specs=[lane, lane, lane, lane],
        out_specs=[whole, whole],
        out_shape=[
            jax.ShapeDtypeStruct((grid_rows, breadth), jnp.float32),
            jax.ShapeDtypeStruct((grid_rows, breadth), jnp.float32),
        ],
        scratch_shapes=[pltpu.VMEM((6 * grid_rows, breadth), jnp.float32)],
        cost_estimate=pl.CostEstimate(
            flops=2 * 6 * grid_rows * breadth * count,
            transcendentals=0,
            bytes_accessed=16 * count + 8 * grid_rows * breadth,
        ),
    )(rows, cols, diag_values, rhs_values)


def gather_kernel(top_ref, rows_ref, cols_ref, out_ref):
    grid_rows, breadth = top_ref.shape
    chunk = rows_ref.shape[1]
    stacked = jnp.concatenate(
        [piece.astype(jnp.bfloat16) for piece in split3(top_ref[...])], axis=0
    )
    cols = cols_ref[...]
    column_hit = lax.broadcasted_iota(jnp.int32, (breadth, chunk), 0) == cols
    right = jnp.where(column_hit, 1.0, 0.0).astype(jnp.bfloat16)
    picked = jnp.dot(stacked, right, preferred_element_type=jnp.float32)
    g = grid_rows
    by_row = picked[0:g] + picked[g : 2 * g] + picked[2 * g : 3 * g]
    rows = rows_ref[...]
    hit = lax.broadcasted_iota(jnp.int32, (grid_rows, chunk), 0) == rows
    out_ref[...] = jnp.sum(jnp.where(hit, by_row, 0.0), axis=0, keepdims=True)


def node_heads(top, rows, cols):
    grid_rows, breadth = top.shape
    count = rows.shape[1]
    lane = pl.BlockSpec((1, CHUNK), lambda i: (0, i))
    return pl.pallas_call(
        gather_kernel,
        grid=(count // CHUNK,),
        in_specs=[pl.BlockSpec((grid_rows, breadth), lambda i: (0, 0)), lane, lane],
        out_specs=lane,
        out_shape=jax.ShapeDtypeStruct((1, count), jnp.float32),
        cost_estimate=pl.CostEstimate(
            flops=2 * 3 * grid_rows * breadth * count,
            transcendentals=0,
            bytes_accessed=12 * count + 4 * grid_rows * breadth,
        ),
    )(top, rows, cols)


def stencil_kernel(total_rows, tables_ref, fields_ref, land_ref, river_ref, out_ref,
                   ks_s, alpha_s, store_s, old_s, cond_s, open_s, w_s, heads_s):
    layers, rows, breadth = out_ref.shape
    classes_n = tables_ref.shape[1]
    tile = lax.axis_index("tile")
    row_id = lax.broadcasted_iota(jnp.int32, (rows, breadth), 0)
    col_id = lax.broadcasted_iota(jnp.int32, (rows, breadth), 1)
    grow = tile * (rows - 2 * GHOST) - GHOST + row_id
    inside = (grow >= 0) & (grow < total_rows)
    land = jnp.where(inside, land_ref[...], 0.0)
    moves = []
    for axis, size, ident in ((0, rows, row_id), (1, breadth, col_id)):
        for shift in (1, size - 1):
            adjacent = jnp.abs(pltpu.roll(ident, shift, axis) - ident) == 1
            moves.append((axis, shift, adjacent))

    def shifted(x):
        return [jnp.where(adjacent, pltpu.roll(x, shift, axis), 0.0) for axis, shift, adjacent in moves]

    def init(z, carry):
        classes = fields_ref[1, z].astype(jnp.int32)
        looked = [jnp.zeros((rows, breadth), jnp.float32) for _ in range(3)]
        for class_id in range(classes_n):
            hit = classes == class_id
            looked = [jnp.where(hit, tables_ref[t, class_id], looked[t]) for t in range(3)]
        ks_s[z] = jnp.where(inside, looked[0], 1.0)
        alpha_s[z] = jnp.where(inside, looked[1], 0.0)
        store_s[z] = jnp.where(inside, looked[2], 1.0)
        old_s[z] = jnp.where(inside, fields_ref[0, z], 0.0)
        return carry

    lax.fori_loop(0, layers, init, 0)
    source = old_s
    count = 0
    for picard in range(ITERS):

        def conduct(z, carry, source=source):
            k = ks_s[z] * jnp.exp(alpha_s[z] * jnp.minimum(source[z], 0.0))
            cond_s[z] = k
            open_s[z] = k * land
            return carry

        lax.fori_loop(0, layers, conduct, 0)

        def weigh(z, carry):
            c = cond_s[z]
            co = open_s[z]
            above = jnp.maximum(z - 1, 0)
            below = jnp.minimum(z + 1, layers - 1)
            far = [jnp.where(z > 0, cond_s[above], 0.0), jnp.where(z < layers - 1, cond_s[below], 0.0)]
            far_open = [jnp.where(z > 0, open_s[above], 0.0), jnp.where(z < layers - 1, open_s[below], 0.0)]
            far += shifted(c)
            far_open += shifted(co)
            for i, (_, _, factor) in enumerate(NEIGHBOURS):
                w_s[i, z] = factor * 2.0 * co * far_open[i] / (c + far[i])
            return carry

        lax.fori_loop(0, layers, weigh, 0)
        for sweep in range(SWEEPS):
            last = picard == ITERS - 1 and sweep == SWEEPS - 1
            target = out_ref if last else heads_s.at[count % 2]
            count += 1

            def relax_layer(z, carry, source=source, target=target):
                h = source[z]
                above = jnp.maximum(z - 1, 0)
                below = jnp.minimum(z + 1, layers - 1)
                near = [jnp.where(z > 0, source[above], 0.0), jnp.where(z < layers - 1, source[below], 0.0)]
                near += shifted(h)
                st = store_s[z]
                total = st * old_s[z]
                diagonal_sum = st
                for i in range(len(NEIGHBOURS)):
                    w = w_s[i, z]
                    total = total + w * near[i]
                    diagonal_sum = diagonal_sum + w
                top = z == 0
                total = total + GRAVITY * (w_s[0, z] - w_s[1, z]) + jnp.where(top, river_ref[1], 0.0)
                target[z] = total / (diagonal_sum + jnp.where(top, river_ref[0], 0.0))
                return carry

            lax.fori_loop(0, layers, relax_layer, 0)
            source = target


def stencil(tables, fields, land, river, total_rows):
    _, layers, rows, breadth = fields.shape
    vmem = pl.BlockSpec(memory_space=pltpu.VMEM)
    field = pltpu.VMEM((layers, rows, breadth), jnp.float32)
    cells = layers * rows * breadth
    return pl.pallas_call(
        functools.partial(stencil_kernel, total_rows),
        in_specs=[pl.BlockSpec(memory_space=pltpu.SMEM), vmem, vmem, vmem],
        out_specs=vmem,
        out_shape=jax.ShapeDtypeStruct((layers, rows, breadth), jnp.float32),
        scratch_shapes=[field] * 6
        + [pltpu.VMEM((6, layers, rows, breadth), jnp.float32), pltpu.VMEM((2, layers, rows, breadth), jnp.float32)],
        compiler_params=pltpu.CompilerParams(vmem_limit_bytes=48 * 1024 * 1024),
        cost_estimate=pl.CostEstimate(flops=400 * cells, transcendentals=2 * cells, bytes_accessed=12 * cells),
    )(tables, fields, land, river)


def exchange_kernel(x_ref, y_ref, first, second, send_a, recv_a, send_b, recv_b, local_sem):
    outer, inner = x_ref.shape[0], x_ref.shape[1]
    me = lax.axis_index("tile")
    layer = lax.axis_index("layer")
    high = me // inner
    low = lax.rem(me, inner)
    mesh_ids = pl.DeviceIdType.MESH
    barrier = pltpu.get_barrier_semaphore()

    def greet_inner(i, carry):
        peer = high * inner + lax.rem(low + i, inner)
        pl.semaphore_signal(barrier, inc=1, device_id=(peer, layer), device_id_type=mesh_ids)
        return carry

    def greet_outer(i, carry):
        peer = lax.rem(high + i, outer) * inner + low
        pl.semaphore_signal(barrier, inc=1, device_id=(peer, layer), device_id_type=mesh_ids)
        return carry

    lax.fori_loop(1, inner, greet_inner, 0)
    lax.fori_loop(1, outer, greet_outer, 0)
    pl.semaphore_wait(barrier, inner + outer - 2)

    def copy_a(target, source):
        return pltpu.make_async_remote_copy(
            src_ref=x_ref.at[:, target],
            dst_ref=first.at[source],
            send_sem=send_a.at[target],
            recv_sem=recv_a.at[source],
            device_id=(high * inner + target, layer),
            device_id_type=mesh_ids,
        )

    def send_first(i, carry):
        copy_a(lax.rem(low + i, inner), low).start()
        return carry

    lax.fori_loop(1, inner, send_first, 0)
    own = pltpu.make_async_copy(x_ref.at[:, low], first.at[low], local_sem.at[0])
    own.start()
    own.wait()

    def finish_first(i, carry):
        copy_a(lax.rem(low + i, inner), low).wait_send()
        copy_a(lax.rem(low + inner - i, inner), lax.rem(low + inner - i, inner)).wait_recv()
        return carry

    lax.fori_loop(1, inner, finish_first, 0)

    def copy_b(target, source):
        return pltpu.make_async_remote_copy(
            src_ref=first.at[:, target],
            dst_ref=second.at[source],
            send_sem=send_b.at[target],
            recv_sem=recv_b.at[source],
            device_id=(target * inner + low, layer),
            device_id_type=mesh_ids,
        )

    def send_second(i, carry):
        copy_b(lax.rem(high + i, outer), high).start()
        return carry

    lax.fori_loop(1, outer, send_second, 0)
    own = pltpu.make_async_copy(first.at[:, high], second.at[high], local_sem.at[1])
    own.start()
    own.wait()

    def finish_second(i, carry):
        copy_b(lax.rem(high + i, outer), high).wait_send()
        copy_b(lax.rem(high + outer - i, outer), lax.rem(high + outer - i, outer)).wait_recv()
        return carry

    lax.fori_loop(1, outer, finish_second, 0)
    y_ref[...] = second[...]


def exchange(x, collective):
    tiles = x.shape[0]
    inner = INNER if tiles % INNER == 0 else 1
    outer = tiles // inner
    block = x.shape[1:]
    vmem = pl.BlockSpec(memory_space=pltpu.VMEM)
    y = pl.pallas_call(
        exchange_kernel,
        in_specs=[vmem],
        out_specs=vmem,
        out_shape=jax.ShapeDtypeStruct((outer, inner) + block, x.dtype),
        scratch_shapes=[
            pltpu.VMEM((inner, outer) + block, x.dtype),
            pltpu.VMEM((outer, inner) + block, x.dtype),
            pltpu.SemaphoreType.DMA((inner,)),
            pltpu.SemaphoreType.DMA((inner,)),
            pltpu.SemaphoreType.DMA((outer,)),
            pltpu.SemaphoreType.DMA((outer,)),
            pltpu.SemaphoreType.DMA((2,)),
        ],
        compiler_params=pltpu.CompilerParams(collective_id=collective, has_side_effects=True),
    )(x.reshape((outer, inner) + block))
    return y.reshape(x.shape)


def with_ghost(block, axis, dim, width):
    count = lax.axis_size(axis)
    forward = [(i, i + 1) for i in range(count - 1)]
    backward = [(i + 1, i) for i in range(count - 1)]
    size = block.shape[dim]
    above = lax.ppermute(lax.slice_in_dim(block, size - width, size, axis=dim), axis, forward)
    below = lax.ppermute(lax.slice_in_dim(block, 0, width, axis=dim), axis, backward)
    return jnp.concatenate([above, block, below], axis=dim)


def on_device(
    head_start,
    soil_class,
    land_mask,
    ks_table,
    alpha_table,
    store_table,
    section,
    cross_owner,
    cross_local,
    node_cell,
    bed_cond,
):
    own_layers, across, breadth = head_start.shape
    reach_rows, node_count = section.shape
    tile_count = lax.axis_size("tile")
    layer_count = lax.axis_size("layer")
    tile = lax.axis_index("tile")
    layer = lax.axis_index("layer")
    quarter = node_count // layer_count
    node_first = layer * quarter

    planes = jnp.concatenate(
        [head_start, soil_class.astype(jnp.float32), land_mask.astype(jnp.float32)[None]], axis=0
    )
    planes = with_ghost(planes, "tile", 1, GHOST)
    extent = across + 2 * GHOST
    fields = planes[: 2 * own_layers].reshape(2, own_layers, extent, breadth)
    fields = lax.all_gather(fields, "layer", axis=1, tiled=True)
    owners = cross_owner[0]
    positions = cross_local[0]
    node_cells = node_cell[0]
    bed_given = bed_cond[0]
    slots = owners.shape[0]
    per_owner = slots // tile_count
    order = jnp.arange(slots, dtype=jnp.int32)
    same = owners[:, None] == owners[None, :]
    rank = jnp.sum((same & (order[None, :] < order[:, None])).astype(jnp.int32), axis=1)
    place = owners * per_owner + rank
    at_place = place[None, :] == order[:, None]
    wanted = jnp.sum(jnp.where(at_place, positions[None, :], 0), axis=1)
    asked = exchange(wanted.reshape(tile_count, per_owner, 1), 0).reshape(slots)
    reply = jnp.take(section, asked, axis=0)
    sorted_section = exchange(reply.reshape(tile_count, per_owner, node_count), 1).reshape(slots, node_count)
    slot_section = jnp.take(sorted_section, place, axis=0)

    in_tile = node_cells >= 0
    bed_terms = jnp.where(in_tile, bed_given, 0.0)
    cell_rows = jnp.where(in_tile, node_cells // breadth, -1)
    cell_cols = jnp.where(in_tile, node_cells % breadth, 0)
    top_diag, top_rhs = river_terms(
        cell_rows.reshape(1, -1),
        cell_cols.reshape(1, -1),
        bed_terms.reshape(1, -1),
        (bed_terms * slot_section).reshape(1, -1),
        across,
        breadth,
    )
    river = with_ghost(jnp.stack([top_diag, top_rhs]), "tile", 1, GHOST)
    tables = jnp.stack([ks_table, alpha_table, store_table])
    head = stencil(tables, fields, planes[2 * own_layers], river, tile_count * across)
    kept = lax.dynamic_slice_in_dim(head[:, GHOST : GHOST + across], layer * own_layers, own_layers, 0)

    top_head = head[0, GHOST : GHOST + across]
    my_cells = lax.dynamic_slice_in_dim(node_cells, node_first, quarter, 1)
    my_bed = lax.dynamic_slice_in_dim(bed_given, node_first, quarter, 1)
    my_section = lax.dynamic_slice_in_dim(slot_section, node_first, quarter, 1)
    my_inside = my_cells >= 0
    picked = node_heads(
        top_head,
        jnp.where(my_inside, my_cells // breadth, -1).reshape(1, -1),
        jnp.where(my_inside, my_cells % breadth, 0).reshape(1, -1),
    ).reshape(slots, quarter)
    slot_in = jnp.where(my_inside, my_bed * (picked - my_section), 0.0)
    sorted_in = jnp.take(slot_in, jnp.sum(jnp.where(at_place, order[None, :], 0), axis=1), axis=0)
    arrived = exchange(sorted_in.reshape(tile_count, per_owner, quarter), 2).reshape(slots, quarter)
    target = asked[None, :] == jnp.arange(reach_rows, dtype=jnp.int32)[:, None]
    inflow = jnp.sum(jnp.where(target[:, :, None], arrived[None], 0.0), axis=1)
    return (kept, inflow)


def solution(mesh):
    placed = (
        P("layer", "tile", None),
        P("layer", "tile", None),
        P("tile", None),
        P(),
        P(),
        P(),
        P("tile", None),
        P("tile", None),
        P("tile", None),
        P("tile", None, None),
        P("tile", None, None),
    )
    return jax.shard_map(
        on_device,
        mesh=mesh,
        in_specs=placed,
        out_specs=(P("layer", "tile", None), P("tile", "layer")),
        check_vma=False,
    )
```

```python
import functools

import jax
import jax.numpy as jnp
from jax import lax
from jax.experimental import pallas as pl
from jax.experimental.pallas import tpu as pltpu
from jax.sharding import PartitionSpec as P

ITERS = 2
SWEEPS = 3
GHOST = 8


LATERAL = 1.0
VERTICAL = 2.0
GRAVITY = 1.0
NEIGHBOURS = (
    (0, -1, VERTICAL),
    (0, 1, VERTICAL),
    (1, -1, LATERAL),
    (1, 1, LATERAL),
    (2, -1, LATERAL),
    (2, 1, LATERAL),
)
CHUNK = 512
INNER = 8


def beside(padded, axis_id, step):
    spans = [slice(1, -1), slice(1, -1), slice(1, -1)]
    spans[axis_id] = slice(1 + step, padded.shape[axis_id] - 1 + step)
    return padded[tuple(spans)]


def neighbor_weights(cond_pad, open_pad):
    centre = cond_pad[1:-1, 1:-1, 1:-1]
    centre_open = open_pad[1:-1, 1:-1, 1:-1]
    result = []
    for axis_id, step, factor in NEIGHBOURS:
        far = beside(cond_pad, axis_id, step)
        far_open = beside(open_pad, axis_id, step)
        result.append(factor * 2.0 * centre_open * far_open / (centre + far))
    return result


def relax(head_pad, weights, store, head_old, riv_diag, riv_rhs):
    total = store * head_old
    diagonal_sum = store
    for weight, (axis_id, step, factor) in zip(weights, NEIGHBOURS):
        total = total + weight * beside(head_pad, axis_id, step)
        diagonal_sum = diagonal_sum + weight
    total = total + GRAVITY * (weights[0] - weights[1]) + riv_rhs
    return total / (diagonal_sum + riv_diag)


def lookup(values_table, classes):
    result = jnp.zeros(classes.shape, jnp.float32)
    for class_id in range(values_table.shape[0]):
        result = jnp.where(classes == class_id, values_table[class_id], result)
    return result


def split3(value):
    high = value.astype(jnp.bfloat16).astype(jnp.float32)
    rest = value - high
    middle = rest.astype(jnp.bfloat16).astype(jnp.float32)
    low = rest - middle
    return high, middle, low


def scatter_kernel(rows_ref, cols_ref, diag_in_ref, rhs_in_ref, diag_ref, rhs_ref, acc_ref):
    step = pl.program_id(0)
    grid_rows, breadth = diag_ref.shape
    chunk = rows_ref.shape[1]

    @pl.when(step == 0)
    def _():
        acc_ref[...] = jnp.zeros_like(acc_ref)

    rows = rows_ref[...]

    @pl.when(jnp.max(rows) >= 0)
    def _():
        hit = lax.broadcasted_iota(jnp.int32, (grid_rows, chunk), 0) == rows
        pieces = []
        for value in (diag_in_ref[...], rhs_in_ref[...]):
            for piece in split3(value):
                pieces.append(jnp.where(hit, piece, 0.0).astype(jnp.bfloat16))
        left = jnp.concatenate(pieces, axis=0)
        cols = cols_ref[...]
        column_hit = lax.broadcasted_iota(jnp.int32, (breadth, chunk), 0) == cols
        right = jnp.where(column_hit, 1.0, 0.0).astype(jnp.bfloat16)
        acc_ref[...] += lax.dot_general(
            left, right, (((1,), (1,)), ((), ())), preferred_element_type=jnp.float32
        )

    @pl.when(step == pl.num_programs(0) - 1)
    def _():
        acc = acc_ref[...]
        g = grid_rows
        diag_ref[...] = acc[0:g] + acc[g : 2 * g] + acc[2 * g : 3 * g]
        rhs_ref[...] = acc[3 * g : 4 * g] + acc[4 * g : 5 * g] + acc[5 * g : 6 * g]


def river_terms(rows, cols, diag_values, rhs_values, grid_rows, breadth):
    count = rows.shape[1]
    lane = pl.BlockSpec((1, CHUNK), lambda i: (0, i))
    whole = pl.BlockSpec((grid_rows, breadth), lambda i: (0, 0))
    return pl.pallas_call(
        scatter_kernel,
        grid=(count // CHUNK,),
        in_specs=[lane, lane, lane, lane],
        out_specs=[whole, whole],
        out_shape=[
            jax.ShapeDtypeStruct((grid_rows, breadth), jnp.float32),
            jax.ShapeDtypeStruct((grid_rows, breadth), jnp.float32),
        ],
        scratch_shapes=[pltpu.VMEM((6 * grid_rows, breadth), jnp.float32)],
        cost_estimate=pl.CostEstimate(
            flops=2 * 6 * grid_rows * breadth * count,
            transcendentals=0,
            bytes_accessed=16 * count + 8 * grid_rows * breadth,
        ),
    )(rows, cols, diag_values, rhs_values)


def gather_kernel(top_ref, rows_ref, cols_ref, out_ref):
    grid_rows, breadth = top_ref.shape
    chunk = rows_ref.shape[1]
    stacked = jnp.concatenate(
        [piece.astype(jnp.bfloat16) for piece in split3(top_ref[...])], axis=0
    )
    cols = cols_ref[...]
    column_hit = lax.broadcasted_iota(jnp.int32, (breadth, chunk), 0) == cols
    right = jnp.where(column_hit, 1.0, 0.0).astype(jnp.bfloat16)
    picked = jnp.dot(stacked, right, preferred_element_type=jnp.float32)
    g = grid_rows
    by_row = picked[0:g] + picked[g : 2 * g] + picked[2 * g : 3 * g]
    rows = rows_ref[...]
    hit = lax.broadcasted_iota(jnp.int32, (grid_rows, chunk), 0) == rows
    out_ref[...] = jnp.sum(jnp.where(hit, by_row, 0.0), axis=0, keepdims=True)


def node_heads(top, rows, cols):
    grid_rows, breadth = top.shape
    count = rows.shape[1]
    lane = pl.BlockSpec((1, CHUNK), lambda i: (0, i))
    return pl.pallas_call(
        gather_kernel,
        grid=(count // CHUNK,),
        in_specs=[pl.BlockSpec((grid_rows, breadth), lambda i: (0, 0)), lane, lane],
        out_specs=lane,
        out_shape=jax.ShapeDtypeStruct((1, count), jnp.float32),
        cost_estimate=pl.CostEstimate(
            flops=2 * 3 * grid_rows * breadth * count,
            transcendentals=0,
            bytes_accessed=12 * count + 4 * grid_rows * breadth,
        ),
    )(top, rows, cols)


def stencil_kernel(total_rows, tables_ref, fields_ref, land_ref, river_ref, out_ref,
                   ks_s, alpha_s, store_s, old_s, cond_s, open_s, w_s, heads_s):
    layers, rows, breadth = out_ref.shape
    classes_n = tables_ref.shape[1]
    tile = lax.axis_index("tile")
    row_id = lax.broadcasted_iota(jnp.int32, (rows, breadth), 0)
    col_id = lax.broadcasted_iota(jnp.int32, (rows, breadth), 1)
    grow = tile * (rows - 2 * GHOST) - GHOST + row_id
    inside = (grow >= 0) & (grow < total_rows)
    land = jnp.where(inside, land_ref[...], 0.0)
    moves = []
    for axis, size, ident in ((0, rows, row_id), (1, breadth, col_id)):
        for shift in (1, size - 1):
            adjacent = jnp.abs(pltpu.roll(ident, shift, axis) - ident) == 1
            moves.append((axis, shift, adjacent))

    def shifted(x):
        return [jnp.where(adjacent, pltpu.roll(x, shift, axis), 0.0) for axis, shift, adjacent in moves]

    def init(z, carry):
        classes = fields_ref[1, z].astype(jnp.int32)
        looked = [jnp.zeros((rows, breadth), jnp.float32) for _ in range(3)]
        for class_id in range(classes_n):
            hit = classes == class_id
            looked = [jnp.where(hit, tables_ref[t, class_id], looked[t]) for t in range(3)]
        ks_s[z] = jnp.where(inside, looked[0], 1.0)
        alpha_s[z] = jnp.where(inside, looked[1], 0.0)
        store_s[z] = jnp.where(inside, looked[2], 1.0)
        old_s[z] = jnp.where(inside, fields_ref[0, z], 0.0)
        return carry

    lax.fori_loop(0, layers, init, 0)
    source = old_s
    count = 0
    for picard in range(ITERS):

        def conduct(z, carry, source=source):
            k = ks_s[z] * jnp.exp(alpha_s[z] * jnp.minimum(source[z], 0.0))
            cond_s[z] = k
            open_s[z] = k * land
            return carry

        lax.fori_loop(0, layers, conduct, 0)

        def weigh(z, carry):
            c = cond_s[z]
            co = open_s[z]
            above = jnp.maximum(z - 1, 0)
            below = jnp.minimum(z + 1, layers - 1)
            far = [jnp.where(z > 0, cond_s[above], 0.0), jnp.where(z < layers - 1, cond_s[below], 0.0)]
            far_open = [jnp.where(z > 0, open_s[above], 0.0), jnp.where(z < layers - 1, open_s[below], 0.0)]
            far += shifted(c)
            far_open += shifted(co)
            for i, (_, _, factor) in enumerate(NEIGHBOURS):
                w_s[i, z] = factor * 2.0 * co * far_open[i] / (c + far[i])
            return carry

        lax.fori_loop(0, layers, weigh, 0)
        for sweep in range(SWEEPS):
            last = picard == ITERS - 1 and sweep == SWEEPS - 1
            target = out_ref if last else heads_s.at[count % 2]
            count += 1

            def relax_layer(z, carry, source=source, target=target):
                h = source[z]
                above = jnp.maximum(z - 1, 0)
                below = jnp.minimum(z + 1, layers - 1)
                near = [jnp.where(z > 0, source[above], 0.0), jnp.where(z < layers - 1, source[below], 0.0)]
                near += shifted(h)
                st = store_s[z]
                total = st * old_s[z]
                diagonal_sum = st
                for i in range(len(NEIGHBOURS)):
                    w = w_s[i, z]
                    total = total + w * near[i]
                    diagonal_sum = diagonal_sum + w
                top = z == 0
                total = total + GRAVITY * (w_s[0, z] - w_s[1, z]) + jnp.where(top, river_ref[1], 0.0)
                target[z] = total / (diagonal_sum + jnp.where(top, river_ref[0], 0.0))
                return carry

            lax.fori_loop(0, layers, relax_layer, 0)
            source = target


def stencil(tables, fields, land, river, total_rows):
    _, layers, rows, breadth = fields.shape
    vmem = pl.BlockSpec(memory_space=pltpu.VMEM)
    field = pltpu.VMEM((layers, rows, breadth), jnp.float32)
    cells = layers * rows * breadth
    return pl.pallas_call(
        functools.partial(stencil_kernel, total_rows),
        in_specs=[pl.BlockSpec(memory_space=pltpu.SMEM), vmem, vmem, vmem],
        out_specs=vmem,
        out_shape=jax.ShapeDtypeStruct((layers, rows, breadth), jnp.float32),
        scratch_shapes=[field] * 6
        + [pltpu.VMEM((6, layers, rows, breadth), jnp.float32), pltpu.VMEM((2, layers, rows, breadth), jnp.float32)],
        compiler_params=pltpu.CompilerParams(vmem_limit_bytes=48 * 1024 * 1024),
        cost_estimate=pl.CostEstimate(flops=400 * cells, transcendentals=2 * cells, bytes_accessed=12 * cells),
    )(tables, fields, land, river)


def exchange_kernel(x_ref, y_ref, first, second, send_a, recv_a, send_b, recv_b, local_sem):
    outer, inner = x_ref.shape[0], x_ref.shape[1]
    me = lax.axis_index("tile")
    layer = lax.axis_index("layer")
    high = me // inner
    low = lax.rem(me, inner)
    mesh_ids = pl.DeviceIdType.MESH
    barrier = pltpu.get_barrier_semaphore()

    def greet_inner(i, carry):
        peer = high * inner + lax.rem(low + i, inner)
        pl.semaphore_signal(barrier, inc=1, device_id=(peer, layer), device_id_type=mesh_ids)
        return carry

    def greet_outer(i, carry):
        peer = lax.rem(high + i, outer) * inner + low
        pl.semaphore_signal(barrier, inc=1, device_id=(peer, layer), device_id_type=mesh_ids)
        return carry

    lax.fori_loop(1, inner, greet_inner, 0)
    lax.fori_loop(1, outer, greet_outer, 0)
    pl.semaphore_wait(barrier, inner + outer - 2)

    def copy_a(target, source):
        return pltpu.make_async_remote_copy(
            src_ref=x_ref.at[:, target],
            dst_ref=first.at[source],
            send_sem=send_a.at[target],
            recv_sem=recv_a.at[source],
            device_id=(high * inner + target, layer),
            device_id_type=mesh_ids,
        )

    def send_first(i, carry):
        copy_a(lax.rem(low + i, inner), low).start()
        return carry

    lax.fori_loop(1, inner, send_first, 0)
    own = pltpu.make_async_copy(x_ref.at[:, low], first.at[low], local_sem.at[0])
    own.start()
    own.wait()

    def finish_first(i, carry):
        copy_a(lax.rem(low + i, inner), low).wait_send()
        copy_a(lax.rem(low + inner - i, inner), lax.rem(low + inner - i, inner)).wait_recv()
        return carry

    lax.fori_loop(1, inner, finish_first, 0)

    def copy_b(target, source):
        return pltpu.make_async_remote_copy(
            src_ref=first.at[:, target],
            dst_ref=second.at[source],
            send_sem=send_b.at[target],
            recv_sem=recv_b.at[source],
            device_id=(target * inner + low, layer),
            device_id_type=mesh_ids,
        )

    def send_second(i, carry):
        copy_b(lax.rem(high + i, outer), high).start()
        return carry

    lax.fori_loop(1, outer, send_second, 0)
    own = pltpu.make_async_copy(first.at[:, high], second.at[high], local_sem.at[1])
    own.start()
    own.wait()

    def finish_second(i, carry):
        copy_b(lax.rem(high + i, outer), high).wait_send()
        copy_b(lax.rem(high + outer - i, outer), lax.rem(high + outer - i, outer)).wait_recv()
        return carry

    lax.fori_loop(1, outer, finish_second, 0)
    y_ref[...] = second[...]


def exchange(x, collective):
    tiles = x.shape[0]
    inner = INNER if tiles % INNER == 0 else 1
    outer = tiles // inner
    block = x.shape[1:]
    vmem = pl.BlockSpec(memory_space=pltpu.VMEM)
    y = pl.pallas_call(
        exchange_kernel,
        in_specs=[vmem],
        out_specs=vmem,
        out_shape=jax.ShapeDtypeStruct((outer, inner) + block, x.dtype),
        scratch_shapes=[
            pltpu.VMEM((inner, outer) + block, x.dtype),
            pltpu.VMEM((outer, inner) + block, x.dtype),
            pltpu.SemaphoreType.DMA((inner,)),
            pltpu.SemaphoreType.DMA((inner,)),
            pltpu.SemaphoreType.DMA((outer,)),
            pltpu.SemaphoreType.DMA((outer,)),
            pltpu.SemaphoreType.DMA((2,)),
        ],
        compiler_params=pltpu.CompilerParams(collective_id=collective, has_side_effects=True),
    )(x.reshape((outer, inner) + block))
    return y.reshape(x.shape)


def combine_kernel(x_ref, y_ref, landed, send_sem, recv_sem, local_sem):
    groups = landed.shape[0]
    me = lax.axis_index("layer")
    tile = lax.axis_index("tile")
    mesh_ids = pl.DeviceIdType.MESH
    barrier = pltpu.get_barrier_semaphore()
    for i in range(1, groups):
        pl.semaphore_signal(barrier, inc=1, device_id=(tile, lax.rem(me + i, groups)), device_id_type=mesh_ids)
    pl.semaphore_wait(barrier, groups - 1)

    def copy(target, source):
        return pltpu.make_async_remote_copy(
            src_ref=x_ref,
            dst_ref=landed.at[source],
            send_sem=send_sem.at[target],
            recv_sem=recv_sem.at[source],
            device_id=(tile, target),
            device_id_type=mesh_ids,
        )

    for i in range(1, groups):
        copy(lax.rem(me + i, groups), me).start()
    own = pltpu.make_async_copy(x_ref, landed.at[me], local_sem)
    own.start()
    own.wait()
    for i in range(1, groups):
        copy(lax.rem(me + i, groups), me).wait_send()
        source = lax.rem(me + groups - i, groups)
        copy(source, source).wait_recv()
    total = landed[0]
    for g in range(1, groups):
        total = total + landed[g]
    y_ref[...] = total


def combine(x, collective):
    groups = lax.axis_size("layer")
    vmem = pl.BlockSpec(memory_space=pltpu.VMEM)
    return pl.pallas_call(
        combine_kernel,
        in_specs=[vmem],
        out_specs=vmem,
        out_shape=jax.ShapeDtypeStruct(x.shape, x.dtype),
        scratch_shapes=[
            pltpu.VMEM((groups,) + x.shape, x.dtype),
            pltpu.SemaphoreType.DMA((groups,)),
            pltpu.SemaphoreType.DMA((groups,)),
            pltpu.SemaphoreType.DMA,
        ],
        compiler_params=pltpu.CompilerParams(collective_id=collective, has_side_effects=True),
    )(x)


def with_ghost(block, axis, dim, width):
    count = lax.axis_size(axis)
    forward = [(i, i + 1) for i in range(count - 1)]
    backward = [(i + 1, i) for i in range(count - 1)]
    size = block.shape[dim]
    above = lax.ppermute(lax.slice_in_dim(block, size - width, size, axis=dim), axis, forward)
    below = lax.ppermute(lax.slice_in_dim(block, 0, width, axis=dim), axis, backward)
    return jnp.concatenate([above, block, below], axis=dim)


def on_device(
    head_start,
    soil_class,
    land_mask,
    ks_table,
    alpha_table,
    store_table,
    section,
    cross_owner,
    cross_local,
    node_cell,
    bed_cond,
):
    own_layers, across, breadth = head_start.shape
    reach_rows, node_count = section.shape
    tile_count = lax.axis_size("tile")
    layer_count = lax.axis_size("layer")
    tile = lax.axis_index("tile")
    layer = lax.axis_index("layer")
    quarter = node_count // layer_count
    node_first = layer * quarter

    planes = jnp.concatenate(
        [head_start, soil_class.astype(jnp.float32), land_mask.astype(jnp.float32)[None]], axis=0
    )
    planes = with_ghost(planes, "tile", 1, GHOST)
    extent = across + 2 * GHOST
    fields = planes[: 2 * own_layers].reshape(2, own_layers, extent, breadth)
    fields = lax.all_gather(fields, "layer", axis=1, tiled=True)
    owners = cross_owner[0]
    positions = cross_local[0]
    node_cells = node_cell[0]
    bed_given = bed_cond[0]
    slots = owners.shape[0]
    per_owner = slots // tile_count
    order = jnp.arange(slots, dtype=jnp.int32)
    same = owners[:, None] == owners[None, :]
    rank = jnp.sum((same & (order[None, :] < order[:, None])).astype(jnp.int32), axis=1)
    place = owners * per_owner + rank
    at_place = place[None, :] == order[:, None]
    wanted = jnp.sum(jnp.where(at_place, positions[None, :], 0), axis=1)
    asked = exchange(wanted.reshape(tile_count, per_owner, 1), 0).reshape(slots)
    reply = jnp.take(section, asked, axis=0)
    sorted_section = exchange(reply.reshape(tile_count, per_owner, node_count), 1).reshape(slots, node_count)
    slot_section = jnp.take(sorted_section, place, axis=0)

    share = slots // layer_count
    share_cells = lax.dynamic_slice_in_dim(node_cells, layer * share, share, 0)
    share_bed = lax.dynamic_slice_in_dim(bed_given, layer * share, share, 0)
    share_section = lax.dynamic_slice_in_dim(slot_section, layer * share, share, 0)
    in_tile = share_cells >= 0
    bed_terms = jnp.where(in_tile, share_bed, 0.0)
    cell_rows = jnp.where(in_tile, share_cells // breadth, -1)
    cell_cols = jnp.where(in_tile, share_cells % breadth, 0)
    top_diag, top_rhs = river_terms(
        cell_rows.reshape(1, -1),
        cell_cols.reshape(1, -1),
        bed_terms.reshape(1, -1),
        (bed_terms * share_section).reshape(1, -1),
        across,
        breadth,
    )
    river = combine(jnp.stack([top_diag, top_rhs]), 3)
    river = with_ghost(river, "tile", 1, GHOST)
    tables = jnp.stack([ks_table, alpha_table, store_table])
    head = stencil(tables, fields, planes[2 * own_layers], river, tile_count * across)
    kept = lax.dynamic_slice_in_dim(head[:, GHOST : GHOST + across], layer * own_layers, own_layers, 0)

    top_head = head[0, GHOST : GHOST + across]
    my_cells = lax.dynamic_slice_in_dim(node_cells, node_first, quarter, 1)
    my_bed = lax.dynamic_slice_in_dim(bed_given, node_first, quarter, 1)
    my_section = lax.dynamic_slice_in_dim(slot_section, node_first, quarter, 1)
    my_inside = my_cells >= 0
    picked = node_heads(
        top_head,
        jnp.where(my_inside, my_cells // breadth, -1).reshape(1, -1),
        jnp.where(my_inside, my_cells % breadth, 0).reshape(1, -1),
    ).reshape(slots, quarter)
    slot_in = jnp.where(my_inside, my_bed * (picked - my_section), 0.0)
    sorted_in = jnp.take(slot_in, jnp.sum(jnp.where(at_place, order[None, :], 0), axis=1), axis=0)
    arrived = exchange(sorted_in.reshape(tile_count, per_owner, quarter), 2).reshape(slots, quarter)
    target = asked[None, :] == jnp.arange(reach_rows, dtype=jnp.int32)[:, None]
    inflow = jnp.sum(jnp.where(target[:, :, None], arrived[None], 0.0), axis=1)
    return (kept, inflow)


def solution(mesh):
    placed = (
        P("layer", "tile", None),
        P("layer", "tile", None),
        P("tile", None),
        P(),
        P(),
        P(),
        P("tile", None),
        P("tile", None),
        P("tile", None),
        P("tile", None, None),
        P("tile", None, None),
    )
    return jax.shard_map(
        on_device,
        mesh=mesh,
        in_specs=placed,
        out_specs=(P("layer", "tile", None), P("tile", "layer")),
        check_vma=False,
    )
```

```python
import functools

import jax
import jax.numpy as jnp
from jax import lax
from jax.experimental import pallas as pl
from jax.experimental.pallas import tpu as pltpu
from jax.sharding import PartitionSpec as P

ITERS = 2
SWEEPS = 3
GHOST = 8


LATERAL = 1.0
VERTICAL = 2.0
GRAVITY = 1.0
NEIGHBOURS = (
    (0, -1, VERTICAL),
    (0, 1, VERTICAL),
    (1, -1, LATERAL),
    (1, 1, LATERAL),
    (2, -1, LATERAL),
    (2, 1, LATERAL),
)
CHUNK = 512


def beside(padded, axis_id, step):
    spans = [slice(1, -1), slice(1, -1), slice(1, -1)]
    spans[axis_id] = slice(1 + step, padded.shape[axis_id] - 1 + step)
    return padded[tuple(spans)]


def neighbor_weights(cond_pad, open_pad):
    centre = cond_pad[1:-1, 1:-1, 1:-1]
    centre_open = open_pad[1:-1, 1:-1, 1:-1]
    result = []
    for axis_id, step, factor in NEIGHBOURS:
        far = beside(cond_pad, axis_id, step)
        far_open = beside(open_pad, axis_id, step)
        result.append(factor * 2.0 * centre_open * far_open / (centre + far))
    return result


def relax(head_pad, weights, store, head_old, riv_diag, riv_rhs):
    total = store * head_old
    diagonal_sum = store
    for weight, (axis_id, step, factor) in zip(weights, NEIGHBOURS):
        total = total + weight * beside(head_pad, axis_id, step)
        diagonal_sum = diagonal_sum + weight
    total = total + GRAVITY * (weights[0] - weights[1]) + riv_rhs
    return total / (diagonal_sum + riv_diag)


def lookup(values_table, classes):
    result = jnp.zeros(classes.shape, jnp.float32)
    for class_id in range(values_table.shape[0]):
        result = jnp.where(classes == class_id, values_table[class_id], result)
    return result


def split3(value):
    high = value.astype(jnp.bfloat16).astype(jnp.float32)
    rest = value - high
    middle = rest.astype(jnp.bfloat16).astype(jnp.float32)
    low = rest - middle
    return high, middle, low


def split2(value):
    high = value.astype(jnp.bfloat16).astype(jnp.float32)
    return high, value - high


def scatter_kernel(rows_ref, cols_ref, values_ref, out_ref, acc_ref):
    step = pl.program_id(0)
    grid_rows, breadth = out_ref.shape
    chunk = rows_ref.shape[1]

    @pl.when(step == 0)
    def _():
        acc_ref[...] = jnp.zeros_like(acc_ref)

    rows = rows_ref[...]

    @pl.when(jnp.max(rows) >= 0)
    def _():
        hit = lax.broadcasted_iota(jnp.int32, (grid_rows, chunk), 0) == rows
        left = jnp.concatenate(
            [jnp.where(hit, piece, 0.0).astype(jnp.bfloat16) for piece in split2(values_ref[...])], axis=0
        )
        cols = cols_ref[...]
        column_hit = lax.broadcasted_iota(jnp.int32, (breadth, chunk), 0) == cols
        right = jnp.where(column_hit, 1.0, 0.0).astype(jnp.bfloat16)
        acc_ref[...] += lax.dot_general(
            left, right, (((1,), (1,)), ((), ())), preferred_element_type=jnp.float32
        )

    @pl.when(step == pl.num_programs(0) - 1)
    def _():
        acc = acc_ref[...]
        out_ref[...] = acc[0:grid_rows] + acc[grid_rows : 2 * grid_rows]


def river_terms(rows, cols, values, grid_rows, breadth):
    count = rows.shape[1]
    lane = pl.BlockSpec((1, CHUNK), lambda i: (0, i))
    return pl.pallas_call(
        scatter_kernel,
        grid=(count // CHUNK,),
        in_specs=[lane, lane, lane],
        out_specs=pl.BlockSpec((grid_rows, breadth), lambda i: (0, 0)),
        out_shape=jax.ShapeDtypeStruct((grid_rows, breadth), jnp.float32),
        scratch_shapes=[pltpu.VMEM((2 * grid_rows, breadth), jnp.float32)],
        cost_estimate=pl.CostEstimate(
            flops=2 * 2 * grid_rows * breadth * count,
            transcendentals=0,
            bytes_accessed=12 * count + 4 * grid_rows * breadth,
        ),
    )(rows, cols, values)


def gather_kernel(top_ref, rows_ref, cols_ref, out_ref):
    grid_rows, breadth = top_ref.shape
    chunk = rows_ref.shape[1]
    stacked = jnp.concatenate(
        [piece.astype(jnp.bfloat16) for piece in split3(top_ref[...])], axis=0
    )
    cols = cols_ref[...]
    column_hit = lax.broadcasted_iota(jnp.int32, (breadth, chunk), 0) == cols
    right = jnp.where(column_hit, 1.0, 0.0).astype(jnp.bfloat16)
    picked = jnp.dot(stacked, right, preferred_element_type=jnp.float32)
    g = grid_rows
    by_row = picked[0:g] + picked[g : 2 * g] + picked[2 * g : 3 * g]
    rows = rows_ref[...]
    hit = lax.broadcasted_iota(jnp.int32, (grid_rows, chunk), 0) == rows
    out_ref[...] = jnp.sum(jnp.where(hit, by_row, 0.0), axis=0, keepdims=True)


def node_heads(top, rows, cols):
    grid_rows, breadth = top.shape
    count = rows.shape[1]
    lane = pl.BlockSpec((1, CHUNK), lambda i: (0, i))
    return pl.pallas_call(
        gather_kernel,
        grid=(count // CHUNK,),
        in_specs=[pl.BlockSpec((grid_rows, breadth), lambda i: (0, 0)), lane, lane],
        out_specs=lane,
        out_shape=jax.ShapeDtypeStruct((1, count), jnp.float32),
        cost_estimate=pl.CostEstimate(
            flops=2 * 3 * grid_rows * breadth * count,
            transcendentals=0,
            bytes_accessed=12 * count + 4 * grid_rows * breadth,
        ),
    )(top, rows, cols)


def stencil_kernel(total_rows, tables_ref, fields_ref, land_ref, river_ref, out_ref,
                   ks_s, alpha_s, store_s, old_s, cond_s, open_s, w_s, heads_s):
    layers, rows, breadth = out_ref.shape
    classes_n = tables_ref.shape[1]
    tile = lax.axis_index("tile")
    row_id = lax.broadcasted_iota(jnp.int32, (rows, breadth), 0)
    col_id = lax.broadcasted_iota(jnp.int32, (rows, breadth), 1)
    grow = tile * (rows - 2 * GHOST) - GHOST + row_id
    inside = (grow >= 0) & (grow < total_rows)
    land = jnp.where(inside, land_ref[...], 0.0)
    moves = []
    for axis, size, ident in ((0, rows, row_id), (1, breadth, col_id)):
        for shift in (1, size - 1):
            adjacent = jnp.abs(pltpu.roll(ident, shift, axis) - ident) == 1
            moves.append((axis, shift, adjacent))

    def shifted(x):
        return [jnp.where(adjacent, pltpu.roll(x, shift, axis), 0.0) for axis, shift, adjacent in moves]

    def init(z, carry):
        classes = fields_ref[1, z].astype(jnp.int32)
        looked = [jnp.zeros((rows, breadth), jnp.float32) for _ in range(3)]
        for class_id in range(classes_n):
            hit = classes == class_id
            looked = [jnp.where(hit, tables_ref[t, class_id], looked[t]) for t in range(3)]
        ks_s[z] = jnp.where(inside, looked[0], 1.0)
        alpha_s[z] = jnp.where(inside, looked[1], 0.0)
        store_s[z] = jnp.where(inside, looked[2], 1.0)
        old_s[z] = jnp.where(inside, fields_ref[0, z], 0.0)
        return carry

    lax.fori_loop(0, layers, init, 0)
    source = old_s
    count = 0
    for picard in range(ITERS):

        def conduct(z, carry, source=source):
            k = ks_s[z] * jnp.exp(alpha_s[z] * jnp.minimum(source[z], 0.0))
            cond_s[z] = k
            open_s[z] = k * land
            return carry

        lax.fori_loop(0, layers, conduct, 0)

        def weigh(z, carry):
            c = cond_s[z]
            co = open_s[z]
            above = jnp.maximum(z - 1, 0)
            below = jnp.minimum(z + 1, layers - 1)
            far = [jnp.where(z > 0, cond_s[above], 0.0), jnp.where(z < layers - 1, cond_s[below], 0.0)]
            far_open = [jnp.where(z > 0, open_s[above], 0.0), jnp.where(z < layers - 1, open_s[below], 0.0)]
            far += shifted(c)
            far_open += shifted(co)
            for i, (_, _, factor) in enumerate(NEIGHBOURS):
                w_s[i, z] = factor * 2.0 * co * far_open[i] / (c + far[i])
            return carry

        lax.fori_loop(0, layers, weigh, 0)
        for sweep in range(SWEEPS):
            last = picard == ITERS - 1 and sweep == SWEEPS - 1
            target = out_ref if last else heads_s.at[count % 2]
            count += 1

            def relax_layer(z, carry, source=source, target=target):
                h = source[z]
                above = jnp.maximum(z - 1, 0)
                below = jnp.minimum(z + 1, layers - 1)
                near = [jnp.where(z > 0, source[above], 0.0), jnp.where(z < layers - 1, source[below], 0.0)]
                near += shifted(h)
                st = store_s[z]
                total = st * old_s[z]
                diagonal_sum = st
                for i in range(len(NEIGHBOURS)):
                    w = w_s[i, z]
                    total = total + w * near[i]
                    diagonal_sum = diagonal_sum + w
                top = z == 0
                total = total + GRAVITY * (w_s[0, z] - w_s[1, z]) + jnp.where(top, river_ref[1], 0.0)
                target[z] = total / (diagonal_sum + jnp.where(top, river_ref[0], 0.0))
                return carry

            lax.fori_loop(0, layers, relax_layer, 0)
            source = target


def stencil(tables, fields, land, river, total_rows):
    _, layers, rows, breadth = fields.shape
    vmem = pl.BlockSpec(memory_space=pltpu.VMEM)
    field = pltpu.VMEM((layers, rows, breadth), jnp.float32)
    cells = layers * rows * breadth
    return pl.pallas_call(
        functools.partial(stencil_kernel, total_rows),
        in_specs=[pl.BlockSpec(memory_space=pltpu.SMEM), vmem, vmem, vmem],
        out_specs=vmem,
        out_shape=jax.ShapeDtypeStruct((layers, rows, breadth), jnp.float32),
        scratch_shapes=[field] * 6
        + [pltpu.VMEM((6, layers, rows, breadth), jnp.float32), pltpu.VMEM((2, layers, rows, breadth), jnp.float32)],
        compiler_params=pltpu.CompilerParams(vmem_limit_bytes=48 * 1024 * 1024),
        cost_estimate=pl.CostEstimate(flops=400 * cells, transcendentals=2 * cells, bytes_accessed=12 * cells),
    )(tables, fields, land, river)


def with_ghost(block, axis, dim, width):
    count = lax.axis_size(axis)
    forward = [(i, i + 1) for i in range(count - 1)]
    backward = [(i + 1, i) for i in range(count - 1)]
    size = block.shape[dim]
    above = lax.ppermute(lax.slice_in_dim(block, size - width, size, axis=dim), axis, forward)
    below = lax.ppermute(lax.slice_in_dim(block, 0, width, axis=dim), axis, backward)
    return jnp.concatenate([above, block, below], axis=dim)


def on_device(
    head_start,
    soil_class,
    land_mask,
    ks_table,
    alpha_table,
    store_table,
    section,
    cross_owner,
    cross_local,
    node_cell,
    bed_cond,
):
    own_layers, across, breadth = head_start.shape
    reach_rows, node_count = section.shape
    tile_count = lax.axis_size("tile")
    layer_count = lax.axis_size("layer")
    tile = lax.axis_index("tile")
    layer = lax.axis_index("layer")
    quarter = node_count // layer_count
    node_first = layer * quarter

    planes = jnp.concatenate(
        [head_start, soil_class.astype(jnp.float32), land_mask.astype(jnp.float32)[None]], axis=0
    )
    planes = with_ghost(planes, "tile", 1, GHOST)
    extent = across + 2 * GHOST
    fields = planes[: 2 * own_layers].reshape(2, own_layers, extent, breadth)
    fields = lax.all_gather(fields, "layer", axis=1, tiled=True)
    owners = cross_owner[0]
    positions = cross_local[0]
    node_cells = node_cell[0]
    bed_given = bed_cond[0]
    slots = owners.shape[0]
    per_owner = slots // tile_count
    order = jnp.arange(slots, dtype=jnp.int32)
    same = owners[:, None] == owners[None, :]
    rank = jnp.sum((same & (order[None, :] < order[:, None])).astype(jnp.int32), axis=1)
    place = owners * per_owner + rank
    at_place = place[None, :] == order[:, None]
    wanted = jnp.sum(jnp.where(at_place, positions[None, :], 0), axis=1)
    in_tile = node_cells >= 0
    bed_terms = jnp.where(in_tile, bed_given, 0.0)
    cell_rows = jnp.where(in_tile, node_cells // breadth, -1).reshape(1, -1)
    cell_cols = jnp.where(in_tile, node_cells % breadth, 0).reshape(1, -1)
    top_diag = river_terms(cell_rows, cell_cols, bed_terms.reshape(1, -1), across, breadth)
    asked = lax.all_to_all(wanted, "tile", 0, 0, tiled=True)
    reply = jnp.take(section, asked, axis=0)
    sorted_section = lax.all_to_all(reply, "tile", 0, 0, tiled=True)
    slot_section = jnp.take(sorted_section, place, axis=0)

    top_rhs = river_terms(cell_rows, cell_cols, (bed_terms * slot_section).reshape(1, -1), across, breadth)
    river = with_ghost(jnp.stack([top_diag, top_rhs]), "tile", 1, GHOST)
    tables = jnp.stack([ks_table, alpha_table, store_table])
    head = stencil(tables, fields, planes[2 * own_layers], river, tile_count * across)
    kept = lax.dynamic_slice_in_dim(head[:, GHOST : GHOST + across], layer * own_layers, own_layers, 0)

    top_head = head[0, GHOST : GHOST + across]
    my_cells = lax.dynamic_slice_in_dim(node_cells, node_first, quarter, 1)
    my_bed = lax.dynamic_slice_in_dim(bed_given, node_first, quarter, 1)
    my_section = lax.dynamic_slice_in_dim(slot_section, node_first, quarter, 1)
    my_inside = my_cells >= 0
    picked = node_heads(
        top_head,
        jnp.where(my_inside, my_cells // breadth, -1).reshape(1, -1),
        jnp.where(my_inside, my_cells % breadth, 0).reshape(1, -1),
    ).reshape(slots, quarter)
    slot_in = jnp.where(my_inside, my_bed * (picked - my_section), 0.0)
    sorted_in = jnp.take(slot_in, jnp.sum(jnp.where(at_place, order[None, :], 0), axis=1), axis=0)
    arrived = lax.all_to_all(sorted_in, "tile", 0, 0, tiled=True)
    target = asked[None, :] == jnp.arange(reach_rows, dtype=jnp.int32)[:, None]
    inflow = jnp.sum(jnp.where(target[:, :, None], arrived[None], 0.0), axis=1)
    return (kept, inflow)


def solution(mesh):
    placed = (
        P("layer", "tile", None),
        P("layer", "tile", None),
        P("tile", None),
        P(),
        P(),
        P(),
        P("tile", None),
        P("tile", None),
        P("tile", None),
        P("tile", None, None),
        P("tile", None, None),
    )
    return jax.shard_map(
        on_device,
        mesh=mesh,
        in_specs=placed,
        out_specs=(P("layer", "tile", None), P("tile", "layer")),
        check_vma=False,
    )
```

```python
import functools

import jax
import jax.numpy as jnp
from jax import lax
from jax.experimental import pallas as pl
from jax.experimental.pallas import tpu as pltpu
from jax.sharding import PartitionSpec as P

ITERS = 2
SWEEPS = 3
GHOST = 8


LATERAL = 1.0
VERTICAL = 2.0
GRAVITY = 1.0
NEIGHBOURS = (
    (0, -1, VERTICAL),
    (0, 1, VERTICAL),
    (1, -1, LATERAL),
    (1, 1, LATERAL),
    (2, -1, LATERAL),
    (2, 1, LATERAL),
)
CHUNK = 2048


def beside(padded, axis_id, step):
    spans = [slice(1, -1), slice(1, -1), slice(1, -1)]
    spans[axis_id] = slice(1 + step, padded.shape[axis_id] - 1 + step)
    return padded[tuple(spans)]


def neighbor_weights(cond_pad, open_pad):
    centre = cond_pad[1:-1, 1:-1, 1:-1]
    centre_open = open_pad[1:-1, 1:-1, 1:-1]
    result = []
    for axis_id, step, factor in NEIGHBOURS:
        far = beside(cond_pad, axis_id, step)
        far_open = beside(open_pad, axis_id, step)
        result.append(factor * 2.0 * centre_open * far_open / (centre + far))
    return result


def relax(head_pad, weights, store, head_old, riv_diag, riv_rhs):
    total = store * head_old
    diagonal_sum = store
    for weight, (axis_id, step, factor) in zip(weights, NEIGHBOURS):
        total = total + weight * beside(head_pad, axis_id, step)
        diagonal_sum = diagonal_sum + weight
    total = total + GRAVITY * (weights[0] - weights[1]) + riv_rhs
    return total / (diagonal_sum + riv_diag)


def lookup(values_table, classes):
    result = jnp.zeros(classes.shape, jnp.float32)
    for class_id in range(values_table.shape[0]):
        result = jnp.where(classes == class_id, values_table[class_id], result)
    return result


def split3(value):
    high = value.astype(jnp.bfloat16).astype(jnp.float32)
    rest = value - high
    middle = rest.astype(jnp.bfloat16).astype(jnp.float32)
    low = rest - middle
    return high, middle, low


def scatter_kernel(rows_ref, cols_ref, diag_in_ref, rhs_in_ref, diag_ref, rhs_ref, acc_ref):
    step = pl.program_id(0)
    grid_rows, breadth = diag_ref.shape
    chunk = rows_ref.shape[1]

    @pl.when(step == 0)
    def _():
        acc_ref[...] = jnp.zeros_like(acc_ref)

    rows = rows_ref[...]

    @pl.when(jnp.max(rows) >= 0)
    def _():
        hit = lax.broadcasted_iota(jnp.int32, (grid_rows, chunk), 0) == rows
        pieces = []
        for value in (diag_in_ref[...], rhs_in_ref[...]):
            for piece in split3(value):
                pieces.append(jnp.where(hit, piece, 0.0).astype(jnp.bfloat16))
        left = jnp.concatenate(pieces, axis=0)
        cols = cols_ref[...]
        column_hit = lax.broadcasted_iota(jnp.int32, (breadth, chunk), 0) == cols
        right = jnp.where(column_hit, 1.0, 0.0).astype(jnp.bfloat16)
        acc_ref[...] += lax.dot_general(
            left, right, (((1,), (1,)), ((), ())), preferred_element_type=jnp.float32
        )

    @pl.when(step == pl.num_programs(0) - 1)
    def _():
        acc = acc_ref[...]
        g = grid_rows
        diag_ref[...] = acc[0:g] + acc[g : 2 * g] + acc[2 * g : 3 * g]
        rhs_ref[...] = acc[3 * g : 4 * g] + acc[4 * g : 5 * g] + acc[5 * g : 6 * g]


def river_terms(rows, cols, diag_values, rhs_values, grid_rows, breadth):
    count = rows.shape[1]
    chunk = min(CHUNK, count)
    lane = pl.BlockSpec((1, chunk), lambda i: (0, i))
    whole = pl.BlockSpec((grid_rows, breadth), lambda i: (0, 0))
    return pl.pallas_call(
        scatter_kernel,
        grid=(count // chunk,),
        in_specs=[lane, lane, lane, lane],
        out_specs=[whole, whole],
        out_shape=[
            jax.ShapeDtypeStruct((grid_rows, breadth), jnp.float32),
            jax.ShapeDtypeStruct((grid_rows, breadth), jnp.float32),
        ],
        scratch_shapes=[pltpu.VMEM((6 * grid_rows, breadth), jnp.float32)],
        compiler_params=pltpu.CompilerParams(vmem_limit_bytes=48 * 1024 * 1024),
        cost_estimate=pl.CostEstimate(
            flops=2 * 6 * grid_rows * breadth * count,
            transcendentals=0,
            bytes_accessed=16 * count + 8 * grid_rows * breadth,
        ),
    )(rows, cols, diag_values, rhs_values)


def gather_kernel(top_ref, rows_ref, cols_ref, out_ref):
    grid_rows, breadth = top_ref.shape
    chunk = rows_ref.shape[1]
    stacked = jnp.concatenate(
        [piece.astype(jnp.bfloat16) for piece in split3(top_ref[...])], axis=0
    )
    cols = cols_ref[...]
    column_hit = lax.broadcasted_iota(jnp.int32, (breadth, chunk), 0) == cols
    right = jnp.where(column_hit, 1.0, 0.0).astype(jnp.bfloat16)
    picked = jnp.dot(stacked, right, preferred_element_type=jnp.float32)
    g = grid_rows
    by_row = picked[0:g] + picked[g : 2 * g] + picked[2 * g : 3 * g]
    rows = rows_ref[...]
    hit = lax.broadcasted_iota(jnp.int32, (grid_rows, chunk), 0) == rows
    out_ref[...] = jnp.sum(jnp.where(hit, by_row, 0.0), axis=0, keepdims=True)


def node_heads(top, rows, cols):
    grid_rows, breadth = top.shape
    count = rows.shape[1]
    chunk = min(CHUNK, count)
    lane = pl.BlockSpec((1, chunk), lambda i: (0, i))
    return pl.pallas_call(
        gather_kernel,
        grid=(count // chunk,),
        compiler_params=pltpu.CompilerParams(vmem_limit_bytes=48 * 1024 * 1024),
        in_specs=[pl.BlockSpec((grid_rows, breadth), lambda i: (0, 0)), lane, lane],
        out_specs=lane,
        out_shape=jax.ShapeDtypeStruct((1, count), jnp.float32),
        cost_estimate=pl.CostEstimate(
            flops=2 * 3 * grid_rows * breadth * count,
            transcendentals=0,
            bytes_accessed=12 * count + 4 * grid_rows * breadth,
        ),
    )(top, rows, cols)


def stencil_kernel(total_rows, tables_ref, fields_ref, land_ref, river_ref, out_ref,
                   ks_s, alpha_s, store_s, old_s, cond_s, open_s, w_s, heads_s):
    layers, rows, breadth = out_ref.shape
    classes_n = tables_ref.shape[1]
    tile = lax.axis_index("tile")
    row_id = lax.broadcasted_iota(jnp.int32, (rows, breadth), 0)
    col_id = lax.broadcasted_iota(jnp.int32, (rows, breadth), 1)
    grow = tile * (rows - 2 * GHOST) - GHOST + row_id
    inside = (grow >= 0) & (grow < total_rows)
    land = jnp.where(inside, land_ref[...], 0.0)
    moves = []
    for axis, size, ident in ((0, rows, row_id), (1, breadth, col_id)):
        for shift in (1, size - 1):
            adjacent = jnp.abs(pltpu.roll(ident, shift, axis) - ident) == 1
            moves.append((axis, shift, adjacent))

    def shifted(x):
        return [jnp.where(adjacent, pltpu.roll(x, shift, axis), 0.0) for axis, shift, adjacent in moves]

    def init(z, carry):
        classes = fields_ref[1, z].astype(jnp.int32)
        looked = [jnp.zeros((rows, breadth), jnp.float32) for _ in range(3)]
        for class_id in range(classes_n):
            hit = classes == class_id
            looked = [jnp.where(hit, tables_ref[t, class_id], looked[t]) for t in range(3)]
        ks_s[z] = jnp.where(inside, looked[0], 1.0)
        alpha_s[z] = jnp.where(inside, looked[1], 0.0)
        store_s[z] = jnp.where(inside, looked[2], 1.0)
        old_s[z] = jnp.where(inside, fields_ref[0, z], 0.0)
        return carry

    lax.fori_loop(0, layers, init, 0)
    source = old_s
    count = 0
    for picard in range(ITERS):

        def conduct(z, carry, source=source):
            k = ks_s[z] * jnp.exp(alpha_s[z] * jnp.minimum(source[z], 0.0))
            cond_s[z] = k
            open_s[z] = k * land
            return carry

        lax.fori_loop(0, layers, conduct, 0)

        def weigh(z, carry):
            c = cond_s[z]
            co = open_s[z]
            above = jnp.maximum(z - 1, 0)
            below = jnp.minimum(z + 1, layers - 1)
            far = [jnp.where(z > 0, cond_s[above], 0.0), jnp.where(z < layers - 1, cond_s[below], 0.0)]
            far_open = [jnp.where(z > 0, open_s[above], 0.0), jnp.where(z < layers - 1, open_s[below], 0.0)]
            far += shifted(c)
            far_open += shifted(co)
            for i, (_, _, factor) in enumerate(NEIGHBOURS):
                w_s[i, z] = factor * 2.0 * co * far_open[i] / (c + far[i])
            return carry

        lax.fori_loop(0, layers, weigh, 0)
        for sweep in range(SWEEPS):
            last = picard == ITERS - 1 and sweep == SWEEPS - 1
            target = out_ref if last else heads_s.at[count % 2]
            count += 1

            def relax_layer(z, carry, source=source, target=target):
                h = source[z]
                above = jnp.maximum(z - 1, 0)
                below = jnp.minimum(z + 1, layers - 1)
                near = [jnp.where(z > 0, source[above], 0.0), jnp.where(z < layers - 1, source[below], 0.0)]
                near += shifted(h)
                st = store_s[z]
                total = st * old_s[z]
                diagonal_sum = st
                for i in range(len(NEIGHBOURS)):
                    w = w_s[i, z]
                    total = total + w * near[i]
                    diagonal_sum = diagonal_sum + w
                top = z == 0
                total = total + GRAVITY * (w_s[0, z] - w_s[1, z]) + jnp.where(top, river_ref[1], 0.0)
                target[z] = total / (diagonal_sum + jnp.where(top, river_ref[0], 0.0))
                return carry

            lax.fori_loop(0, layers, relax_layer, 0)
            source = target


def stencil(tables, fields, land, river, total_rows):
    _, layers, rows, breadth = fields.shape
    vmem = pl.BlockSpec(memory_space=pltpu.VMEM)
    field = pltpu.VMEM((layers, rows, breadth), jnp.float32)
    cells = layers * rows * breadth
    return pl.pallas_call(
        functools.partial(stencil_kernel, total_rows),
        in_specs=[pl.BlockSpec(memory_space=pltpu.SMEM), vmem, vmem, vmem],
        out_specs=vmem,
        out_shape=jax.ShapeDtypeStruct((layers, rows, breadth), jnp.float32),
        scratch_shapes=[field] * 6
        + [pltpu.VMEM((6, layers, rows, breadth), jnp.float32), pltpu.VMEM((2, layers, rows, breadth), jnp.float32)],
        compiler_params=pltpu.CompilerParams(vmem_limit_bytes=48 * 1024 * 1024),
        cost_estimate=pl.CostEstimate(flops=400 * cells, transcendentals=2 * cells, bytes_accessed=12 * cells),
    )(tables, fields, land, river)


def with_ghost(block, axis, dim, width):
    count = lax.axis_size(axis)
    forward = [(i, i + 1) for i in range(count - 1)]
    backward = [(i + 1, i) for i in range(count - 1)]
    size = block.shape[dim]
    above = lax.ppermute(lax.slice_in_dim(block, size - width, size, axis=dim), axis, forward)
    below = lax.ppermute(lax.slice_in_dim(block, 0, width, axis=dim), axis, backward)
    return jnp.concatenate([above, block, below], axis=dim)


def on_device(
    head_start,
    soil_class,
    land_mask,
    ks_table,
    alpha_table,
    store_table,
    section,
    cross_owner,
    cross_local,
    node_cell,
    bed_cond,
):
    own_layers, across, breadth = head_start.shape
    reach_rows, node_count = section.shape
    tile_count = lax.axis_size("tile")
    layer_count = lax.axis_size("layer")
    tile = lax.axis_index("tile")
    layer = lax.axis_index("layer")
    quarter = node_count // layer_count
    node_first = layer * quarter

    planes = jnp.concatenate(
        [head_start, soil_class.astype(jnp.float32), land_mask.astype(jnp.float32)[None]], axis=0
    )
    planes = with_ghost(planes, "tile", 1, GHOST)
    extent = across + 2 * GHOST
    fields = planes[: 2 * own_layers].reshape(2, own_layers, extent, breadth)
    fields = lax.all_gather(fields, "layer", axis=1, tiled=True)
    owners = cross_owner[0]
    positions = cross_local[0]
    node_cells = node_cell[0]
    bed_given = bed_cond[0]
    slots = owners.shape[0]
    per_owner = slots // tile_count
    order = jnp.arange(slots, dtype=jnp.int32)
    same = owners[:, None] == owners[None, :]
    rank = jnp.sum((same & (order[None, :] < order[:, None])).astype(jnp.int32), axis=1)
    place = owners * per_owner + rank
    at_place = place[None, :] == order[:, None]
    wanted = jnp.sum(jnp.where(at_place, positions[None, :], 0), axis=1)
    asked = lax.all_to_all(wanted, "tile", 0, 0, tiled=True)
    reply = jnp.take(section, asked, axis=0)
    sorted_section = lax.all_to_all(reply, "tile", 0, 0, tiled=True)
    slot_section = jnp.take(sorted_section, place, axis=0)

    in_tile = node_cells >= 0
    bed_terms = jnp.where(in_tile, bed_given, 0.0)
    cell_rows = jnp.where(in_tile, node_cells // breadth, -1)
    cell_cols = jnp.where(in_tile, node_cells % breadth, 0)
    top_diag, top_rhs = river_terms(
        cell_rows.reshape(1, -1),
        cell_cols.reshape(1, -1),
        bed_terms.reshape(1, -1),
        (bed_terms * slot_section).reshape(1, -1),
        across,
        breadth,
    )
    river = with_ghost(jnp.stack([top_diag, top_rhs]), "tile", 1, GHOST)
    tables = jnp.stack([ks_table, alpha_table, store_table])
    head = stencil(tables, fields, planes[2 * own_layers], river, tile_count * across)
    kept = lax.dynamic_slice_in_dim(head[:, GHOST : GHOST + across], layer * own_layers, own_layers, 0)

    top_head = head[0, GHOST : GHOST + across]
    my_cells = lax.dynamic_slice_in_dim(node_cells, node_first, quarter, 1)
    my_bed = lax.dynamic_slice_in_dim(bed_given, node_first, quarter, 1)
    my_section = lax.dynamic_slice_in_dim(slot_section, node_first, quarter, 1)
    my_inside = my_cells >= 0
    picked = node_heads(
        top_head,
        jnp.where(my_inside, my_cells // breadth, -1).reshape(1, -1),
        jnp.where(my_inside, my_cells % breadth, 0).reshape(1, -1),
    ).reshape(slots, quarter)
    slot_in = jnp.where(my_inside, my_bed * (picked - my_section), 0.0)
    sorted_in = jnp.take(slot_in, jnp.sum(jnp.where(at_place, order[None, :], 0), axis=1), axis=0)
    arrived = lax.all_to_all(sorted_in, "tile", 0, 0, tiled=True)
    target = asked[None, :] == jnp.arange(reach_rows, dtype=jnp.int32)[:, None]
    inflow = jnp.sum(jnp.where(target[:, :, None], arrived[None], 0.0), axis=1)
    return (kept, inflow)


def solution(mesh):
    placed = (
        P("layer", "tile", None),
        P("layer", "tile", None),
        P("tile", None),
        P(),
        P(),
        P(),
        P("tile", None),
        P("tile", None),
        P("tile", None),
        P("tile", None, None),
        P("tile", None, None),
    )
    return jax.shard_map(
        on_device,
        mesh=mesh,
        in_specs=placed,
        out_specs=(P("layer", "tile", None), P("tile", "layer")),
        check_vma=False,
    )
```

```python
import functools

import jax
import jax.numpy as jnp
from jax import lax
from jax.experimental import pallas as pl
from jax.experimental.pallas import tpu as pltpu
from jax.sharding import PartitionSpec as P

ITERS = 2
SWEEPS = 3
GHOST = 8


LATERAL = 1.0
VERTICAL = 2.0
GRAVITY = 1.0
NEIGHBOURS = (
    (0, -1, VERTICAL),
    (0, 1, VERTICAL),
    (1, -1, LATERAL),
    (1, 1, LATERAL),
    (2, -1, LATERAL),
    (2, 1, LATERAL),
)
CHUNK = 4096


def beside(padded, axis_id, step):
    spans = [slice(1, -1), slice(1, -1), slice(1, -1)]
    spans[axis_id] = slice(1 + step, padded.shape[axis_id] - 1 + step)
    return padded[tuple(spans)]


def neighbor_weights(cond_pad, open_pad):
    centre = cond_pad[1:-1, 1:-1, 1:-1]
    centre_open = open_pad[1:-1, 1:-1, 1:-1]
    result = []
    for axis_id, step, factor in NEIGHBOURS:
        far = beside(cond_pad, axis_id, step)
        far_open = beside(open_pad, axis_id, step)
        result.append(factor * 2.0 * centre_open * far_open / (centre + far))
    return result


def relax(head_pad, weights, store, head_old, riv_diag, riv_rhs):
    total = store * head_old
    diagonal_sum = store
    for weight, (axis_id, step, factor) in zip(weights, NEIGHBOURS):
        total = total + weight * beside(head_pad, axis_id, step)
        diagonal_sum = diagonal_sum + weight
    total = total + GRAVITY * (weights[0] - weights[1]) + riv_rhs
    return total / (diagonal_sum + riv_diag)


def lookup(values_table, classes):
    result = jnp.zeros(classes.shape, jnp.float32)
    for class_id in range(values_table.shape[0]):
        result = jnp.where(classes == class_id, values_table[class_id], result)
    return result


def split3(value):
    high = value.astype(jnp.bfloat16).astype(jnp.float32)
    rest = value - high
    middle = rest.astype(jnp.bfloat16).astype(jnp.float32)
    low = rest - middle
    return high, middle, low


def scatter_kernel(rows_ref, cols_ref, diag_in_ref, rhs_in_ref, diag_ref, rhs_ref, acc_ref):
    step = pl.program_id(0)
    grid_rows, breadth = diag_ref.shape
    chunk = rows_ref.shape[1]

    @pl.when(step == 0)
    def _():
        acc_ref[...] = jnp.zeros_like(acc_ref)

    rows = rows_ref[...]

    @pl.when(jnp.max(rows) >= 0)
    def _():
        hit = lax.broadcasted_iota(jnp.int32, (grid_rows, chunk), 0) == rows
        pieces = []
        for value in (diag_in_ref[...], rhs_in_ref[...]):
            for piece in split3(value):
                pieces.append(jnp.where(hit, piece, 0.0).astype(jnp.bfloat16))
        left = jnp.concatenate(pieces, axis=0)
        cols = cols_ref[...]
        column_hit = lax.broadcasted_iota(jnp.int32, (breadth, chunk), 0) == cols
        right = jnp.where(column_hit, 1.0, 0.0).astype(jnp.bfloat16)
        acc_ref[...] += lax.dot_general(
            left, right, (((1,), (1,)), ((), ())), preferred_element_type=jnp.float32
        )

    @pl.when(step == pl.num_programs(0) - 1)
    def _():
        acc = acc_ref[...]
        g = grid_rows
        diag_ref[...] = acc[0:g] + acc[g : 2 * g] + acc[2 * g : 3 * g]
        rhs_ref[...] = acc[3 * g : 4 * g] + acc[4 * g : 5 * g] + acc[5 * g : 6 * g]


def river_terms(rows, cols, diag_values, rhs_values, grid_rows, breadth):
    count = rows.shape[1]
    chunk = min(CHUNK, count)
    lane = pl.BlockSpec((1, chunk), lambda i: (0, i))
    whole = pl.BlockSpec((grid_rows, breadth), lambda i: (0, 0))
    return pl.pallas_call(
        scatter_kernel,
        grid=(count // chunk,),
        in_specs=[lane, lane, lane, lane],
        out_specs=[whole, whole],
        out_shape=[
            jax.ShapeDtypeStruct((grid_rows, breadth), jnp.float32),
            jax.ShapeDtypeStruct((grid_rows, breadth), jnp.float32),
        ],
        scratch_shapes=[pltpu.VMEM((6 * grid_rows, breadth), jnp.float32)],
        compiler_params=pltpu.CompilerParams(vmem_limit_bytes=48 * 1024 * 1024),
        cost_estimate=pl.CostEstimate(
            flops=2 * 6 * grid_rows * breadth * count,
            transcendentals=0,
            bytes_accessed=16 * count + 8 * grid_rows * breadth,
        ),
    )(rows, cols, diag_values, rhs_values)


def gather_kernel(top_ref, rows_ref, cols_ref, out_ref):
    grid_rows, breadth = top_ref.shape
    chunk = rows_ref.shape[1]
    stacked = jnp.concatenate(
        [piece.astype(jnp.bfloat16) for piece in split3(top_ref[...])], axis=0
    )
    cols = cols_ref[...]
    column_hit = lax.broadcasted_iota(jnp.int32, (breadth, chunk), 0) == cols
    right = jnp.where(column_hit, 1.0, 0.0).astype(jnp.bfloat16)
    picked = jnp.dot(stacked, right, preferred_element_type=jnp.float32)
    g = grid_rows
    by_row = picked[0:g] + picked[g : 2 * g] + picked[2 * g : 3 * g]
    rows = rows_ref[...]
    hit = lax.broadcasted_iota(jnp.int32, (grid_rows, chunk), 0) == rows
    out_ref[...] = jnp.sum(jnp.where(hit, by_row, 0.0), axis=0, keepdims=True)


def node_heads(top, rows, cols):
    grid_rows, breadth = top.shape
    count = rows.shape[1]
    chunk = min(CHUNK, count)
    lane = pl.BlockSpec((1, chunk), lambda i: (0, i))
    return pl.pallas_call(
        gather_kernel,
        grid=(count // chunk,),
        compiler_params=pltpu.CompilerParams(vmem_limit_bytes=48 * 1024 * 1024),
        in_specs=[pl.BlockSpec((grid_rows, breadth), lambda i: (0, 0)), lane, lane],
        out_specs=lane,
        out_shape=jax.ShapeDtypeStruct((1, count), jnp.float32),
        cost_estimate=pl.CostEstimate(
            flops=2 * 3 * grid_rows * breadth * count,
            transcendentals=0,
            bytes_accessed=12 * count + 4 * grid_rows * breadth,
        ),
    )(top, rows, cols)


def stencil_kernel(total_rows, tables_ref, fields_ref, land_ref, river_ref, out_ref,
                   ks_s, alpha_s, store_s, old_s, cond_s, open_s, w_s, heads_s):
    layers, rows, breadth = out_ref.shape
    classes_n = tables_ref.shape[1]
    tile = lax.axis_index("tile")
    row_id = lax.broadcasted_iota(jnp.int32, (rows, breadth), 0)
    col_id = lax.broadcasted_iota(jnp.int32, (rows, breadth), 1)
    grow = tile * (rows - 2 * GHOST) - GHOST + row_id
    inside = (grow >= 0) & (grow < total_rows)
    land = jnp.where(inside, land_ref[...], 0.0)
    moves = []
    for axis, size, ident in ((0, rows, row_id), (1, breadth, col_id)):
        for shift in (1, size - 1):
            adjacent = jnp.abs(pltpu.roll(ident, shift, axis) - ident) == 1
            moves.append((axis, shift, adjacent))

    def shifted(x):
        return [jnp.where(adjacent, pltpu.roll(x, shift, axis), 0.0) for axis, shift, adjacent in moves]

    def init(z, carry):
        classes = fields_ref[1, z].astype(jnp.int32)
        looked = [jnp.zeros((rows, breadth), jnp.float32) for _ in range(3)]
        for class_id in range(classes_n):
            hit = classes == class_id
            looked = [jnp.where(hit, tables_ref[t, class_id], looked[t]) for t in range(3)]
        ks_s[z] = jnp.where(inside, looked[0], 1.0)
        alpha_s[z] = jnp.where(inside, looked[1], 0.0)
        store_s[z] = jnp.where(inside, looked[2], 1.0)
        old_s[z] = jnp.where(inside, fields_ref[0, z], 0.0)
        return carry

    lax.fori_loop(0, layers, init, 0)
    source = old_s
    count = 0
    for picard in range(ITERS):

        def conduct(z, carry, source=source):
            k = ks_s[z] * jnp.exp(alpha_s[z] * jnp.minimum(source[z], 0.0))
            cond_s[z] = k
            open_s[z] = k * land
            return carry

        lax.fori_loop(0, layers, conduct, 0)

        def weigh(z, carry):
            c = cond_s[z]
            co = open_s[z]
            above = jnp.maximum(z - 1, 0)
            below = jnp.minimum(z + 1, layers - 1)
            far = [jnp.where(z > 0, cond_s[above], 0.0), jnp.where(z < layers - 1, cond_s[below], 0.0)]
            far_open = [jnp.where(z > 0, open_s[above], 0.0), jnp.where(z < layers - 1, open_s[below], 0.0)]
            far += shifted(c)
            far_open += shifted(co)
            for i, (_, _, factor) in enumerate(NEIGHBOURS):
                w_s[i, z] = factor * 2.0 * co * far_open[i] / (c + far[i])
            return carry

        lax.fori_loop(0, layers, weigh, 0)
        for sweep in range(SWEEPS):
            last = picard == ITERS - 1 and sweep == SWEEPS - 1
            target = out_ref if last else heads_s.at[count % 2]
            count += 1

            def relax_layer(z, carry, source=source, target=target):
                h = source[z]
                above = jnp.maximum(z - 1, 0)
                below = jnp.minimum(z + 1, layers - 1)
                near = [jnp.where(z > 0, source[above], 0.0), jnp.where(z < layers - 1, source[below], 0.0)]
                near += shifted(h)
                st = store_s[z]
                total = st * old_s[z]
                diagonal_sum = st
                for i in range(len(NEIGHBOURS)):
                    w = w_s[i, z]
                    total = total + w * near[i]
                    diagonal_sum = diagonal_sum + w
                top = z == 0
                total = total + GRAVITY * (w_s[0, z] - w_s[1, z]) + jnp.where(top, river_ref[1], 0.0)
                target[z] = total / (diagonal_sum + jnp.where(top, river_ref[0], 0.0))
                return carry

            lax.fori_loop(0, layers, relax_layer, 0)
            source = target


def stencil(tables, fields, land, river, total_rows):
    _, layers, rows, breadth = fields.shape
    vmem = pl.BlockSpec(memory_space=pltpu.VMEM)
    field = pltpu.VMEM((layers, rows, breadth), jnp.float32)
    cells = layers * rows * breadth
    return pl.pallas_call(
        functools.partial(stencil_kernel, total_rows),
        in_specs=[pl.BlockSpec(memory_space=pltpu.SMEM), vmem, vmem, vmem],
        out_specs=vmem,
        out_shape=jax.ShapeDtypeStruct((layers, rows, breadth), jnp.float32),
        scratch_shapes=[field] * 6
        + [pltpu.VMEM((6, layers, rows, breadth), jnp.float32), pltpu.VMEM((2, layers, rows, breadth), jnp.float32)],
        compiler_params=pltpu.CompilerParams(vmem_limit_bytes=48 * 1024 * 1024),
        cost_estimate=pl.CostEstimate(flops=400 * cells, transcendentals=2 * cells, bytes_accessed=12 * cells),
    )(tables, fields, land, river)


def with_ghost(block, axis, dim, width):
    count = lax.axis_size(axis)
    forward = [(i, i + 1) for i in range(count - 1)]
    backward = [(i + 1, i) for i in range(count - 1)]
    size = block.shape[dim]
    above = lax.ppermute(lax.slice_in_dim(block, size - width, size, axis=dim), axis, forward)
    below = lax.ppermute(lax.slice_in_dim(block, 0, width, axis=dim), axis, backward)
    return jnp.concatenate([above, block, below], axis=dim)


def on_device(
    head_start,
    soil_class,
    land_mask,
    ks_table,
    alpha_table,
    store_table,
    section,
    cross_owner,
    cross_local,
    node_cell,
    bed_cond,
):
    own_layers, across, breadth = head_start.shape
    reach_rows, node_count = section.shape
    tile_count = lax.axis_size("tile")
    layer_count = lax.axis_size("layer")
    tile = lax.axis_index("tile")
    layer = lax.axis_index("layer")
    quarter = node_count // layer_count
    node_first = layer * quarter

    fields = jnp.stack([head_start, soil_class.astype(jnp.float32)])
    fields = lax.all_gather(fields, "layer", axis=1, tiled=True)
    fields = with_ghost(fields, "tile", 2, GHOST)
    land = with_ghost(land_mask.astype(jnp.float32), "tile", 0, GHOST)

    owners = cross_owner[0]
    positions = cross_local[0]
    node_cells = node_cell[0]
    bed_given = bed_cond[0]
    slots = owners.shape[0]
    per_owner = slots // tile_count
    order = jnp.arange(slots, dtype=jnp.int32)
    same = owners[:, None] == owners[None, :]
    rank = jnp.sum((same & (order[None, :] < order[:, None])).astype(jnp.int32), axis=1)
    place = owners * per_owner + rank
    at_place = place[None, :] == order[:, None]
    wanted = jnp.sum(jnp.where(at_place, positions[None, :], 0), axis=1)
    asked = lax.all_to_all(wanted, "tile", 0, 0, tiled=True)
    reply = jnp.take(section, asked, axis=0)
    sorted_section = lax.all_to_all(reply, "tile", 0, 0, tiled=True)
    slot_section = jnp.take(sorted_section, place, axis=0)

    in_tile = node_cells >= 0
    bed_terms = jnp.where(in_tile, bed_given, 0.0)
    cell_rows = jnp.where(in_tile, node_cells // breadth, -1)
    cell_cols = jnp.where(in_tile, node_cells % breadth, 0)
    top_diag, top_rhs = river_terms(
        cell_rows.reshape(1, -1),
        cell_cols.reshape(1, -1),
        bed_terms.reshape(1, -1),
        (bed_terms * slot_section).reshape(1, -1),
        across,
        breadth,
    )
    river = with_ghost(jnp.stack([top_diag, top_rhs]), "tile", 1, GHOST)
    tables = jnp.stack([ks_table, alpha_table, store_table])
    head = stencil(tables, fields, land, river, tile_count * across)
    kept = lax.dynamic_slice_in_dim(head[:, GHOST : GHOST + across], layer * own_layers, own_layers, 0)

    top_head = head[0, GHOST : GHOST + across]
    my_cells = lax.dynamic_slice_in_dim(node_cells, node_first, quarter, 1)
    my_bed = lax.dynamic_slice_in_dim(bed_given, node_first, quarter, 1)
    my_section = lax.dynamic_slice_in_dim(slot_section, node_first, quarter, 1)
    my_inside = my_cells >= 0
    picked = node_heads(
        top_head,
        jnp.where(my_inside, my_cells // breadth, -1).reshape(1, -1),
        jnp.where(my_inside, my_cells % breadth, 0).reshape(1, -1),
    ).reshape(slots, quarter)
    slot_in = jnp.where(my_inside, my_bed * (picked - my_section), 0.0)
    sorted_in = jnp.take(slot_in, jnp.sum(jnp.where(at_place, order[None, :], 0), axis=1), axis=0)
    arrived = lax.all_to_all(sorted_in, "tile", 0, 0, tiled=True)
    target = asked[None, :] == jnp.arange(reach_rows, dtype=jnp.int32)[:, None]
    inflow = jnp.sum(jnp.where(target[:, :, None], arrived[None], 0.0), axis=1)
    return (kept, inflow)


def solution(mesh):
    placed = (
        P("layer", "tile", None),
        P("layer", "tile", None),
        P("tile", None),
        P(),
        P(),
        P(),
        P("tile", None),
        P("tile", None),
        P("tile", None),
        P("tile", None, None),
        P("tile", None, None),
    )
    return jax.shard_map(
        on_device,
        mesh=mesh,
        in_specs=placed,
        out_specs=(P("layer", "tile", None), P("tile", "layer")),
        check_vma=False,
    )
```

```python
import functools

import jax
import jax.numpy as jnp
from jax import lax
from jax.experimental import pallas as pl
from jax.experimental.pallas import tpu as pltpu
from jax.sharding import PartitionSpec as P

ITERS = 2
SWEEPS = 3
GHOST = 8


LATERAL = 1.0
VERTICAL = 2.0
GRAVITY = 1.0
NEIGHBOURS = (
    (0, -1, VERTICAL),
    (0, 1, VERTICAL),
    (1, -1, LATERAL),
    (1, 1, LATERAL),
    (2, -1, LATERAL),
    (2, 1, LATERAL),
)
CHUNK = 4096


def beside(padded, axis_id, step):
    spans = [slice(1, -1), slice(1, -1), slice(1, -1)]
    spans[axis_id] = slice(1 + step, padded.shape[axis_id] - 1 + step)
    return padded[tuple(spans)]


def neighbor_weights(cond_pad, open_pad):
    centre = cond_pad[1:-1, 1:-1, 1:-1]
    centre_open = open_pad[1:-1, 1:-1, 1:-1]
    result = []
    for axis_id, step, factor in NEIGHBOURS:
        far = beside(cond_pad, axis_id, step)
        far_open = beside(open_pad, axis_id, step)
        result.append(factor * 2.0 * centre_open * far_open / (centre + far))
    return result


def relax(head_pad, weights, store, head_old, riv_diag, riv_rhs):
    total = store * head_old
    diagonal_sum = store
    for weight, (axis_id, step, factor) in zip(weights, NEIGHBOURS):
        total = total + weight * beside(head_pad, axis_id, step)
        diagonal_sum = diagonal_sum + weight
    total = total + GRAVITY * (weights[0] - weights[1]) + riv_rhs
    return total / (diagonal_sum + riv_diag)


def lookup(values_table, classes):
    result = jnp.zeros(classes.shape, jnp.float32)
    for class_id in range(values_table.shape[0]):
        result = jnp.where(classes == class_id, values_table[class_id], result)
    return result


def split3(value):
    high = value.astype(jnp.bfloat16).astype(jnp.float32)
    rest = value - high
    middle = rest.astype(jnp.bfloat16).astype(jnp.float32)
    low = rest - middle
    return high, middle, low


def scatter_kernel(rows_ref, cols_ref, diag_in_ref, rhs_in_ref, diag_ref, rhs_ref, acc_ref):
    step = pl.program_id(0)
    grid_rows, breadth = diag_ref.shape
    chunk = rows_ref.shape[1]

    @pl.when(step == 0)
    def _():
        acc_ref[...] = jnp.zeros_like(acc_ref)

    rows = rows_ref[...]

    @pl.when(jnp.max(rows) >= 0)
    def _():
        hit = lax.broadcasted_iota(jnp.int32, (grid_rows, chunk), 0) == rows
        pieces = []
        for value in (diag_in_ref[...], rhs_in_ref[...]):
            for piece in split3(value):
                pieces.append(jnp.where(hit, piece, 0.0).astype(jnp.bfloat16))
        left = jnp.concatenate(pieces, axis=0)
        cols = cols_ref[...]
        column_hit = lax.broadcasted_iota(jnp.int32, (breadth, chunk), 0) == cols
        right = jnp.where(column_hit, 1.0, 0.0).astype(jnp.bfloat16)
        acc_ref[...] += lax.dot_general(
            left, right, (((1,), (1,)), ((), ())), preferred_element_type=jnp.float32
        )

    @pl.when(step == pl.num_programs(0) - 1)
    def _():
        acc = acc_ref[...]
        g = grid_rows
        diag_ref[...] = acc[0:g] + acc[g : 2 * g] + acc[2 * g : 3 * g]
        rhs_ref[...] = acc[3 * g : 4 * g] + acc[4 * g : 5 * g] + acc[5 * g : 6 * g]


def river_terms(rows, cols, diag_values, rhs_values, grid_rows, breadth):
    count = rows.shape[1]
    chunk = min(CHUNK, count)
    lane = pl.BlockSpec((1, chunk), lambda i: (0, i))
    whole = pl.BlockSpec((grid_rows, breadth), lambda i: (0, 0))
    return pl.pallas_call(
        scatter_kernel,
        grid=(count // chunk,),
        in_specs=[lane, lane, lane, lane],
        out_specs=[whole, whole],
        out_shape=[
            jax.ShapeDtypeStruct((grid_rows, breadth), jnp.float32),
            jax.ShapeDtypeStruct((grid_rows, breadth), jnp.float32),
        ],
        scratch_shapes=[pltpu.VMEM((6 * grid_rows, breadth), jnp.float32)],
        compiler_params=pltpu.CompilerParams(vmem_limit_bytes=48 * 1024 * 1024),
        cost_estimate=pl.CostEstimate(
            flops=2 * 6 * grid_rows * breadth * count,
            transcendentals=0,
            bytes_accessed=16 * count + 8 * grid_rows * breadth,
        ),
    )(rows, cols, diag_values, rhs_values)


def gather_kernel(top_ref, rows_ref, cols_ref, out_ref):
    grid_rows, breadth = top_ref.shape
    chunk = rows_ref.shape[1]
    stacked = jnp.concatenate(
        [piece.astype(jnp.bfloat16) for piece in split3(top_ref[...])], axis=0
    )
    cols = cols_ref[...]
    column_hit = lax.broadcasted_iota(jnp.int32, (breadth, chunk), 0) == cols
    right = jnp.where(column_hit, 1.0, 0.0).astype(jnp.bfloat16)
    picked = jnp.dot(stacked, right, preferred_element_type=jnp.float32)
    g = grid_rows
    by_row = picked[0:g] + picked[g : 2 * g] + picked[2 * g : 3 * g]
    rows = rows_ref[...]
    hit = lax.broadcasted_iota(jnp.int32, (grid_rows, chunk), 0) == rows
    out_ref[...] = jnp.sum(jnp.where(hit, by_row, 0.0), axis=0, keepdims=True)


def node_heads(top, rows, cols):
    grid_rows, breadth = top.shape
    count = rows.shape[1]
    chunk = min(CHUNK, count)
    lane = pl.BlockSpec((1, chunk), lambda i: (0, i))
    return pl.pallas_call(
        gather_kernel,
        grid=(count // chunk,),
        compiler_params=pltpu.CompilerParams(vmem_limit_bytes=48 * 1024 * 1024),
        in_specs=[pl.BlockSpec((grid_rows, breadth), lambda i: (0, 0)), lane, lane],
        out_specs=lane,
        out_shape=jax.ShapeDtypeStruct((1, count), jnp.float32),
        cost_estimate=pl.CostEstimate(
            flops=2 * 3 * grid_rows * breadth * count,
            transcendentals=0,
            bytes_accessed=12 * count + 4 * grid_rows * breadth,
        ),
    )(top, rows, cols)


def stencil_kernel(total_rows, tables_ref, fields_ref, land_ref, river_ref, out_ref,
                   ks_s, alpha_s, store_s, old_s, cond_s, open_s, w_s, heads_s):
    layers, rows, breadth = out_ref.shape
    classes_n = tables_ref.shape[1]
    tile = lax.axis_index("tile")
    row_id = lax.broadcasted_iota(jnp.int32, (rows, breadth), 0)
    col_id = lax.broadcasted_iota(jnp.int32, (rows, breadth), 1)
    grow = tile * (rows - 2 * GHOST) - GHOST + row_id
    inside = (grow >= 0) & (grow < total_rows)
    land = jnp.where(inside, land_ref[...], 0.0)
    moves = []
    for axis, size, ident in ((0, rows, row_id), (1, breadth, col_id)):
        for shift in (1, size - 1):
            adjacent = jnp.abs(pltpu.roll(ident, shift, axis) - ident) == 1
            moves.append((axis, shift, adjacent))

    def shifted(x):
        return [jnp.where(adjacent, pltpu.roll(x, shift, axis), 0.0) for axis, shift, adjacent in moves]

    def init(z, carry):
        classes = fields_ref[1, z].astype(jnp.int32)
        looked = [jnp.zeros((rows, breadth), jnp.float32) for _ in range(3)]
        for class_id in range(classes_n):
            hit = classes == class_id
            looked = [jnp.where(hit, tables_ref[t, class_id], looked[t]) for t in range(3)]
        ks_s[z] = jnp.where(inside, looked[0], 1.0)
        alpha_s[z] = jnp.where(inside, looked[1], 0.0)
        store_s[z] = jnp.where(inside, looked[2], 1.0)
        old_s[z] = jnp.where(inside, fields_ref[0, z], 0.0)
        return carry

    lax.fori_loop(0, layers, init, 0)
    source = old_s
    count = 0
    for picard in range(ITERS):

        def conduct(z, carry, source=source):
            k = ks_s[z] * jnp.exp(alpha_s[z] * jnp.minimum(source[z], 0.0))
            cond_s[z] = k
            open_s[z] = k * land
            return carry

        lax.fori_loop(0, layers, conduct, 0)

        def weigh(z, carry):
            c = cond_s[z]
            co = open_s[z]
            above = jnp.maximum(z - 1, 0)
            below = jnp.minimum(z + 1, layers - 1)
            far = [jnp.where(z > 0, cond_s[above], 0.0), jnp.where(z < layers - 1, cond_s[below], 0.0)]
            far_open = [jnp.where(z > 0, open_s[above], 0.0), jnp.where(z < layers - 1, open_s[below], 0.0)]
            far += shifted(c)
            far_open += shifted(co)
            for i, (_, _, factor) in enumerate(NEIGHBOURS):
                w_s[i, z] = factor * 2.0 * co * far_open[i] / (c + far[i])
            return carry

        lax.fori_loop(0, layers, weigh, 0)
        for sweep in range(SWEEPS):
            last = picard == ITERS - 1 and sweep == SWEEPS - 1
            target = out_ref if last else heads_s.at[count % 2]
            count += 1

            def relax_layer(z, carry, source=source, target=target):
                h = source[z]
                above = jnp.maximum(z - 1, 0)
                below = jnp.minimum(z + 1, layers - 1)
                near = [jnp.where(z > 0, source[above], 0.0), jnp.where(z < layers - 1, source[below], 0.0)]
                near += shifted(h)
                st = store_s[z]
                total = st * old_s[z]
                diagonal_sum = st
                for i in range(len(NEIGHBOURS)):
                    w = w_s[i, z]
                    total = total + w * near[i]
                    diagonal_sum = diagonal_sum + w
                top = z == 0
                total = total + GRAVITY * (w_s[0, z] - w_s[1, z]) + jnp.where(top, river_ref[1], 0.0)
                target[z] = total / (diagonal_sum + jnp.where(top, river_ref[0], 0.0))
                return carry

            lax.fori_loop(0, layers, relax_layer, 0)
            source = target


def stencil(tables, fields, land, river, total_rows):
    _, layers, rows, breadth = fields.shape
    vmem = pl.BlockSpec(memory_space=pltpu.VMEM)
    field = pltpu.VMEM((layers, rows, breadth), jnp.float32)
    cells = layers * rows * breadth
    return pl.pallas_call(
        functools.partial(stencil_kernel, total_rows),
        in_specs=[pl.BlockSpec(memory_space=pltpu.SMEM), vmem, vmem, vmem],
        out_specs=vmem,
        out_shape=jax.ShapeDtypeStruct((layers, rows, breadth), jnp.float32),
        scratch_shapes=[field] * 6
        + [pltpu.VMEM((6, layers, rows, breadth), jnp.float32), pltpu.VMEM((2, layers, rows, breadth), jnp.float32)],
        compiler_params=pltpu.CompilerParams(vmem_limit_bytes=48 * 1024 * 1024),
        cost_estimate=pl.CostEstimate(flops=400 * cells, transcendentals=2 * cells, bytes_accessed=12 * cells),
    )(tables, fields, land, river)


def with_ghost(block, axis, dim, width):
    count = lax.axis_size(axis)
    forward = [(i, i + 1) for i in range(count - 1)]
    backward = [(i + 1, i) for i in range(count - 1)]
    size = block.shape[dim]
    above = lax.ppermute(lax.slice_in_dim(block, size - width, size, axis=dim), axis, forward)
    below = lax.ppermute(lax.slice_in_dim(block, 0, width, axis=dim), axis, backward)
    return jnp.concatenate([above, block, below], axis=dim)


def on_device(
    head_start,
    soil_class,
    land_mask,
    ks_table,
    alpha_table,
    store_table,
    section,
    cross_owner,
    cross_local,
    node_cell,
    bed_cond,
):
    own_layers, across, breadth = head_start.shape
    reach_rows, node_count = section.shape
    tile_count = lax.axis_size("tile")
    layer_count = lax.axis_size("layer")
    tile = lax.axis_index("tile")
    layer = lax.axis_index("layer")
    quarter = node_count // layer_count
    node_first = layer * quarter

    fields = jnp.stack([head_start, soil_class.astype(jnp.float32)])
    edges = with_ghost(fields, "tile", 2, GHOST)
    edges = jnp.concatenate([edges[:, :, :GHOST], edges[:, :, GHOST + across :]], axis=2)
    fields = lax.all_gather(fields, "layer", axis=1, tiled=True)
    edges = lax.all_gather(edges, "layer", axis=1, tiled=True)
    fields = jnp.concatenate([edges[:, :, :GHOST], fields, edges[:, :, GHOST:]], axis=2)
    land = with_ghost(land_mask.astype(jnp.float32), "tile", 0, GHOST)

    owners = cross_owner[0]
    positions = cross_local[0]
    node_cells = node_cell[0]
    bed_given = bed_cond[0]
    slots = owners.shape[0]
    per_owner = slots // tile_count
    order = jnp.arange(slots, dtype=jnp.int32)
    same = owners[:, None] == owners[None, :]
    rank = jnp.sum((same & (order[None, :] < order[:, None])).astype(jnp.int32), axis=1)
    place = owners * per_owner + rank
    at_place = place[None, :] == order[:, None]
    wanted = jnp.sum(jnp.where(at_place, positions[None, :], 0), axis=1)
    asked = lax.all_to_all(wanted, "tile", 0, 0, tiled=True)
    reply = jnp.take(section, asked, axis=0)
    sorted_section = lax.all_to_all(reply, "tile", 0, 0, tiled=True)
    slot_section = jnp.take(sorted_section, place, axis=0)

    in_tile = node_cells >= 0
    bed_terms = jnp.where(in_tile, bed_given, 0.0)
    cell_rows = jnp.where(in_tile, node_cells // breadth, -1)
    cell_cols = jnp.where(in_tile, node_cells % breadth, 0)
    top_diag, top_rhs = river_terms(
        cell_rows.reshape(1, -1),
        cell_cols.reshape(1, -1),
        bed_terms.reshape(1, -1),
        (bed_terms * slot_section).reshape(1, -1),
        across,
        breadth,
    )
    river = with_ghost(jnp.stack([top_diag, top_rhs]), "tile", 1, GHOST)
    tables = jnp.stack([ks_table, alpha_table, store_table])
    head = stencil(tables, fields, land, river, tile_count * across)
    kept = lax.dynamic_slice_in_dim(head[:, GHOST : GHOST + across], layer * own_layers, own_layers, 0)

    top_head = head[0, GHOST : GHOST + across]
    my_cells = lax.dynamic_slice_in_dim(node_cells, node_first, quarter, 1)
    my_bed = lax.dynamic_slice_in_dim(bed_given, node_first, quarter, 1)
    my_section = lax.dynamic_slice_in_dim(slot_section, node_first, quarter, 1)
    my_inside = my_cells >= 0
    picked = node_heads(
        top_head,
        jnp.where(my_inside, my_cells // breadth, -1).reshape(1, -1),
        jnp.where(my_inside, my_cells % breadth, 0).reshape(1, -1),
    ).reshape(slots, quarter)
    slot_in = jnp.where(my_inside, my_bed * (picked - my_section), 0.0)
    sorted_in = jnp.take(slot_in, jnp.sum(jnp.where(at_place, order[None, :], 0), axis=1), axis=0)
    arrived = lax.all_to_all(sorted_in, "tile", 0, 0, tiled=True)
    target = asked[None, :] == jnp.arange(reach_rows, dtype=jnp.int32)[:, None]
    inflow = jnp.sum(jnp.where(target[:, :, None], arrived[None], 0.0), axis=1)
    return (kept, inflow)


def solution(mesh):
    placed = (
        P("layer", "tile", None),
        P("layer", "tile", None),
        P("tile", None),
        P(),
        P(),
        P(),
        P("tile", None),
        P("tile", None),
        P("tile", None),
        P("tile", None, None),
        P("tile", None, None),
    )
    return jax.shard_map(
        on_device,
        mesh=mesh,
        in_specs=placed,
        out_specs=(P("layer", "tile", None), P("tile", "layer")),
        check_vma=False,
    )
```

```python
import functools

import jax
import jax.numpy as jnp
from jax import lax
from jax.experimental import pallas as pl
from jax.experimental.pallas import tpu as pltpu
from jax.sharding import PartitionSpec as P

ITERS = 2
SWEEPS = 3
GHOST = 8


LATERAL = 1.0
VERTICAL = 2.0
GRAVITY = 1.0
NEIGHBOURS = (
    (0, -1, VERTICAL),
    (0, 1, VERTICAL),
    (1, -1, LATERAL),
    (1, 1, LATERAL),
    (2, -1, LATERAL),
    (2, 1, LATERAL),
)
CHUNK = 2048


def beside(padded, axis_id, step):
    spans = [slice(1, -1), slice(1, -1), slice(1, -1)]
    spans[axis_id] = slice(1 + step, padded.shape[axis_id] - 1 + step)
    return padded[tuple(spans)]


def neighbor_weights(cond_pad, open_pad):
    centre = cond_pad[1:-1, 1:-1, 1:-1]
    centre_open = open_pad[1:-1, 1:-1, 1:-1]
    result = []
    for axis_id, step, factor in NEIGHBOURS:
        far = beside(cond_pad, axis_id, step)
        far_open = beside(open_pad, axis_id, step)
        result.append(factor * 2.0 * centre_open * far_open / (centre + far))
    return result


def relax(head_pad, weights, store, head_old, riv_diag, riv_rhs):
    total = store * head_old
    diagonal_sum = store
    for weight, (axis_id, step, factor) in zip(weights, NEIGHBOURS):
        total = total + weight * beside(head_pad, axis_id, step)
        diagonal_sum = diagonal_sum + weight
    total = total + GRAVITY * (weights[0] - weights[1]) + riv_rhs
    return total / (diagonal_sum + riv_diag)


def lookup(values_table, classes):
    result = jnp.zeros(classes.shape, jnp.float32)
    for class_id in range(values_table.shape[0]):
        result = jnp.where(classes == class_id, values_table[class_id], result)
    return result


def split3(value):
    high = value.astype(jnp.bfloat16).astype(jnp.float32)
    rest = value - high
    middle = rest.astype(jnp.bfloat16).astype(jnp.float32)
    low = rest - middle
    return high, middle, low


def scatter_kernel(rows_ref, cols_ref, diag_in_ref, rhs_in_ref, diag_ref, rhs_ref, acc_ref):
    step = pl.program_id(0)
    grid_rows, breadth = diag_ref.shape
    chunk = rows_ref.shape[1]

    @pl.when(step == 0)
    def _():
        acc_ref[...] = jnp.zeros_like(acc_ref)

    rows = rows_ref[...]

    @pl.when(jnp.max(rows) >= 0)
    def _():
        hit = lax.broadcasted_iota(jnp.int32, (grid_rows, chunk), 0) == rows
        pieces = []
        for value in (diag_in_ref[...], rhs_in_ref[...]):
            for piece in split3(value):
                pieces.append(jnp.where(hit, piece, 0.0).astype(jnp.bfloat16))
        left = jnp.concatenate(pieces, axis=0)
        cols = cols_ref[...]
        column_hit = lax.broadcasted_iota(jnp.int32, (breadth, chunk), 0) == cols
        right = jnp.where(column_hit, 1.0, 0.0).astype(jnp.bfloat16)
        acc_ref[...] += lax.dot_general(
            left, right, (((1,), (1,)), ((), ())), preferred_element_type=jnp.float32
        )

    @pl.when(step == pl.num_programs(0) - 1)
    def _():
        acc = acc_ref[...]
        g = grid_rows
        diag_ref[...] = acc[0:g] + acc[g : 2 * g] + acc[2 * g : 3 * g]
        rhs_ref[...] = acc[3 * g : 4 * g] + acc[4 * g : 5 * g] + acc[5 * g : 6 * g]


def river_terms(rows, cols, diag_values, rhs_values, grid_rows, breadth):
    count = rows.shape[1]
    chunk = min(CHUNK, count)
    lane = pl.BlockSpec((1, chunk), lambda i: (0, i))
    whole = pl.BlockSpec((grid_rows, breadth), lambda i: (0, 0))
    return pl.pallas_call(
        scatter_kernel,
        grid=(count // chunk,),
        in_specs=[lane, lane, lane, lane],
        out_specs=[whole, whole],
        out_shape=[
            jax.ShapeDtypeStruct((grid_rows, breadth), jnp.float32),
            jax.ShapeDtypeStruct((grid_rows, breadth), jnp.float32),
        ],
        scratch_shapes=[pltpu.VMEM((6 * grid_rows, breadth), jnp.float32)],
        compiler_params=pltpu.CompilerParams(vmem_limit_bytes=48 * 1024 * 1024),
        cost_estimate=pl.CostEstimate(
            flops=2 * 6 * grid_rows * breadth * count,
            transcendentals=0,
            bytes_accessed=16 * count + 8 * grid_rows * breadth,
        ),
    )(rows, cols, diag_values, rhs_values)


def gather_kernel(top_ref, rows_ref, cols_ref, out_ref):
    grid_rows, breadth = top_ref.shape
    chunk = rows_ref.shape[1]
    stacked = jnp.concatenate(
        [piece.astype(jnp.bfloat16) for piece in split3(top_ref[...])], axis=0
    )
    cols = cols_ref[...]
    column_hit = lax.broadcasted_iota(jnp.int32, (breadth, chunk), 0) == cols
    right = jnp.where(column_hit, 1.0, 0.0).astype(jnp.bfloat16)
    picked = jnp.dot(stacked, right, preferred_element_type=jnp.float32)
    g = grid_rows
    by_row = picked[0:g] + picked[g : 2 * g] + picked[2 * g : 3 * g]
    rows = rows_ref[...]
    hit = lax.broadcasted_iota(jnp.int32, (grid_rows, chunk), 0) == rows
    out_ref[...] = jnp.sum(jnp.where(hit, by_row, 0.0), axis=0, keepdims=True)


def node_heads(top, rows, cols):
    grid_rows, breadth = top.shape
    count = rows.shape[1]
    chunk = min(CHUNK, count)
    lane = pl.BlockSpec((1, chunk), lambda i: (0, i))
    return pl.pallas_call(
        gather_kernel,
        grid=(count // chunk,),
        compiler_params=pltpu.CompilerParams(vmem_limit_bytes=48 * 1024 * 1024),
        in_specs=[pl.BlockSpec((grid_rows, breadth), lambda i: (0, 0)), lane, lane],
        out_specs=lane,
        out_shape=jax.ShapeDtypeStruct((1, count), jnp.float32),
        cost_estimate=pl.CostEstimate(
            flops=2 * 3 * grid_rows * breadth * count,
            transcendentals=0,
            bytes_accessed=12 * count + 4 * grid_rows * breadth,
        ),
    )(top, rows, cols)


def stencil_kernel(total_rows, tables_ref, fields_ref, land_ref, river_ref, out_ref,
                   ks_s, alpha_s, store_s, old_s, cond_s, open_s, w_s, heads_s):
    layers, rows, breadth = out_ref.shape
    classes_n = tables_ref.shape[1]
    tile = lax.axis_index("tile")
    row_id = lax.broadcasted_iota(jnp.int32, (rows, breadth), 0)
    col_id = lax.broadcasted_iota(jnp.int32, (rows, breadth), 1)
    grow = tile * (rows - 2 * GHOST) - GHOST + row_id
    inside = (grow >= 0) & (grow < total_rows)
    land = jnp.where(inside, land_ref[...], 0.0)
    moves = []
    for axis, size, ident in ((0, rows, row_id), (1, breadth, col_id)):
        for shift in (1, size - 1):
            adjacent = jnp.abs(pltpu.roll(ident, shift, axis) - ident) == 1
            moves.append((axis, shift, adjacent))

    def shifted(x):
        return [jnp.where(adjacent, pltpu.roll(x, shift, axis), 0.0) for axis, shift, adjacent in moves]

    def init(z, carry):
        classes = fields_ref[1, z].astype(jnp.int32)
        looked = [jnp.zeros((rows, breadth), jnp.float32) for _ in range(3)]
        for class_id in range(classes_n):
            hit = classes == class_id
            looked = [jnp.where(hit, tables_ref[t, class_id], looked[t]) for t in range(3)]
        ks_s[z] = jnp.where(inside, looked[0], 1.0)
        alpha_s[z] = jnp.where(inside, looked[1], 0.0)
        store_s[z] = jnp.where(inside, looked[2], 1.0)
        old_s[z] = jnp.where(inside, fields_ref[0, z], 0.0)
        return carry

    lax.fori_loop(0, layers, init, 0)
    source = old_s
    count = 0
    for picard in range(ITERS):

        def conduct(z, carry, source=source):
            k = ks_s[z] * jnp.exp(alpha_s[z] * jnp.minimum(source[z], 0.0))
            cond_s[z] = k
            open_s[z] = k * land
            return carry

        lax.fori_loop(0, layers, conduct, 0)

        def weigh(z, carry):
            c = cond_s[z]
            co = open_s[z]
            below = jnp.minimum(z + 1, layers - 1)
            far = jnp.where(z < layers - 1, cond_s[below], 0.0)
            far_open = jnp.where(z < layers - 1, open_s[below], 0.0)
            w_s[1, z] = VERTICAL * 2.0 * co * far_open / (c + far)
            w_s[0, z] = jnp.where(z > 0, w_s[1, jnp.maximum(z - 1, 0)], 0.0)
            for axis, first, second in ((0, 0, 1), (1, 2, 3)):
                _, shift, adjacent = moves[first]
                face = LATERAL * 2.0 * co * jnp.where(adjacent, pltpu.roll(co, shift, axis), 0.0) / (
                    c + jnp.where(adjacent, pltpu.roll(c, shift, axis), 0.0)
                )
                _, back, back_adjacent = moves[second]
                w_s[2 * axis + 2, z] = face
                w_s[2 * axis + 3, z] = jnp.where(back_adjacent, pltpu.roll(face, back, axis), 0.0)
            return carry

        lax.fori_loop(0, layers, weigh, 0)
        for sweep in range(SWEEPS):
            last = picard == ITERS - 1 and sweep == SWEEPS - 1
            target = out_ref if last else heads_s.at[count % 2]
            count += 1

            def relax_layer(z, carry, source=source, target=target):
                h = source[z]
                above = jnp.maximum(z - 1, 0)
                below = jnp.minimum(z + 1, layers - 1)
                near = [jnp.where(z > 0, source[above], 0.0), jnp.where(z < layers - 1, source[below], 0.0)]
                near += shifted(h)
                st = store_s[z]
                total = st * old_s[z]
                diagonal_sum = st
                for i in range(len(NEIGHBOURS)):
                    w = w_s[i, z]
                    total = total + w * near[i]
                    diagonal_sum = diagonal_sum + w
                top = z == 0
                total = total + GRAVITY * (w_s[0, z] - w_s[1, z]) + jnp.where(top, river_ref[1], 0.0)
                target[z] = total / (diagonal_sum + jnp.where(top, river_ref[0], 0.0))
                return carry

            lax.fori_loop(0, layers, relax_layer, 0)
            source = target


def stencil(tables, fields, land, river, total_rows):
    _, layers, rows, breadth = fields.shape
    vmem = pl.BlockSpec(memory_space=pltpu.VMEM)
    field = pltpu.VMEM((layers, rows, breadth), jnp.float32)
    cells = layers * rows * breadth
    return pl.pallas_call(
        functools.partial(stencil_kernel, total_rows),
        in_specs=[pl.BlockSpec(memory_space=pltpu.SMEM), vmem, vmem, vmem],
        out_specs=vmem,
        out_shape=jax.ShapeDtypeStruct((layers, rows, breadth), jnp.float32),
        scratch_shapes=[field] * 6
        + [pltpu.VMEM((6, layers, rows, breadth), jnp.float32), pltpu.VMEM((2, layers, rows, breadth), jnp.float32)],
        compiler_params=pltpu.CompilerParams(vmem_limit_bytes=48 * 1024 * 1024),
        cost_estimate=pl.CostEstimate(flops=400 * cells, transcendentals=2 * cells, bytes_accessed=12 * cells),
    )(tables, fields, land, river)


def with_ghost(block, axis, dim, width):
    count = lax.axis_size(axis)
    forward = [(i, i + 1) for i in range(count - 1)]
    backward = [(i + 1, i) for i in range(count - 1)]
    size = block.shape[dim]
    above = lax.ppermute(lax.slice_in_dim(block, size - width, size, axis=dim), axis, forward)
    below = lax.ppermute(lax.slice_in_dim(block, 0, width, axis=dim), axis, backward)
    return jnp.concatenate([above, block, below], axis=dim)


def on_device(
    head_start,
    soil_class,
    land_mask,
    ks_table,
    alpha_table,
    store_table,
    section,
    cross_owner,
    cross_local,
    node_cell,
    bed_cond,
):
    own_layers, across, breadth = head_start.shape
    reach_rows, node_count = section.shape
    tile_count = lax.axis_size("tile")
    layer_count = lax.axis_size("layer")
    tile = lax.axis_index("tile")
    layer = lax.axis_index("layer")
    quarter = node_count // layer_count
    node_first = layer * quarter

    planes = jnp.concatenate(
        [head_start, soil_class.astype(jnp.float32), land_mask.astype(jnp.float32)[None]], axis=0
    )
    planes = with_ghost(planes, "tile", 1, GHOST)
    extent = across + 2 * GHOST
    fields = planes[: 2 * own_layers].reshape(2, own_layers, extent, breadth)
    fields = lax.all_gather(fields, "layer", axis=1, tiled=True)
    owners = cross_owner[0]
    positions = cross_local[0]
    node_cells = node_cell[0]
    bed_given = bed_cond[0]
    slots = owners.shape[0]
    per_owner = slots // tile_count
    order = jnp.arange(slots, dtype=jnp.int32)
    same = owners[:, None] == owners[None, :]
    rank = jnp.sum((same & (order[None, :] < order[:, None])).astype(jnp.int32), axis=1)
    place = owners * per_owner + rank
    at_place = place[None, :] == order[:, None]
    wanted = jnp.sum(jnp.where(at_place, positions[None, :], 0), axis=1)
    asked = lax.all_to_all(wanted, "tile", 0, 0, tiled=True)
    reply = jnp.take(section, asked, axis=0)
    sorted_section = lax.all_to_all(reply, "tile", 0, 0, tiled=True)
    slot_section = jnp.take(sorted_section, place, axis=0)

    in_tile = node_cells >= 0
    bed_terms = jnp.where(in_tile, bed_given, 0.0)
    cell_rows = jnp.where(in_tile, node_cells // breadth, -1)
    cell_cols = jnp.where(in_tile, node_cells % breadth, 0)
    top_diag, top_rhs = river_terms(
        cell_rows.reshape(1, -1),
        cell_cols.reshape(1, -1),
        bed_terms.reshape(1, -1),
        (bed_terms * slot_section).reshape(1, -1),
        across,
        breadth,
    )
    river = with_ghost(jnp.stack([top_diag, top_rhs]), "tile", 1, GHOST)
    tables = jnp.stack([ks_table, alpha_table, store_table])
    head = stencil(tables, fields, planes[2 * own_layers], river, tile_count * across)
    kept = lax.dynamic_slice_in_dim(head[:, GHOST : GHOST + across], layer * own_layers, own_layers, 0)

    top_head = head[0, GHOST : GHOST + across]
    my_cells = lax.dynamic_slice_in_dim(node_cells, node_first, quarter, 1)
    my_bed = lax.dynamic_slice_in_dim(bed_given, node_first, quarter, 1)
    my_section = lax.dynamic_slice_in_dim(slot_section, node_first, quarter, 1)
    my_inside = my_cells >= 0
    picked = node_heads(
        top_head,
        jnp.where(my_inside, my_cells // breadth, -1).reshape(1, -1),
        jnp.where(my_inside, my_cells % breadth, 0).reshape(1, -1),
    ).reshape(slots, quarter)
    slot_in = jnp.where(my_inside, my_bed * (picked - my_section), 0.0)
    sorted_in = jnp.take(slot_in, jnp.sum(jnp.where(at_place, order[None, :], 0), axis=1), axis=0)
    arrived = lax.all_to_all(sorted_in, "tile", 0, 0, tiled=True)
    target = asked[None, :] == jnp.arange(reach_rows, dtype=jnp.int32)[:, None]
    inflow = jnp.sum(jnp.where(target[:, :, None], arrived[None], 0.0), axis=1)
    return (kept, inflow)


def solution(mesh):
    placed = (
        P("layer", "tile", None),
        P("layer", "tile", None),
        P("tile", None),
        P(),
        P(),
        P(),
        P("tile", None),
        P("tile", None),
        P("tile", None),
        P("tile", None, None),
        P("tile", None, None),
    )
    return jax.shard_map(
        on_device,
        mesh=mesh,
        in_specs=placed,
        out_specs=(P("layer", "tile", None), P("tile", "layer")),
        check_vma=False,
    )
```

```python
import functools

import jax
import jax.numpy as jnp
from jax import lax
from jax.experimental import pallas as pl
from jax.experimental.pallas import tpu as pltpu
from jax.sharding import PartitionSpec as P

ITERS = 2
SWEEPS = 3
GHOST = 8


LATERAL = 1.0
VERTICAL = 2.0
GRAVITY = 1.0
NEIGHBOURS = (
    (0, -1, VERTICAL),
    (0, 1, VERTICAL),
    (1, -1, LATERAL),
    (1, 1, LATERAL),
    (2, -1, LATERAL),
    (2, 1, LATERAL),
)
CHUNK = 2048


def beside(padded, axis_id, step):
    spans = [slice(1, -1), slice(1, -1), slice(1, -1)]
    spans[axis_id] = slice(1 + step, padded.shape[axis_id] - 1 + step)
    return padded[tuple(spans)]


def neighbor_weights(cond_pad, open_pad):
    centre = cond_pad[1:-1, 1:-1, 1:-1]
    centre_open = open_pad[1:-1, 1:-1, 1:-1]
    result = []
    for axis_id, step, factor in NEIGHBOURS:
        far = beside(cond_pad, axis_id, step)
        far_open = beside(open_pad, axis_id, step)
        result.append(factor * 2.0 * centre_open * far_open / (centre + far))
    return result


def relax(head_pad, weights, store, head_old, riv_diag, riv_rhs):
    total = store * head_old
    diagonal_sum = store
    for weight, (axis_id, step, factor) in zip(weights, NEIGHBOURS):
        total = total + weight * beside(head_pad, axis_id, step)
        diagonal_sum = diagonal_sum + weight
    total = total + GRAVITY * (weights[0] - weights[1]) + riv_rhs
    return total / (diagonal_sum + riv_diag)


def lookup(values_table, classes):
    result = jnp.zeros(classes.shape, jnp.float32)
    for class_id in range(values_table.shape[0]):
        result = jnp.where(classes == class_id, values_table[class_id], result)
    return result


def split3(value):
    high = value.astype(jnp.bfloat16).astype(jnp.float32)
    rest = value - high
    middle = rest.astype(jnp.bfloat16).astype(jnp.float32)
    low = rest - middle
    return high, middle, low


def scatter_kernel(rows_ref, cols_ref, diag_in_ref, rhs_in_ref, diag_ref, rhs_ref, acc_ref):
    step = pl.program_id(0)
    grid_rows, breadth = diag_ref.shape
    chunk = rows_ref.shape[1]

    @pl.when(step == 0)
    def _():
        acc_ref[...] = jnp.zeros_like(acc_ref)

    rows = rows_ref[...]

    @pl.when(jnp.max(rows) >= 0)
    def _():
        hit = lax.broadcasted_iota(jnp.int32, (grid_rows, chunk), 0) == rows
        pieces = []
        for value in (diag_in_ref[...], rhs_in_ref[...]):
            for piece in split3(value):
                pieces.append(jnp.where(hit, piece, 0.0).astype(jnp.bfloat16))
        left = jnp.concatenate(pieces, axis=0)
        cols = cols_ref[...]
        column_hit = lax.broadcasted_iota(jnp.int32, (breadth, chunk), 0) == cols
        right = jnp.where(column_hit, 1.0, 0.0).astype(jnp.bfloat16)
        acc_ref[...] += lax.dot_general(
            left, right, (((1,), (1,)), ((), ())), preferred_element_type=jnp.float32
        )

    @pl.when(step == pl.num_programs(0) - 1)
    def _():
        acc = acc_ref[...]
        g = grid_rows
        diag_ref[...] = acc[0:g] + acc[g : 2 * g] + acc[2 * g : 3 * g]
        rhs_ref[...] = acc[3 * g : 4 * g] + acc[4 * g : 5 * g] + acc[5 * g : 6 * g]


def river_terms(rows, cols, diag_values, rhs_values, grid_rows, breadth):
    count = rows.shape[1]
    chunk = min(CHUNK, count)
    lane = pl.BlockSpec((1, chunk), lambda i: (0, i))
    whole = pl.BlockSpec((grid_rows, breadth), lambda i: (0, 0))
    return pl.pallas_call(
        scatter_kernel,
        grid=(count // chunk,),
        in_specs=[lane, lane, lane, lane],
        out_specs=[whole, whole],
        out_shape=[
            jax.ShapeDtypeStruct((grid_rows, breadth), jnp.float32),
            jax.ShapeDtypeStruct((grid_rows, breadth), jnp.float32),
        ],
        scratch_shapes=[pltpu.VMEM((6 * grid_rows, breadth), jnp.float32)],
        compiler_params=pltpu.CompilerParams(vmem_limit_bytes=48 * 1024 * 1024),
        cost_estimate=pl.CostEstimate(
            flops=2 * 6 * grid_rows * breadth * count,
            transcendentals=0,
            bytes_accessed=16 * count + 8 * grid_rows * breadth,
        ),
    )(rows, cols, diag_values, rhs_values)


def gather_kernel(top_ref, rows_ref, cols_ref, out_ref):
    grid_rows, breadth = top_ref.shape
    chunk = rows_ref.shape[1]
    stacked = jnp.concatenate(
        [piece.astype(jnp.bfloat16) for piece in split3(top_ref[...])], axis=0
    )
    cols = cols_ref[...]
    column_hit = lax.broadcasted_iota(jnp.int32, (breadth, chunk), 0) == cols
    right = jnp.where(column_hit, 1.0, 0.0).astype(jnp.bfloat16)
    picked = jnp.dot(stacked, right, preferred_element_type=jnp.float32)
    g = grid_rows
    by_row = picked[0:g] + picked[g : 2 * g] + picked[2 * g : 3 * g]
    rows = rows_ref[...]
    hit = lax.broadcasted_iota(jnp.int32, (grid_rows, chunk), 0) == rows
    out_ref[...] = jnp.sum(jnp.where(hit, by_row, 0.0), axis=0, keepdims=True)


def node_heads(top, rows, cols):
    grid_rows, breadth = top.shape
    count = rows.shape[1]
    chunk = min(CHUNK, count)
    lane = pl.BlockSpec((1, chunk), lambda i: (0, i))
    return pl.pallas_call(
        gather_kernel,
        grid=(count // chunk,),
        compiler_params=pltpu.CompilerParams(vmem_limit_bytes=48 * 1024 * 1024),
        in_specs=[pl.BlockSpec((grid_rows, breadth), lambda i: (0, 0)), lane, lane],
        out_specs=lane,
        out_shape=jax.ShapeDtypeStruct((1, count), jnp.float32),
        cost_estimate=pl.CostEstimate(
            flops=2 * 3 * grid_rows * breadth * count,
            transcendentals=0,
            bytes_accessed=12 * count + 4 * grid_rows * breadth,
        ),
    )(top, rows, cols)


def stencil_kernel(total_rows, tables_ref, fields_ref, land_ref, river_ref, out_ref,
                   ks_s, alpha_s, store_s, old_s, cond_s, open_s, w_s, heads_s):
    layers, rows, breadth = out_ref.shape
    classes_n = tables_ref.shape[1]
    tile = lax.axis_index("tile")
    row_id = lax.broadcasted_iota(jnp.int32, (rows, breadth), 0)
    col_id = lax.broadcasted_iota(jnp.int32, (rows, breadth), 1)
    grow = tile * (rows - 2 * GHOST) - GHOST + row_id
    inside = (grow >= 0) & (grow < total_rows)
    land = jnp.where(inside, land_ref[...], 0.0)
    moves = []
    for axis, size, ident in ((0, rows, row_id), (1, breadth, col_id)):
        for shift in (1, size - 1):
            adjacent = jnp.abs(pltpu.roll(ident, shift, axis) - ident) == 1
            moves.append((axis, shift, adjacent))

    def shifted(x):
        return [jnp.where(adjacent, pltpu.roll(x, shift, axis), 0.0) for axis, shift, adjacent in moves]

    def init(z, carry):
        classes = fields_ref[1, z].astype(jnp.int32)
        looked = [jnp.zeros((rows, breadth), jnp.float32) for _ in range(3)]
        for class_id in range(classes_n):
            hit = classes == class_id
            looked = [jnp.where(hit, tables_ref[t, class_id], looked[t]) for t in range(3)]
        ks_s[z] = jnp.where(inside, looked[0], 1.0)
        alpha_s[z] = jnp.where(inside, looked[1], 0.0)
        store_s[z] = jnp.where(inside, looked[2], 1.0)
        old_s[z] = jnp.where(inside, fields_ref[0, z], 0.0)
        return carry

    lax.fori_loop(0, layers, init, 0)
    source = old_s
    count = 0
    for picard in range(ITERS):

        def conduct(z, carry, source=source):
            k = ks_s[z] * jnp.exp(alpha_s[z] * jnp.minimum(source[z], 0.0))
            cond_s[z] = k
            open_s[z] = k * land
            return carry

        lax.fori_loop(0, layers, conduct, 0)

        def weigh(z, carry):
            c = cond_s[z]
            co = open_s[z]
            below = jnp.minimum(z + 1, layers - 1)
            far = jnp.where(z < layers - 1, cond_s[below], 0.0)
            far_open = jnp.where(z < layers - 1, open_s[below], 0.0)
            w_s[1, z] = VERTICAL * 2.0 * co * far_open / (c + far)
            w_s[0, z] = jnp.where(z > 0, w_s[1, jnp.maximum(z - 1, 0)], 0.0)
            for axis, first, second in ((0, 0, 1), (1, 2, 3)):
                _, shift, adjacent = moves[first]
                face = LATERAL * 2.0 * co * jnp.where(adjacent, pltpu.roll(co, shift, axis), 0.0) / (
                    c + jnp.where(adjacent, pltpu.roll(c, shift, axis), 0.0)
                )
                _, back, back_adjacent = moves[second]
                w_s[2 * axis + 2, z] = face
                w_s[2 * axis + 3, z] = jnp.where(back_adjacent, pltpu.roll(face, back, axis), 0.0)
            return carry

        lax.fori_loop(0, layers, weigh, 0)
        for sweep in range(SWEEPS):
            last = picard == ITERS - 1 and sweep == SWEEPS - 1
            target = out_ref if last else heads_s.at[count % 2]
            count += 1

            def relax_layer(z, carry, source=source, target=target):
                h = source[z]
                above = jnp.maximum(z - 1, 0)
                below = jnp.minimum(z + 1, layers - 1)
                near = [jnp.where(z > 0, source[above], 0.0), jnp.where(z < layers - 1, source[below], 0.0)]
                near += shifted(h)
                st = store_s[z]
                total = st * old_s[z]
                diagonal_sum = st
                for i in range(len(NEIGHBOURS)):
                    w = w_s[i, z]
                    total = total + w * near[i]
                    diagonal_sum = diagonal_sum + w
                top = z == 0
                total = total + GRAVITY * (w_s[0, z] - w_s[1, z]) + jnp.where(top, river_ref[1], 0.0)
                target[z] = total / (diagonal_sum + jnp.where(top, river_ref[0], 0.0))
                return carry

            lax.fori_loop(0, layers, relax_layer, 0)
            source = target


def stencil(tables, fields, land, river, total_rows):
    _, layers, rows, breadth = fields.shape
    vmem = pl.BlockSpec(memory_space=pltpu.VMEM)
    field = pltpu.VMEM((layers, rows, breadth), jnp.float32)
    cells = layers * rows * breadth
    return pl.pallas_call(
        functools.partial(stencil_kernel, total_rows),
        in_specs=[pl.BlockSpec(memory_space=pltpu.SMEM), vmem, vmem, vmem],
        out_specs=vmem,
        out_shape=jax.ShapeDtypeStruct((layers, rows, breadth), jnp.float32),
        scratch_shapes=[field] * 6
        + [pltpu.VMEM((6, layers, rows, breadth), jnp.float32), pltpu.VMEM((2, layers, rows, breadth), jnp.float32)],
        compiler_params=pltpu.CompilerParams(vmem_limit_bytes=48 * 1024 * 1024),
        cost_estimate=pl.CostEstimate(flops=400 * cells, transcendentals=2 * cells, bytes_accessed=12 * cells),
    )(tables, fields, land, river)


def with_ghost(block, axis, dim, width):
    count = lax.axis_size(axis)
    forward = [(i, i + 1) for i in range(count - 1)]
    backward = [(i + 1, i) for i in range(count - 1)]
    size = block.shape[dim]
    above = lax.ppermute(lax.slice_in_dim(block, size - width, size, axis=dim), axis, forward)
    below = lax.ppermute(lax.slice_in_dim(block, 0, width, axis=dim), axis, backward)
    return jnp.concatenate([above, block, below], axis=dim)


def on_device(
    head_start,
    soil_class,
    land_mask,
    ks_table,
    alpha_table,
    store_table,
    section,
    cross_owner,
    cross_local,
    node_cell,
    bed_cond,
):
    own_layers, across, breadth = head_start.shape
    reach_rows, node_count = section.shape
    tile_count = lax.axis_size("tile")
    layer_count = lax.axis_size("layer")
    tile = lax.axis_index("tile")
    layer = lax.axis_index("layer")
    quarter = node_count // layer_count
    node_first = layer * quarter

    planes = jnp.concatenate(
        [head_start, soil_class.astype(jnp.float32), land_mask.astype(jnp.float32)[None]], axis=0
    )
    planes = with_ghost(planes, "tile", 1, GHOST)
    extent = across + 2 * GHOST
    raw = jnp.stack([head_start, soil_class.astype(jnp.float32)])
    edges = planes[: 2 * own_layers].reshape(2, own_layers, extent, breadth)
    edges = jnp.concatenate([edges[:, :, :GHOST], edges[:, :, GHOST + across :]], axis=2)
    owners = cross_owner[0]
    positions = cross_local[0]
    node_cells = node_cell[0]
    bed_given = bed_cond[0]
    slots = owners.shape[0]
    per_owner = slots // tile_count
    order = jnp.arange(slots, dtype=jnp.int32)
    same = owners[:, None] == owners[None, :]
    rank = jnp.sum((same & (order[None, :] < order[:, None])).astype(jnp.int32), axis=1)
    place = owners * per_owner + rank
    at_place = place[None, :] == order[:, None]
    wanted = jnp.sum(jnp.where(at_place, positions[None, :], 0), axis=1)
    asked = lax.all_to_all(wanted, "tile", 0, 0, tiled=True)
    asked, raw = lax.optimization_barrier((asked, raw))
    raw = lax.all_gather(raw, "layer", axis=1, tiled=True)
    edges = lax.all_gather(edges, "layer", axis=1, tiled=True)
    fields = jnp.concatenate([edges[:, :, :GHOST], raw, edges[:, :, GHOST:]], axis=2)
    reply = jnp.take(section, asked, axis=0)
    sorted_section = lax.all_to_all(reply, "tile", 0, 0, tiled=True)
    slot_section = jnp.take(sorted_section, place, axis=0)

    in_tile = node_cells >= 0
    bed_terms = jnp.where(in_tile, bed_given, 0.0)
    cell_rows = jnp.where(in_tile, node_cells // breadth, -1)
    cell_cols = jnp.where(in_tile, node_cells % breadth, 0)
    top_diag, top_rhs = river_terms(
        cell_rows.reshape(1, -1),
        cell_cols.reshape(1, -1),
        bed_terms.reshape(1, -1),
        (bed_terms * slot_section).reshape(1, -1),
        across,
        breadth,
    )
    river = with_ghost(jnp.stack([top_diag, top_rhs]), "tile", 1, GHOST)
    tables = jnp.stack([ks_table, alpha_table, store_table])
    head = stencil(tables, fields, planes[2 * own_layers], river, tile_count * across)
    kept = lax.dynamic_slice_in_dim(head[:, GHOST : GHOST + across], layer * own_layers, own_layers, 0)

    top_head = head[0, GHOST : GHOST + across]
    my_cells = lax.dynamic_slice_in_dim(node_cells, node_first, quarter, 1)
    my_bed = lax.dynamic_slice_in_dim(bed_given, node_first, quarter, 1)
    my_section = lax.dynamic_slice_in_dim(slot_section, node_first, quarter, 1)
    my_inside = my_cells >= 0
    picked = node_heads(
        top_head,
        jnp.where(my_inside, my_cells // breadth, -1).reshape(1, -1),
        jnp.where(my_inside, my_cells % breadth, 0).reshape(1, -1),
    ).reshape(slots, quarter)
    slot_in = jnp.where(my_inside, my_bed * (picked - my_section), 0.0)
    sorted_in = jnp.take(slot_in, jnp.sum(jnp.where(at_place, order[None, :], 0), axis=1), axis=0)
    arrived = lax.all_to_all(sorted_in, "tile", 0, 0, tiled=True)
    target = asked[None, :] == jnp.arange(reach_rows, dtype=jnp.int32)[:, None]
    inflow = jnp.sum(jnp.where(target[:, :, None], arrived[None], 0.0), axis=1)
    return (kept, inflow)


def solution(mesh):
    placed = (
        P("layer", "tile", None),
        P("layer", "tile", None),
        P("tile", None),
        P(),
        P(),
        P(),
        P("tile", None),
        P("tile", None),
        P("tile", None),
        P("tile", None, None),
        P("tile", None, None),
    )
    return jax.shard_map(
        on_device,
        mesh=mesh,
        in_specs=placed,
        out_specs=(P("layer", "tile", None), P("tile", "layer")),
        check_vma=False,
    )
```

```python
import functools

import jax
import jax.numpy as jnp
from jax import lax
from jax.experimental import pallas as pl
from jax.experimental.pallas import tpu as pltpu
from jax.sharding import PartitionSpec as P

ITERS = 2
SWEEPS = 3
GHOST = 8


LATERAL = 1.0
VERTICAL = 2.0
GRAVITY = 1.0
NEIGHBOURS = (
    (0, -1, VERTICAL),
    (0, 1, VERTICAL),
    (1, -1, LATERAL),
    (1, 1, LATERAL),
    (2, -1, LATERAL),
    (2, 1, LATERAL),
)
CHUNK = 4096


def beside(padded, axis_id, step):
    spans = [slice(1, -1), slice(1, -1), slice(1, -1)]
    spans[axis_id] = slice(1 + step, padded.shape[axis_id] - 1 + step)
    return padded[tuple(spans)]


def neighbor_weights(cond_pad, open_pad):
    centre = cond_pad[1:-1, 1:-1, 1:-1]
    centre_open = open_pad[1:-1, 1:-1, 1:-1]
    result = []
    for axis_id, step, factor in NEIGHBOURS:
        far = beside(cond_pad, axis_id, step)
        far_open = beside(open_pad, axis_id, step)
        result.append(factor * 2.0 * centre_open * far_open / (centre + far))
    return result


def relax(head_pad, weights, store, head_old, riv_diag, riv_rhs):
    total = store * head_old
    diagonal_sum = store
    for weight, (axis_id, step, factor) in zip(weights, NEIGHBOURS):
        total = total + weight * beside(head_pad, axis_id, step)
        diagonal_sum = diagonal_sum + weight
    total = total + GRAVITY * (weights[0] - weights[1]) + riv_rhs
    return total / (diagonal_sum + riv_diag)


def lookup(values_table, classes):
    result = jnp.zeros(classes.shape, jnp.float32)
    for class_id in range(values_table.shape[0]):
        result = jnp.where(classes == class_id, values_table[class_id], result)
    return result


def split3(value):
    high = value.astype(jnp.bfloat16).astype(jnp.float32)
    rest = value - high
    middle = rest.astype(jnp.bfloat16).astype(jnp.float32)
    low = rest - middle
    return high, middle, low


def scatter_kernel(rows_ref, cols_ref, diag_in_ref, rhs_in_ref, diag_ref, rhs_ref, acc_ref):
    step = pl.program_id(0)
    grid_rows, breadth = diag_ref.shape
    chunk = rows_ref.shape[1]

    @pl.when(step == 0)
    def _():
        acc_ref[...] = jnp.zeros_like(acc_ref)

    rows = rows_ref[...]

    @pl.when(jnp.max(rows) >= 0)
    def _():
        hit = lax.broadcasted_iota(jnp.int32, (grid_rows, chunk), 0) == rows
        pieces = []
        for value in (diag_in_ref[...], rhs_in_ref[...]):
            for piece in split3(value):
                pieces.append(jnp.where(hit, piece, 0.0).astype(jnp.bfloat16))
        left = jnp.concatenate(pieces, axis=0)
        cols = cols_ref[...]
        column_hit = lax.broadcasted_iota(jnp.int32, (breadth, chunk), 0) == cols
        right = jnp.where(column_hit, 1.0, 0.0).astype(jnp.bfloat16)
        acc_ref[...] += lax.dot_general(
            left, right, (((1,), (1,)), ((), ())), preferred_element_type=jnp.float32
        )

    @pl.when(step == pl.num_programs(0) - 1)
    def _():
        acc = acc_ref[...]
        g = grid_rows
        diag_ref[...] = acc[0:g] + acc[g : 2 * g] + acc[2 * g : 3 * g]
        rhs_ref[...] = acc[3 * g : 4 * g] + acc[4 * g : 5 * g] + acc[5 * g : 6 * g]


def river_terms(rows, cols, diag_values, rhs_values, grid_rows, breadth):
    count = rows.shape[1]
    chunk = min(CHUNK, count)
    lane = pl.BlockSpec((1, chunk), lambda i: (0, i))
    whole = pl.BlockSpec((grid_rows, breadth), lambda i: (0, 0))
    return pl.pallas_call(
        scatter_kernel,
        grid=(count // chunk,),
        in_specs=[lane, lane, lane, lane],
        out_specs=[whole, whole],
        out_shape=[
            jax.ShapeDtypeStruct((grid_rows, breadth), jnp.float32),
            jax.ShapeDtypeStruct((grid_rows, breadth), jnp.float32),
        ],
        scratch_shapes=[pltpu.VMEM((6 * grid_rows, breadth), jnp.float32)],
        compiler_params=pltpu.CompilerParams(vmem_limit_bytes=48 * 1024 * 1024),
        cost_estimate=pl.CostEstimate(
            flops=2 * 6 * grid_rows * breadth * count,
            transcendentals=0,
            bytes_accessed=16 * count + 8 * grid_rows * breadth,
        ),
    )(rows, cols, diag_values, rhs_values)


def gather_kernel(top_ref, rows_ref, cols_ref, out_ref):
    grid_rows, breadth = top_ref.shape
    chunk = rows_ref.shape[1]
    stacked = jnp.concatenate(
        [piece.astype(jnp.bfloat16) for piece in split3(top_ref[...])], axis=0
    )
    cols = cols_ref[...]
    column_hit = lax.broadcasted_iota(jnp.int32, (breadth, chunk), 0) == cols
    right = jnp.where(column_hit, 1.0, 0.0).astype(jnp.bfloat16)
    picked = jnp.dot(stacked, right, preferred_element_type=jnp.float32)
    g = grid_rows
    by_row = picked[0:g] + picked[g : 2 * g] + picked[2 * g : 3 * g]
    rows = rows_ref[...]
    hit = lax.broadcasted_iota(jnp.int32, (grid_rows, chunk), 0) == rows
    out_ref[...] = jnp.sum(jnp.where(hit, by_row, 0.0), axis=0, keepdims=True)


def node_heads(top, rows, cols):
    grid_rows, breadth = top.shape
    count = rows.shape[1]
    chunk = min(CHUNK, count)
    lane = pl.BlockSpec((1, chunk), lambda i: (0, i))
    return pl.pallas_call(
        gather_kernel,
        grid=(count // chunk,),
        compiler_params=pltpu.CompilerParams(vmem_limit_bytes=48 * 1024 * 1024),
        in_specs=[pl.BlockSpec((grid_rows, breadth), lambda i: (0, 0)), lane, lane],
        out_specs=lane,
        out_shape=jax.ShapeDtypeStruct((1, count), jnp.float32),
        cost_estimate=pl.CostEstimate(
            flops=2 * 3 * grid_rows * breadth * count,
            transcendentals=0,
            bytes_accessed=12 * count + 4 * grid_rows * breadth,
        ),
    )(top, rows, cols)


def stencil_kernel(total_rows, tables_ref, fields_ref, land_ref, river_ref, out_ref,
                   ks_s, alpha_s, store_s, old_s, cond_s, open_s, w_s, heads_s):
    layers, rows, breadth = out_ref.shape
    classes_n = tables_ref.shape[1]
    tile = lax.axis_index("tile")
    row_id = lax.broadcasted_iota(jnp.int32, (rows, breadth), 0)
    col_id = lax.broadcasted_iota(jnp.int32, (rows, breadth), 1)
    grow = tile * (rows - 2 * GHOST) - GHOST + row_id
    inside = (grow >= 0) & (grow < total_rows)
    land = jnp.where(inside, land_ref[...], 0.0)
    moves = []
    for axis, size, ident in ((0, rows, row_id), (1, breadth, col_id)):
        for shift in (1, size - 1):
            adjacent = jnp.abs(pltpu.roll(ident, shift, axis) - ident) == 1
            moves.append((axis, shift, adjacent))

    def shifted(x):
        return [jnp.where(adjacent, pltpu.roll(x, shift, axis), 0.0) for axis, shift, adjacent in moves]

    def init(z, carry):
        classes = fields_ref[1, z].astype(jnp.int32)
        looked = [jnp.zeros((rows, breadth), jnp.float32) for _ in range(3)]
        for class_id in range(classes_n):
            hit = classes == class_id
            looked = [jnp.where(hit, tables_ref[t, class_id], looked[t]) for t in range(3)]
        ks_s[z] = jnp.where(inside, looked[0], 1.0)
        alpha_s[z] = jnp.where(inside, looked[1], 0.0)
        store_s[z] = jnp.where(inside, looked[2], 1.0)
        old_s[z] = jnp.where(inside, fields_ref[0, z], 0.0)
        return carry

    lax.fori_loop(0, layers, init, 0)
    source = old_s
    count = 0
    for picard in range(ITERS):

        def conduct(z, carry, source=source):
            k = ks_s[z] * jnp.exp(alpha_s[z] * jnp.minimum(source[z], 0.0))
            cond_s[z] = k
            open_s[z] = k * land
            return carry

        lax.fori_loop(0, layers, conduct, 0)

        def weigh(z, carry):
            c = cond_s[z]
            co = open_s[z]
            below = jnp.minimum(z + 1, layers - 1)
            far = jnp.where(z < layers - 1, cond_s[below], 0.0)
            far_open = jnp.where(z < layers - 1, open_s[below], 0.0)
            w_s[1, z] = VERTICAL * 2.0 * co * far_open / (c + far)
            w_s[0, z] = jnp.where(z > 0, w_s[1, jnp.maximum(z - 1, 0)], 0.0)
            for axis, first, second in ((0, 0, 1), (1, 2, 3)):
                _, shift, adjacent = moves[first]
                face = LATERAL * 2.0 * co * jnp.where(adjacent, pltpu.roll(co, shift, axis), 0.0) / (
                    c + jnp.where(adjacent, pltpu.roll(c, shift, axis), 0.0)
                )
                _, back, back_adjacent = moves[second]
                w_s[2 * axis + 2, z] = face
                w_s[2 * axis + 3, z] = jnp.where(back_adjacent, pltpu.roll(face, back, axis), 0.0)
            return carry

        lax.fori_loop(0, layers, weigh, 0)
        for sweep in range(SWEEPS):
            last = picard == ITERS - 1 and sweep == SWEEPS - 1
            target = out_ref if last else heads_s.at[count % 2]
            count += 1

            def relax_layer(z, carry, source=source, target=target):
                h = source[z]
                above = jnp.maximum(z - 1, 0)
                below = jnp.minimum(z + 1, layers - 1)
                near = [jnp.where(z > 0, source[above], 0.0), jnp.where(z < layers - 1, source[below], 0.0)]
                near += shifted(h)
                st = store_s[z]
                total = st * old_s[z]
                diagonal_sum = st
                for i in range(len(NEIGHBOURS)):
                    w = w_s[i, z]
                    total = total + w * near[i]
                    diagonal_sum = diagonal_sum + w
                top = z == 0
                total = total + GRAVITY * (w_s[0, z] - w_s[1, z]) + jnp.where(top, river_ref[1], 0.0)
                target[z] = total / (diagonal_sum + jnp.where(top, river_ref[0], 0.0))
                return carry

            lax.fori_loop(0, layers, relax_layer, 0)
            source = target


def stencil(tables, fields, land, river, total_rows):
    _, layers, rows, breadth = fields.shape
    vmem = pl.BlockSpec(memory_space=pltpu.VMEM)
    field = pltpu.VMEM((layers, rows, breadth), jnp.float32)
    cells = layers * rows * breadth
    return pl.pallas_call(
        functools.partial(stencil_kernel, total_rows),
        in_specs=[pl.BlockSpec(memory_space=pltpu.SMEM), vmem, vmem, vmem],
        out_specs=vmem,
        out_shape=jax.ShapeDtypeStruct((layers, rows, breadth), jnp.float32),
        scratch_shapes=[field] * 6
        + [pltpu.VMEM((6, layers, rows, breadth), jnp.float32), pltpu.VMEM((2, layers, rows, breadth), jnp.float32)],
        compiler_params=pltpu.CompilerParams(vmem_limit_bytes=48 * 1024 * 1024),
        cost_estimate=pl.CostEstimate(flops=400 * cells, transcendentals=2 * cells, bytes_accessed=12 * cells),
    )(tables, fields, land, river)


def with_ghost(block, axis, dim, width):
    count = lax.axis_size(axis)
    forward = [(i, i + 1) for i in range(count - 1)]
    backward = [(i + 1, i) for i in range(count - 1)]
    size = block.shape[dim]
    above = lax.ppermute(lax.slice_in_dim(block, size - width, size, axis=dim), axis, forward)
    below = lax.ppermute(lax.slice_in_dim(block, 0, width, axis=dim), axis, backward)
    return jnp.concatenate([above, block, below], axis=dim)


def on_device(
    head_start,
    soil_class,
    land_mask,
    ks_table,
    alpha_table,
    store_table,
    section,
    cross_owner,
    cross_local,
    node_cell,
    bed_cond,
):
    own_layers, across, breadth = head_start.shape
    reach_rows, node_count = section.shape
    tile_count = lax.axis_size("tile")
    layer_count = lax.axis_size("layer")
    tile = lax.axis_index("tile")
    layer = lax.axis_index("layer")
    quarter = node_count // layer_count
    node_first = layer * quarter

    planes = jnp.concatenate(
        [head_start, soil_class.astype(jnp.float32), land_mask.astype(jnp.float32)[None]], axis=0
    )
    planes = with_ghost(planes, "tile", 1, GHOST)
    extent = across + 2 * GHOST
    raw = jnp.stack([head_start, soil_class.astype(jnp.float32)])
    edges = planes[: 2 * own_layers].reshape(2, own_layers, extent, breadth)
    edges = jnp.concatenate([edges[:, :, :GHOST], edges[:, :, GHOST + across :]], axis=2)
    owners = cross_owner[0]
    positions = cross_local[0]
    node_cells = node_cell[0]
    bed_given = bed_cond[0]
    slots = owners.shape[0]
    per_owner = slots // tile_count
    order = jnp.arange(slots, dtype=jnp.int32)
    same = owners[:, None] == owners[None, :]
    rank = jnp.sum((same & (order[None, :] < order[:, None])).astype(jnp.int32), axis=1)
    place = owners * per_owner + rank
    at_place = place[None, :] == order[:, None]
    wanted = jnp.sum(jnp.where(at_place, positions[None, :], 0), axis=1)
    asked = lax.all_to_all(wanted, "tile", 0, 0, tiled=True)
    asked, raw = lax.optimization_barrier((asked, raw))
    raw = lax.all_gather(raw, "layer", axis=1, tiled=True)
    edges = lax.all_gather(edges, "layer", axis=1, tiled=True)
    fields = jnp.concatenate([edges[:, :, :GHOST], raw, edges[:, :, GHOST:]], axis=2)
    reply = jnp.take(section, asked, axis=0)
    sorted_section = lax.all_to_all(reply, "tile", 0, 0, tiled=True)
    slot_section = jnp.take(sorted_section, place, axis=0)

    in_tile = node_cells >= 0
    bed_terms = jnp.where(in_tile, bed_given, 0.0)
    cell_rows = jnp.where(in_tile, node_cells // breadth, -1)
    cell_cols = jnp.where(in_tile, node_cells % breadth, 0)
    top_diag, top_rhs = river_terms(
        cell_rows.reshape(1, -1),
        cell_cols.reshape(1, -1),
        bed_terms.reshape(1, -1),
        (bed_terms * slot_section).reshape(1, -1),
        across,
        breadth,
    )
    river = with_ghost(jnp.stack([top_diag, top_rhs]), "tile", 1, GHOST)
    tables = jnp.stack([ks_table, alpha_table, store_table])
    head = stencil(tables, fields, planes[2 * own_layers], river, tile_count * across)
    kept = lax.dynamic_slice_in_dim(head[:, GHOST : GHOST + across], layer * own_layers, own_layers, 0)

    top_head = head[0, GHOST : GHOST + across]
    my_cells = lax.dynamic_slice_in_dim(node_cells, node_first, quarter, 1)
    my_bed = lax.dynamic_slice_in_dim(bed_given, node_first, quarter, 1)
    my_section = lax.dynamic_slice_in_dim(slot_section, node_first, quarter, 1)
    my_inside = my_cells >= 0
    picked = node_heads(
        top_head,
        jnp.where(my_inside, my_cells // breadth, -1).reshape(1, -1),
        jnp.where(my_inside, my_cells % breadth, 0).reshape(1, -1),
    ).reshape(slots, quarter)
    slot_in = jnp.where(my_inside, my_bed * (picked - my_section), 0.0)
    sorted_in = jnp.take(slot_in, jnp.sum(jnp.where(at_place, order[None, :], 0), axis=1), axis=0)
    arrived = lax.all_to_all(sorted_in, "tile", 0, 0, tiled=True)
    target = asked[None, :] == jnp.arange(reach_rows, dtype=jnp.int32)[:, None]
    inflow = jnp.sum(jnp.where(target[:, :, None], arrived[None], 0.0), axis=1)
    return (kept, inflow)


def solution(mesh):
    placed = (
        P("layer", "tile", None),
        P("layer", "tile", None),
        P("tile", None),
        P(),
        P(),
        P(),
        P("tile", None),
        P("tile", None),
        P("tile", None),
        P("tile", None, None),
        P("tile", None, None),
    )
    return jax.shard_map(
        on_device,
        mesh=mesh,
        in_specs=placed,
        out_specs=(P("layer", "tile", None), P("tile", "layer")),
        check_vma=False,
    )
```

```python
import functools

import jax
import jax.numpy as jnp
from jax import lax
from jax.experimental import pallas as pl
from jax.experimental.pallas import tpu as pltpu
from jax.sharding import PartitionSpec as P

ITERS = 2
SWEEPS = 3
GHOST = 8


LATERAL = 1.0
VERTICAL = 2.0
GRAVITY = 1.0
NEIGHBOURS = (
    (0, -1, VERTICAL),
    (0, 1, VERTICAL),
    (1, -1, LATERAL),
    (1, 1, LATERAL),
    (2, -1, LATERAL),
    (2, 1, LATERAL),
)
CHUNK = 8192


def beside(padded, axis_id, step):
    spans = [slice(1, -1), slice(1, -1), slice(1, -1)]
    spans[axis_id] = slice(1 + step, padded.shape[axis_id] - 1 + step)
    return padded[tuple(spans)]


def neighbor_weights(cond_pad, open_pad):
    centre = cond_pad[1:-1, 1:-1, 1:-1]
    centre_open = open_pad[1:-1, 1:-1, 1:-1]
    result = []
    for axis_id, step, factor in NEIGHBOURS:
        far = beside(cond_pad, axis_id, step)
        far_open = beside(open_pad, axis_id, step)
        result.append(factor * 2.0 * centre_open * far_open / (centre + far))
    return result


def relax(head_pad, weights, store, head_old, riv_diag, riv_rhs):
    total = store * head_old
    diagonal_sum = store
    for weight, (axis_id, step, factor) in zip(weights, NEIGHBOURS):
        total = total + weight * beside(head_pad, axis_id, step)
        diagonal_sum = diagonal_sum + weight
    total = total + GRAVITY * (weights[0] - weights[1]) + riv_rhs
    return total / (diagonal_sum + riv_diag)


def lookup(values_table, classes):
    result = jnp.zeros(classes.shape, jnp.float32)
    for class_id in range(values_table.shape[0]):
        result = jnp.where(classes == class_id, values_table[class_id], result)
    return result


def split3(value):
    high = value.astype(jnp.bfloat16).astype(jnp.float32)
    rest = value - high
    middle = rest.astype(jnp.bfloat16).astype(jnp.float32)
    low = rest - middle
    return high, middle, low


def scatter_kernel(rows_ref, cols_ref, diag_in_ref, rhs_in_ref, diag_ref, rhs_ref, acc_ref):
    step = pl.program_id(0)
    grid_rows, breadth = diag_ref.shape
    chunk = rows_ref.shape[1]

    @pl.when(step == 0)
    def _():
        acc_ref[...] = jnp.zeros_like(acc_ref)

    rows = rows_ref[...]

    @pl.when(jnp.max(rows) >= 0)
    def _():
        hit = lax.broadcasted_iota(jnp.int32, (grid_rows, chunk), 0) == rows
        pieces = []
        for value in (diag_in_ref[...], rhs_in_ref[...]):
            for piece in split3(value):
                pieces.append(jnp.where(hit, piece, 0.0).astype(jnp.bfloat16))
        left = jnp.concatenate(pieces, axis=0)
        cols = cols_ref[...]
        column_hit = lax.broadcasted_iota(jnp.int32, (breadth, chunk), 0) == cols
        right = jnp.where(column_hit, 1.0, 0.0).astype(jnp.bfloat16)
        acc_ref[...] += lax.dot_general(
            left, right, (((1,), (1,)), ((), ())), preferred_element_type=jnp.float32
        )

    @pl.when(step == pl.num_programs(0) - 1)
    def _():
        acc = acc_ref[...]
        g = grid_rows
        diag_ref[...] = acc[0:g] + acc[g : 2 * g] + acc[2 * g : 3 * g]
        rhs_ref[...] = acc[3 * g : 4 * g] + acc[4 * g : 5 * g] + acc[5 * g : 6 * g]


def river_terms(rows, cols, diag_values, rhs_values, grid_rows, breadth):
    count = rows.shape[1]
    chunk = min(CHUNK, count)
    lane = pl.BlockSpec((1, chunk), lambda i: (0, i))
    whole = pl.BlockSpec((grid_rows, breadth), lambda i: (0, 0))
    return pl.pallas_call(
        scatter_kernel,
        grid=(count // chunk,),
        in_specs=[lane, lane, lane, lane],
        out_specs=[whole, whole],
        out_shape=[
            jax.ShapeDtypeStruct((grid_rows, breadth), jnp.float32),
            jax.ShapeDtypeStruct((grid_rows, breadth), jnp.float32),
        ],
        scratch_shapes=[pltpu.VMEM((6 * grid_rows, breadth), jnp.float32)],
        compiler_params=pltpu.CompilerParams(vmem_limit_bytes=48 * 1024 * 1024),
        cost_estimate=pl.CostEstimate(
            flops=2 * 6 * grid_rows * breadth * count,
            transcendentals=0,
            bytes_accessed=16 * count + 8 * grid_rows * breadth,
        ),
    )(rows, cols, diag_values, rhs_values)


def gather_kernel(top_ref, rows_ref, cols_ref, out_ref):
    grid_rows, breadth = top_ref.shape
    chunk = rows_ref.shape[1]
    stacked = jnp.concatenate(
        [piece.astype(jnp.bfloat16) for piece in split3(top_ref[...])], axis=0
    )
    cols = cols_ref[...]
    column_hit = lax.broadcasted_iota(jnp.int32, (breadth, chunk), 0) == cols
    right = jnp.where(column_hit, 1.0, 0.0).astype(jnp.bfloat16)
    picked = jnp.dot(stacked, right, preferred_element_type=jnp.float32)
    g = grid_rows
    by_row = picked[0:g] + picked[g : 2 * g] + picked[2 * g : 3 * g]
    rows = rows_ref[...]
    hit = lax.broadcasted_iota(jnp.int32, (grid_rows, chunk), 0) == rows
    out_ref[...] = jnp.sum(jnp.where(hit, by_row, 0.0), axis=0, keepdims=True)


def node_heads(top, rows, cols):
    grid_rows, breadth = top.shape
    count = rows.shape[1]
    chunk = min(CHUNK, count)
    lane = pl.BlockSpec((1, chunk), lambda i: (0, i))
    return pl.pallas_call(
        gather_kernel,
        grid=(count // chunk,),
        compiler_params=pltpu.CompilerParams(vmem_limit_bytes=48 * 1024 * 1024),
        in_specs=[pl.BlockSpec((grid_rows, breadth), lambda i: (0, 0)), lane, lane],
        out_specs=lane,
        out_shape=jax.ShapeDtypeStruct((1, count), jnp.float32),
        cost_estimate=pl.CostEstimate(
            flops=2 * 3 * grid_rows * breadth * count,
            transcendentals=0,
            bytes_accessed=12 * count + 4 * grid_rows * breadth,
        ),
    )(top, rows, cols)


def stencil_kernel(total_rows, tables_ref, fields_ref, land_ref, river_ref, out_ref,
                   ks_s, alpha_s, store_s, old_s, cond_s, open_s, w_s, heads_s):
    layers, rows, breadth = out_ref.shape
    classes_n = tables_ref.shape[1]
    tile = lax.axis_index("tile")
    row_id = lax.broadcasted_iota(jnp.int32, (rows, breadth), 0)
    col_id = lax.broadcasted_iota(jnp.int32, (rows, breadth), 1)
    grow = tile * (rows - 2 * GHOST) - GHOST + row_id
    inside = (grow >= 0) & (grow < total_rows)
    land = jnp.where(inside, land_ref[...], 0.0)
    moves = []
    for axis, size, ident in ((0, rows, row_id), (1, breadth, col_id)):
        for shift in (1, size - 1):
            adjacent = jnp.abs(pltpu.roll(ident, shift, axis) - ident) == 1
            moves.append((axis, shift, adjacent))

    def shifted(x):
        return [jnp.where(adjacent, pltpu.roll(x, shift, axis), 0.0) for axis, shift, adjacent in moves]

    def init(z, carry):
        classes = fields_ref[1, z].astype(jnp.int32)
        looked = [jnp.zeros((rows, breadth), jnp.float32) for _ in range(3)]
        for class_id in range(classes_n):
            hit = classes == class_id
            looked = [jnp.where(hit, tables_ref[t, class_id], looked[t]) for t in range(3)]
        ks_s[z] = jnp.where(inside, looked[0], 1.0)
        alpha_s[z] = jnp.where(inside, looked[1], 0.0)
        store_s[z] = jnp.where(inside, looked[2], 1.0)
        old_s[z] = jnp.where(inside, fields_ref[0, z], 0.0)
        return carry

    lax.fori_loop(0, layers, init, 0)
    source = old_s
    count = 0
    for picard in range(ITERS):

        def conduct(z, carry, source=source):
            k = ks_s[z] * jnp.exp(alpha_s[z] * jnp.minimum(source[z], 0.0))
            cond_s[z] = k
            open_s[z] = k * land
            return carry

        lax.fori_loop(0, layers, conduct, 0)

        def weigh(z, carry):
            c = cond_s[z]
            co = open_s[z]
            below = jnp.minimum(z + 1, layers - 1)
            far = jnp.where(z < layers - 1, cond_s[below], 0.0)
            far_open = jnp.where(z < layers - 1, open_s[below], 0.0)
            w_s[1, z] = VERTICAL * 2.0 * co * far_open / (c + far)
            w_s[0, z] = jnp.where(z > 0, w_s[1, jnp.maximum(z - 1, 0)], 0.0)
            for axis, first, second in ((0, 0, 1), (1, 2, 3)):
                _, shift, adjacent = moves[first]
                face = LATERAL * 2.0 * co * jnp.where(adjacent, pltpu.roll(co, shift, axis), 0.0) / (
                    c + jnp.where(adjacent, pltpu.roll(c, shift, axis), 0.0)
                )
                _, back, back_adjacent = moves[second]
                w_s[2 * axis + 2, z] = face
                w_s[2 * axis + 3, z] = jnp.where(back_adjacent, pltpu.roll(face, back, axis), 0.0)
            return carry

        lax.fori_loop(0, layers, weigh, 0)
        for sweep in range(SWEEPS):
            last = picard == ITERS - 1 and sweep == SWEEPS - 1
            target = out_ref if last else heads_s.at[count % 2]
            count += 1

            def relax_layer(z, carry, source=source, target=target):
                h = source[z]
                above = jnp.maximum(z - 1, 0)
                below = jnp.minimum(z + 1, layers - 1)
                near = [jnp.where(z > 0, source[above], 0.0), jnp.where(z < layers - 1, source[below], 0.0)]
                near += shifted(h)
                st = store_s[z]
                total = st * old_s[z]
                diagonal_sum = st
                for i in range(len(NEIGHBOURS)):
                    w = w_s[i, z]
                    total = total + w * near[i]
                    diagonal_sum = diagonal_sum + w
                top = z == 0
                total = total + GRAVITY * (w_s[0, z] - w_s[1, z]) + jnp.where(top, river_ref[1], 0.0)
                target[z] = total / (diagonal_sum + jnp.where(top, river_ref[0], 0.0))
                return carry

            lax.fori_loop(0, layers, relax_layer, 0)
            source = target


def stencil(tables, fields, land, river, total_rows):
    _, layers, rows, breadth = fields.shape
    vmem = pl.BlockSpec(memory_space=pltpu.VMEM)
    field = pltpu.VMEM((layers, rows, breadth), jnp.float32)
    cells = layers * rows * breadth
    return pl.pallas_call(
        functools.partial(stencil_kernel, total_rows),
        in_specs=[pl.BlockSpec(memory_space=pltpu.SMEM), vmem, vmem, vmem],
        out_specs=vmem,
        out_shape=jax.ShapeDtypeStruct((layers, rows, breadth), jnp.float32),
        scratch_shapes=[field] * 6
        + [pltpu.VMEM((6, layers, rows, breadth), jnp.float32), pltpu.VMEM((2, layers, rows, breadth), jnp.float32)],
        compiler_params=pltpu.CompilerParams(vmem_limit_bytes=48 * 1024 * 1024),
        cost_estimate=pl.CostEstimate(flops=400 * cells, transcendentals=2 * cells, bytes_accessed=12 * cells),
    )(tables, fields, land, river)


def with_ghost(block, axis, dim, width):
    count = lax.axis_size(axis)
    forward = [(i, i + 1) for i in range(count - 1)]
    backward = [(i + 1, i) for i in range(count - 1)]
    size = block.shape[dim]
    above = lax.ppermute(lax.slice_in_dim(block, size - width, size, axis=dim), axis, forward)
    below = lax.ppermute(lax.slice_in_dim(block, 0, width, axis=dim), axis, backward)
    return jnp.concatenate([above, block, below], axis=dim)


def on_device(
    head_start,
    soil_class,
    land_mask,
    ks_table,
    alpha_table,
    store_table,
    section,
    cross_owner,
    cross_local,
    node_cell,
    bed_cond,
):
    own_layers, across, breadth = head_start.shape
    reach_rows, node_count = section.shape
    tile_count = lax.axis_size("tile")
    layer_count = lax.axis_size("layer")
    tile = lax.axis_index("tile")
    layer = lax.axis_index("layer")
    quarter = node_count // layer_count
    node_first = layer * quarter

    planes = jnp.concatenate(
        [head_start, soil_class.astype(jnp.float32), land_mask.astype(jnp.float32)[None]], axis=0
    )
    planes = with_ghost(planes, "tile", 1, GHOST)
    extent = across + 2 * GHOST
    raw = jnp.stack([head_start, soil_class.astype(jnp.float32)])
    edges = planes[: 2 * own_layers].reshape(2, own_layers, extent, breadth)
    edges = jnp.concatenate([edges[:, :, :GHOST], edges[:, :, GHOST + across :]], axis=2)
    owners = cross_owner[0]
    positions = cross_local[0]
    node_cells = node_cell[0]
    bed_given = bed_cond[0]
    slots = owners.shape[0]
    per_owner = slots // tile_count
    order = jnp.arange(slots, dtype=jnp.int32)
    same = owners[:, None] == owners[None, :]
    rank = jnp.sum((same & (order[None, :] < order[:, None])).astype(jnp.int32), axis=1)
    place = owners * per_owner + rank
    at_place = place[None, :] == order[:, None]
    wanted = jnp.sum(jnp.where(at_place, positions[None, :], 0), axis=1)
    asked = lax.all_to_all(wanted, "tile", 0, 0, tiled=True)
    asked, raw = lax.optimization_barrier((asked, raw))
    raw = lax.all_gather(raw, "layer", axis=1, tiled=True)
    edges = lax.all_gather(edges, "layer", axis=1, tiled=True)
    fields = jnp.concatenate([edges[:, :, :GHOST], raw, edges[:, :, GHOST:]], axis=2)
    reply = jnp.take(section, asked, axis=0)
    sorted_section = lax.all_to_all(reply, "tile", 0, 0, tiled=True)
    slot_section = jnp.take(sorted_section, place, axis=0)

    in_tile = node_cells >= 0
    bed_terms = jnp.where(in_tile, bed_given, 0.0)
    cell_rows = jnp.where(in_tile, node_cells // breadth, -1)
    cell_cols = jnp.where(in_tile, node_cells % breadth, 0)
    top_diag, top_rhs = river_terms(
        cell_rows.reshape(1, -1),
        cell_cols.reshape(1, -1),
        bed_terms.reshape(1, -1),
        (bed_terms * slot_section).reshape(1, -1),
        across,
        breadth,
    )
    river = with_ghost(jnp.stack([top_diag, top_rhs]), "tile", 1, GHOST)
    tables = jnp.stack([ks_table, alpha_table, store_table])
    head = stencil(tables, fields, planes[2 * own_layers], river, tile_count * across)
    kept = lax.dynamic_slice_in_dim(head[:, GHOST : GHOST + across], layer * own_layers, own_layers, 0)

    top_head = head[0, GHOST : GHOST + across]
    my_cells = lax.dynamic_slice_in_dim(node_cells, node_first, quarter, 1)
    my_bed = lax.dynamic_slice_in_dim(bed_given, node_first, quarter, 1)
    my_section = lax.dynamic_slice_in_dim(slot_section, node_first, quarter, 1)
    my_inside = my_cells >= 0
    picked = node_heads(
        top_head,
        jnp.where(my_inside, my_cells // breadth, -1).reshape(1, -1),
        jnp.where(my_inside, my_cells % breadth, 0).reshape(1, -1),
    ).reshape(slots, quarter)
    slot_in = jnp.where(my_inside, my_bed * (picked - my_section), 0.0)
    sorted_in = jnp.take(slot_in, jnp.sum(jnp.where(at_place, order[None, :], 0), axis=1), axis=0)
    arrived = lax.all_to_all(sorted_in, "tile", 0, 0, tiled=True)
    target = asked[None, :] == jnp.arange(reach_rows, dtype=jnp.int32)[:, None]
    inflow = jnp.sum(jnp.where(target[:, :, None], arrived[None], 0.0), axis=1)
    return (kept, inflow)


def solution(mesh):
    placed = (
        P("layer", "tile", None),
        P("layer", "tile", None),
        P("tile", None),
        P(),
        P(),
        P(),
        P("tile", None),
        P("tile", None),
        P("tile", None),
        P("tile", None, None),
        P("tile", None, None),
    )
    return jax.shard_map(
        on_device,
        mesh=mesh,
        in_specs=placed,
        out_specs=(P("layer", "tile", None), P("tile", "layer")),
        check_vma=False,
    )
```
